32 devices in a mesh: front: 8 (over y, x, core), tile: 4 (over z).
Axes of the slice: x: 2, y: 2, z: 4, core: 2. Of those that a mesh axis runs over, the one named last changes fastest.
Arguments:
- pivot_inverse: float32 [8, 2, 512, 512], P('front', None, 'tile'), may hold values from -0.26516504 to 0.26516504
- panel_upper: float32 [8, 2, 512, 2048], P('front', None, None, 'tile'), may hold values from -6 to 6
- panel_lower: float32 [8, 2, 2048, 512], P('front', None, 'tile'), may hold values from -4.2426407 to 4.2426407
- index_map: int32 [8, 2, 2048], replicated, may hold values from 0 to 4095, as said below
- parent_base: float32 [8, 4096, 4096], P('front', None, 'tile'), may hold values from -512 to 512
Outputs:
- parent_front: float32 [8, 4096, 4096], P('front', None, 'tile')
The draws below stay inside these ranges and needn't reach their ends.
Inputs may be any that keep to these rules, and one draw needn't show every extreme that they name: Each list index_map[g, c] holds 2048 distinct parent indices in no particular order, among them 0 and 4095.
All inputs are finite; a program needn't handle non-finite values.
Results may differ from the reference program's by a relative error of at most 0.0003.
Values sent between devices are 32-bit elements; how exact they have to be, the bound alone decides.
A program may use at most 128 MiB of HBM per device.

```python
import jax
import jax.numpy as jnp
from jax import lax

NP = 512
NC = 2048
NPF = 4096
CHILDREN = 2
GROUPS = 8


lower_gain = 16.0


def float_values(key, label, shape, scale):
    sub = jax.random.fold_in(key, label)
    values = jnp.clip(jax.random.normal(sub, shape, jnp.float32), -6.0, 6.0)
    return values * scale


def draw_pivot_inverse(key, part):
    return float_values(key, 11, (GROUPS, CHILDREN, NP, NP), NP ** (-0.5))


def draw_panel_upper(key, part):
    return float_values(key, 12, (GROUPS, CHILDREN, NP, NC), 1.0)


def draw_panel_lower(key, part):
    return float_values(key, 13, (GROUPS, CHILDREN, NC, NP), lower_gain * NP ** (-0.5))


def draw_index_map(key, part):
    keys = jax.random.split(jax.random.fold_in(key, 14), GROUPS * CHILDREN)

    def one_list(single):
        first_key, second_key = jax.random.split(single)
        shuffled = jax.random.permutation(first_key, NPF - 2) + 1
        chosen = shuffled[:NC - 2].astype(jnp.int32)
        first = jnp.zeros((1,), jnp.int32)
        last = jnp.full((1,), NPF - 1, jnp.int32)
        joined = jnp.concatenate([first, chosen, last])
        order = jax.random.permutation(second_key, NC)
        return joined[order].astype(jnp.int32)
    lists = jax.vmap(one_list)(keys)
    return lists.reshape(GROUPS, CHILDREN, NC).astype(jnp.int32)


def exact_block(inverse, upper, lower, mapping):
    factor = jnp.dot(inverse, upper, precision=lax.Precision.HIGHEST)
    update = jnp.dot(lower, factor, precision=lax.Precision.HIGHEST)
    extended = jnp.zeros((NPF, NPF), jnp.float32)
    return extended.at[mapping[:, None], mapping[None, :]].set(update)


def draw_parent_base(key, part):
    inverse = draw_pivot_inverse(key, part)
    upper = draw_panel_upper(key, part)
    lower = draw_panel_lower(key, part)
    mapping = draw_index_map(key, part)
    noise_key = jax.random.fold_in(key, 15)

    def one_parent(group):
        partner = jnp.bitwise_xor(group, 1).astype(jnp.int32)
        first = exact_block(inverse[group, 0], upper[group, 0], lower[group, 0], mapping[group, 0])
        second = exact_block(inverse[partner, 1], upper[partner, 1], lower[partner, 1], mapping[partner, 1])
        noise = float_values(jax.random.fold_in(noise_key, group), 16, (NPF, NPF), 1.0)
        return jnp.clip(noise + first + second, -512.0, 512.0)
    groups = jnp.arange(GROUPS, dtype=jnp.int32)
    return lax.map(one_parent, groups)


def setup_inputs(seed: int = 0) -> dict:
    key_of = jax.random.split(jax.random.key(seed), 6)
    pivot_inverse = draw_pivot_inverse(jax.random.fold_in(key_of[5], 71), 0)
    panel_upper = draw_panel_upper(jax.random.fold_in(key_of[5], 71), 0)
    panel_lower = draw_panel_lower(jax.random.fold_in(key_of[5], 71), 0)
    index_map = draw_index_map(jax.random.fold_in(key_of[5], 71), 0)
    parent_base = draw_parent_base(jax.random.fold_in(key_of[5], 71), 0)
    return {"pivot_inverse": pivot_inverse, "panel_upper": panel_upper, "panel_lower": panel_lower, "index_map": index_map, "parent_base": parent_base}


def split_parts(matrix):
    high = matrix.astype(jnp.bfloat16)
    back = lax.optimization_barrier(high).astype(jnp.float32)
    low = (matrix - back).astype(jnp.bfloat16)
    return high, low


def split_product(left, right):
    left_high, left_low = split_parts(left)
    right_high, right_low = split_parts(right)
    total = jnp.dot(left_high, right_high, preferred_element_type=jnp.float32)
    total = total + jnp.dot(left_high, right_low, preferred_element_type=jnp.float32)
    return total + jnp.dot(left_low, right_high, preferred_element_type=jnp.float32)


def child_block(pivot_inverse, panel_upper, panel_lower, index_map, group, child):
    inverse = pivot_inverse[group, child]
    upper = panel_upper[group, child]
    lower = panel_lower[group, child]
    mapping = index_map[group, child].astype(jnp.int32)
    factor = split_product(inverse, upper)
    update = split_product(lower, factor)
    return place_update(mapping, update)


def place_update(mapping, update):
    extended = jnp.zeros((NPF, NPF), jnp.float32)
    return extended.at[mapping[:, None], mapping[None, :]].set(update)


def reference(pivot_inverse, panel_upper, panel_lower, index_map, parent_base):
    def one_parent(group):
        partner = jnp.bitwise_xor(group, 1).astype(jnp.int32)
        first = child_block(pivot_inverse, panel_upper, panel_lower, index_map, group, 0)
        second = child_block(pivot_inverse, panel_upper, panel_lower, index_map, partner, 1)
        return parent_base[group] - first - second

    groups = jnp.arange(parent_base.shape[0], dtype=jnp.int32)
    return lax.map(one_parent, groups)
```

```python
import functools

import jax
import jax.numpy as jnp
from jax import lax
from jax.experimental import pallas as pl
from jax.experimental.pallas import tpu as pltpu
from jax.sharding import PartitionSpec as P

MESH = pl.DeviceIdType.MESH


def parts(value):
    high = value.astype(jnp.bfloat16)
    return high, (value - high.astype(jnp.float32)).astype(jnp.bfloat16)


def dot(left, right, contract=(1, 0)):
    dims = (((contract[0],), (contract[1],)), ((), ()))
    return lax.dot_general(left, right, dims, preferred_element_type=jnp.float32)


def one_hot(match):
    return match.astype(jnp.float32).astype(jnp.bfloat16)


def front_kernel(
    n, inv_in, up_in, low_in, map_ref, base_in, x_out,
    up, inv, low, up_h, up_l, inv_h, inv_l, low_h, low_l, lx_h, lx_l, f_buf, f_h, f_l, x_buf,
    local_sem, part_send, part_recv, up_send, up_recv, inv_send, inv_recv,
    low_send, low_recv, f_send, f_recv, in_sem, out_sem,
):
    t = lax.axis_index("tile")
    f = lax.axis_index("front")
    partner = lax.rem(f, 2) * -2 + 1 + f
    count = map_ref.shape[2]
    wc = up.shape[3]
    kr = inv.shape[2]
    lr = low.shape[2]
    order, width = x_out.shape
    chunk = min(256, width)
    chunks = width // chunk
    middle = (t >= 1) & (t <= n - 2)
    at_end = (t == 0) | (t == n - 1)
    lower = t < n // 2

    barrier = pltpu.get_barrier_semaphore()
    pl.semaphore_signal(barrier, inc=1, device_id=(partner, t), device_id_type=MESH)

    @pl.when(t > 0)
    def _():
        pl.semaphore_signal(barrier, inc=1, device_id=(f, t - 1), device_id_type=MESH)

    @pl.when(t < n - 1)
    def _():
        pl.semaphore_signal(barrier, inc=1, device_id=(f, t + 1), device_id_type=MESH)

    @pl.when(at_end)
    def _():
        pl.semaphore_wait(barrier, 2)

    @pl.when(middle)
    def _():
        pl.semaphore_wait(barrier, 3)

    sources = (up_in, inv_in, low_in)
    targets = (up, inv, low)

    def local(kind):
        return pltpu.make_async_copy(sources[kind].at[0], targets[kind].at[0, t], local_sem.at[kind])

    def exchange(kind):
        return pltpu.make_async_remote_copy(
            src_ref=sources[kind].at[1], dst_ref=targets[kind].at[1, t],
            send_sem=part_send.at[kind], recv_sem=part_recv.at[kind],
            device_id=(partner, t), device_id_type=MESH,
        )

    def hop(kind, child, shard, side):
        send, recv = ((up_send, up_recv), (inv_send, inv_recv), (low_send, low_recv))[kind]
        ref = targets[kind].at[child, shard]
        return pltpu.make_async_remote_copy(
            src_ref=ref, dst_ref=ref,
            send_sem=send.at[side, child, shard], recv_sem=recv.at[child, shard],
            device_id=(f, lax.rem(t + (1 if side == 0 else n - 1), n)), device_id_type=MESH,
        )

    def takes(kind, side):
        if kind == 2:
            return t + 1 <= n - 1 if side == 0 else t - 1 >= 0
        return t + 1 <= n - 2 if side == 0 else t - 1 >= 1

    def send(kind, child, shard, side):
        @pl.when(takes(kind, side))
        def _():
            hop(kind, child, shard, side).start()

    def send_own(kind, child):
        send(kind, child, t, 0)
        send(kind, child, t, 1)

    def pass_on(kinds, child, d, side, where):
        shard = t - d if side == 0 else t + d
        inside = shard >= 0 if side == 0 else shard <= n - 1

        @pl.when(inside & where)
        def _():
            for kind in kinds:
                hop(kind, child, shard, side).wait_recv()
                send(kind, child, shard, side)

    def relay_low(child, d):
        pass_on((2,), child, d, 0, t >= 0)
        pass_on((2,), child, d, 1, t >= 0)

    def near(child):
        @pl.loop(1, n)
        def _(d):
            pass_on((1, 0), child, d, 0, middle & lower)
            pass_on((1, 0), child, d, 1, middle & (t >= n // 2))

    def far(child):
        @pl.loop(1, n)
        def _(d):
            pass_on((1, 0), child, d, 1, middle & lower)
            pass_on((1, 0), child, d, 0, middle & (t >= n // 2))

    def place_rows(child):
        @pl.loop(0, n)
        def _(s):
            rows = pl.ds(pl.multiple_of(s * lr, lr), lr)
            high, low_part = parts(low[child, s])
            low_h[rows, :] = high
            low_l[rows, :] = low_part

        span = min(256, order)

        @pl.loop(0, order // span)
        def _(j):
            base = pl.multiple_of(j * span, span)
            rows = lax.broadcasted_iota(jnp.int32, (span, count), 0) + base
            choose = one_hot(rows == map_ref[child])
            lx_h[child, pl.ds(base, span), :] = dot(choose, low_h[...]).astype(jnp.bfloat16)
            lx_l[child, pl.ds(base, span), :] = dot(choose, low_l[...]).astype(jnp.bfloat16)

    def split_child(child):
        @pl.loop(0, n)
        def _(s):
            high, low_part = parts(up[child, s])
            up_h[s] = high
            up_l[s] = low_part
            rows = pl.ds(pl.multiple_of(s * kr, kr), kr)
            high, low_part = parts(inv[child, s])
            inv_h[rows, :] = high
            inv_l[rows, :] = low_part

    def factor(child, start, j):
        columns = lax.broadcasted_iota(jnp.int32, (chunk, wc), 0) + (start + j * chunk)
        high = low_part = None
        for s in range(n):
            choose = one_hot(columns == map_ref[child, :, s * wc:(s + 1) * wc])
            a = dot(choose, up_h[s], (1, 1))
            b = dot(choose, up_l[s], (1, 1))
            high = a if high is None else high + a
            low_part = b if low_part is None else low_part + b
        high = high.astype(jnp.bfloat16)
        low_part = low_part.astype(jnp.bfloat16)
        total = dot(high, inv_h[...], (1, 1))
        total = total + dot(low_part, inv_h[...], (1, 1))
        return total + dot(high, inv_l[...], (1, 1))

    def strip(j):
        return pl.ds(pl.multiple_of(j * chunk, chunk), chunk)

    def end_copy(child, j, target):
        ref = f_buf.at[child, strip(j)]
        return pltpu.make_async_remote_copy(
            src_ref=ref, dst_ref=ref,
            send_sem=f_send.at[child, j], recv_sem=f_recv.at[child, j],
            device_id=(f, target), device_id_type=MESH,
        )

    server = (t == 1) | (t == n - 2)
    end = lax.div(t - 1, n - 3) * (n - 1)
    aside = lax.rem(t + 1, n)

    def serve(child):
        @pl.when(middle)
        def _():
            split_child(child)

            @pl.when(server)
            def _():
                @pl.loop(0, chunks)
                def _(j):
                    f_buf[child, strip(j), :] = factor(child, end * width, j)
                    end_copy(child, j, end).start()

            @pl.loop(0, chunks)
            def _(j):
                high, low_part = parts(factor(child, t * width, j))
                f_h[child, strip(j), :] = high
                f_l[child, strip(j), :] = low_part

    def take_factor(child, j):
        @pl.when(at_end)
        def _():
            end_copy(child, j, aside).wait_recv()
            high, low_part = parts(f_buf[child, strip(j), :])
            f_h[child, strip(j), :] = high
            f_l[child, strip(j), :] = low_part

    slots = x_buf.shape[0]
    ahead = slots // 2
    tall = x_buf.shape[1]
    per = order // tall
    blocks = per * chunks

    def window(ref, i):
        rows = pl.ds(pl.multiple_of(lax.rem(i, per) * tall, tall), tall)
        return ref.at[rows, strip(lax.div(i, per))]

    def subtract(child):
        source = base_in if child == 0 else x_out

        def load(i):
            slot = lax.rem(i, slots)
            return pltpu.make_async_copy(window(source, i), x_buf.at[slot], in_sem.at[slot])

        def store(i):
            slot = lax.rem(i, slots)
            return pltpu.make_async_copy(x_buf.at[slot], window(x_out, i), out_sem.at[slot])

        for i in range(ahead):
            load(i).start()

        @pl.loop(0, blocks)
        def _(i):
            j = lax.div(i, per)

            @pl.when(lax.rem(i, per) == 0)
            def _():
                take_factor(child, j)

            @pl.when(i + ahead < blocks)
            def _():
                @pl.when(i >= slots - ahead)
                def _():
                    store(i - (slots - ahead)).wait()

                load(i + ahead).start()

            rows = pl.ds(pl.multiple_of(lax.rem(i, per) * tall, tall), tall)
            high = f_h[child, strip(j), :]
            left = lx_h[child, rows, :]
            total = dot(left, high, (1, 1))
            total = total + dot(left, f_l[child, strip(j), :], (1, 1))
            total = total + dot(lx_l[child, rows, :], high, (1, 1))
            load(i).wait()
            slot = lax.rem(i, slots)
            x_buf[slot] = x_buf[slot] - total
            store(i).start()

        for i in range(max(blocks - slots, 0), blocks):
            store(i).wait()

    for kind in (2, 1, 0):
        exchange(kind).start()
        local(kind).start()
    local(2).wait()
    send_own(2, 0)
    exchange(2).wait()
    send_own(2, 1)
    for kind in (1, 0):
        local(kind).wait()
        exchange(kind).wait()

    @pl.when(at_end)
    def _():
        for child in range(2):
            send_own(1, child)
            send_own(0, child)

    relay_low(0, 1)
    relay_low(1, 1)

    @pl.when(middle)
    def _():
        send_own(1, 0)
        send_own(0, 0)

    relay_low(0, 2)
    near(0)

    @pl.when(middle)
    def _():
        send_own(1, 1)
        send_own(0, 1)

    relay_low(1, 2)

    @pl.loop(3, n - 1)
    def _(d):
        relay_low(0, d)
        relay_low(1, d)

    relay_low(0, n - 1)
    place_rows(0)
    near(1)
    relay_low(1, n - 1)
    place_rows(1)
    far(0)
    serve(0)
    subtract(0)
    far(1)
    serve(1)
    subtract(1)

    for child in range(2):
        @pl.loop(0, n)
        def _(s):
            for side in range(2):
                for kind in range(3):
                    @pl.when(takes(kind, side) & (s <= t if side == 0 else s >= t))
                    def _():
                        hop(kind, child, s, side).wait_send()

        @pl.when(server)
        def _():
            @pl.loop(0, chunks)
            def _(j):
                end_copy(child, j, aside).wait_send()


def assembled(inverse, upper, lower, maps, base, n):
    order, width = base.shape
    pivots = inverse.shape[2]
    count = maps.shape[2]
    kr, wc, lr = inverse.shape[1], upper.shape[2], lower.shape[1]
    vmem = pltpu.VMEM
    dma = pltpu.SemaphoreType.DMA
    f32, b16 = jnp.float32, jnp.bfloat16
    chunk = min(256, width)
    chunks = width // chunk
    slots = 4
    whole = pl.BlockSpec(memory_space=pl.ANY)
    return pl.pallas_call(
        functools.partial(front_kernel, n),
        out_shape=jax.ShapeDtypeStruct((order, width), f32),
        in_specs=[whole] * 3 + [pl.BlockSpec(memory_space=vmem), whole],
        out_specs=whole,
        scratch_shapes=[
            vmem((2, n, pivots, wc), f32),
            vmem((2, n, kr, pivots), f32),
            vmem((2, n, lr, pivots), f32),
            vmem((n, pivots, wc), b16),
            vmem((n, pivots, wc), b16),
            vmem((n * kr, pivots), b16),
            vmem((n * kr, pivots), b16),
            vmem((count, pivots), b16),
            vmem((count, pivots), b16),
            vmem((2, order, pivots), b16),
            vmem((2, order, pivots), b16),
            vmem((2, width, pivots), f32),
            vmem((2, width, pivots), b16),
            vmem((2, width, pivots), b16),
            vmem((slots, min(1024, order), chunk), f32),
            dma((3,)), dma((3,)), dma((3,)),
            dma((2, 2, n)), dma((2, n)),
            dma((2, 2, n)), dma((2, n)),
            dma((2, 2, n)), dma((2, n)),
            dma((2, chunks)), dma((2, chunks)),
            dma((slots,)), dma((slots,)),
        ],
        compiler_params=pltpu.CompilerParams(
            collective_id=0, has_side_effects=True, vmem_limit_bytes=63 * 1024 * 1024
        ),
    )(inverse, upper, lower, maps, base)


def shards(pivot_inverse, panel_upper, panel_lower, index_map, parent_base):
    n = lax.axis_size("tile")
    group = lax.axis_index("front")
    partner = jnp.bitwise_xor(group, 1)
    maps = jnp.stack([
        lax.dynamic_index_in_dim(index_map, group, 0, keepdims=False)[0],
        lax.dynamic_index_in_dim(index_map, partner, 0, keepdims=False)[1],
    ])
    return assembled(
        pivot_inverse[0], panel_upper[0], panel_lower[0], maps[:, None, :], parent_base[0], n
    )[None]


def solution(mesh):
    return jax.shard_map(
        shards,
        mesh=mesh,
        in_specs=(
            P("front", None, "tile", None),
            P("front", None, None, "tile"),
            P("front", None, "tile", None),
            P(),
            P("front", None, "tile"),
        ),
        out_specs=P("front", None, "tile"),
        check_vma=False,
    )
```

```python
import functools
import math

import jax
import jax.numpy as jnp
from jax import lax
from jax.experimental import pallas as pl
from jax.experimental.pallas import tpu as pltpu
from jax.sharding import PartitionSpec as P

MESH = pl.DeviceIdType.MESH


def parts(value):
    high = value.astype(jnp.bfloat16)
    return high, (value - high.astype(jnp.float32)).astype(jnp.bfloat16)


def dot(left, right, contract=(1, 0)):
    dims = (((contract[0],), (contract[1],)), ((), ()))
    return lax.dot_general(left, right, dims, preferred_element_type=jnp.float32)


def one_hot(match):
    return match.astype(jnp.float32).astype(jnp.bfloat16)


def front_kernel(
    n, limits, inv_in, up_in, low_in, index_ref, base_in, x_out,
    map_ref, up, inv, low, up_h, up_l, inv_h, inv_l, low_h, low_l, lx_h, lx_l, f_buf, f_h, f_l, x_buf,
    local_sem, part_send, part_recv, up_send, up_recv, inv_send, inv_recv,
    low_send, low_recv, f_send, f_recv, in_sem, out_sem, *packing,
):
    packed = limits is not None
    if packed:
        ranks, want, row_want, row_in, c_out, c_in, c_h, c_l, g_h, g_l, c_send, c_recv = packing
        cap, cross = limits
    t = lax.axis_index("tile")
    f = lax.axis_index("front")
    partner = lax.rem(f, 2) * -2 + 1 + f
    count = map_ref.shape[2]
    wc = up.shape[3]
    kr = inv.shape[2]
    lr = low.shape[2]
    order, width = x_out.shape
    chunk = min(256, width)
    chunks = width // chunk
    middle = (t >= 1) & (t <= n - 2)
    at_end = (t == 0) | (t == n - 1)
    lower = t < n // 2
    server = (t == 1) | (t == n - 2)
    end = lax.div(t - 1, n - 3) * (n - 1)
    aside = lax.rem(t + 1, n)
    first = jnp.where(lower, 0, n // 2) if packed else 0

    barrier = pltpu.get_barrier_semaphore()
    pl.semaphore_signal(barrier, inc=1, device_id=(partner, t), device_id_type=MESH)

    @pl.when(t > 0)
    def _():
        pl.semaphore_signal(barrier, inc=1, device_id=(f, t - 1), device_id_type=MESH)

    @pl.when(t < n - 1)
    def _():
        pl.semaphore_signal(barrier, inc=1, device_id=(f, t + 1), device_id_type=MESH)

    @pl.when(at_end)
    def _():
        pl.semaphore_wait(barrier, 2)

    @pl.when(middle)
    def _():
        pl.semaphore_wait(barrier, 3)

    sources = (up_in, inv_in, low_in)
    targets = (up, inv, low)

    def place(kind, child, shard):
        return targets[kind].at[child, shard - first if kind == 0 else shard]

    def local(kind):
        return pltpu.make_async_copy(sources[kind].at[0], place(kind, 0, t), local_sem.at[kind])

    def exchange(kind):
        return pltpu.make_async_remote_copy(
            src_ref=sources[kind].at[1], dst_ref=place(kind, 1, t),
            send_sem=part_send.at[kind], recv_sem=part_recv.at[kind],
            device_id=(partner, t), device_id_type=MESH,
        )

    def hop(kind, child, shard, side):
        send, recv = ((up_send, up_recv), (inv_send, inv_recv), (low_send, low_recv))[kind]
        ref = place(kind, child, shard)
        return pltpu.make_async_remote_copy(
            src_ref=ref, dst_ref=ref,
            send_sem=send.at[side, child, shard], recv_sem=recv.at[child, shard],
            device_id=(f, lax.rem(t + (1 if side == 0 else n - 1), n)), device_id_type=MESH,
        )

    def takes(kind, side):
        if kind == 2:
            return t + 1 <= n - 1 if side == 0 else t - 1 >= 0
        if kind == 0 and packed:
            return t == 0 if side == 0 else t == n - 1
        return t + 1 <= n - 2 if side == 0 else t - 1 >= 1

    def send(kind, child, shard, side):
        @pl.when(takes(kind, side))
        def _():
            hop(kind, child, shard, side).start()

    def send_own(kind, child):
        send(kind, child, t, 0)
        send(kind, child, t, 1)

    def pass_on(kinds, child, d, side, where):
        shard = t - d if side == 0 else t + d
        inside = shard >= 0 if side == 0 else shard <= n - 1

        @pl.when(inside & where)
        def _():
            for kind in kinds:
                hop(kind, child, shard, side).wait_recv()
                send(kind, child, shard, side)

    def relay_low(child, d):
        pass_on((2,), child, d, 0, t >= 0)
        pass_on((2,), child, d, 1, t >= 0)

    kinds = (1,) if packed else (1, 0)

    def near(child):
        @pl.loop(1, n)
        def _(d):
            pass_on(kinds, child, d, 0, middle & lower)
            pass_on(kinds, child, d, 1, middle & (t >= n // 2))

    def far(child):
        @pl.loop(1, n)
        def _(d):
            pass_on(kinds, child, d, 1, middle & lower)
            pass_on(kinds, child, d, 0, middle & (t >= n // 2))

    def listed(child, shard):
        return map_ref[child, :, pl.ds(pl.multiple_of(shard * wc, wc), wc)]

    def tables(child):
        row = lax.broadcasted_iota(jnp.int32, (8, 1), 0)
        half, side = width // 2, order // 2
        tile = jnp.where(middle, end, t) * width
        ours = jnp.where(lower, 0, side)
        starts = (tile, tile + half, side - ours, ours)
        spans = (half, half, side, side)
        low_end = high_end = jnp.zeros((8, 1), jnp.int32)
        for q in range(4):
            low_end = jnp.where(row == q, starts[q], low_end)
            high_end = jnp.where(row == q, starts[q] + spans[q], high_end)
        before = lax.broadcasted_iota(jnp.int32, (wc, wc), 0) < lax.broadcasted_iota(jnp.int32, (wc, wc), 1)
        before = one_hot(before)
        passed = jnp.zeros((8, 1), jnp.float32)
        which = lax.broadcasted_iota(jnp.int32, (8, wc), 0)
        wants = [jnp.zeros((cap, 8), jnp.float32)] * 2
        rows = [jnp.zeros((8, row_want.shape[3]), jnp.float32)] * 2
        inward = jnp.zeros((8, row_in.shape[2]), jnp.float32)
        for s in range(n):
            columns = map_ref[child, :, s * wc:(s + 1) * wc]
            is_ours = (first <= s) & (s < first + n // 2)
            fits = (row < 2) | ((row == 2) & is_ours) | ((row == 3) & ~is_ours)
            inside = (columns >= low_end) & (columns < high_end) & fits
            mark = one_hot(inside)
            rank = jnp.where(inside, (dot(mark, before) + passed).astype(jnp.int32), -1)
            passed = passed + jnp.sum(mark.astype(jnp.float32), axis=1, keepdims=True)
            ranks[child, :, s * wc:(s + 1) * wc] = rank
            digits = jnp.where(which == 0, columns >> 7, jnp.where(which == 1, columns & 127, 1))
            digits = digits.astype(jnp.float32).astype(jnp.bfloat16)

            def pick(q, size):
                return one_hot(lax.broadcasted_iota(jnp.int32, (size, wc), 0) == rank[q:q + 1])

            for h in range(2):
                wants[h] = wants[h] + dot(pick(h, cap), digits, (1, 1))
                rows[h] = rows[h] + dot(digits, pick(h, row_want.shape[3]), (1, 1))
            inward = inward + dot(digits, pick(3, row_in.shape[2]), (1, 1))

        def across(found):
            value = found[0:1].astype(jnp.int32) * 128 + found[1:2].astype(jnp.int32)
            return jnp.where(found[2:3] > 0, value, -1)

        for h in range(2):
            found = wants[h].astype(jnp.int32)
            want[child, h] = jnp.where(found[:, 2:3] > 0, found[:, 0:1] * 128 + found[:, 1:2], -1)
            row_want[child, h] = across(rows[h])
        row_in[child] = across(inward)

    def cross_copy(child):
        return pltpu.make_async_remote_copy(
            src_ref=c_out.at[child], dst_ref=c_in.at[child],
            send_sem=c_send.at[child], recv_sem=c_recv.at[child],
            device_id=(f, n - 1 - t), device_id_type=MESH,
        )

    def pack(child):
        @pl.when(middle)
        def _():
            @pl.when(lower)
            def _():
                hop(0, child, 0, 0).wait_recv()

            @pl.when(t >= n // 2)
            def _():
                hop(0, child, n - 1, 1).wait_recv()

            for k in range(n // 2):
                high, low_part = parts(up[child, k])
                up_h[child, k] = high
                up_l[child, k] = low_part
            total = None
            for k in range(n // 2):
                shard = pl.ds(pl.multiple_of((first + k) * wc, wc), wc)
                rank = ranks[child, 2:3, shard]
                choose = one_hot(lax.broadcasted_iota(jnp.int32, (cross, wc), 0) == rank)
                piece = dot(choose, up_h[child, k], (1, 1)) + dot(choose, up_l[child, k], (1, 1))
                total = piece if total is None else total + piece
            c_out[child] = total
            cross_copy(child).start()

    def place_rows(child):
        @pl.loop(0, n)
        def _(s):
            rows = pl.ds(pl.multiple_of(s * lr, lr), lr)
            high, low_part = parts(low[child, s])
            low_h[rows, :] = high
            low_l[rows, :] = low_part

        span = min(256, order)

        @pl.loop(0, order // span)
        def _(j):
            base = pl.multiple_of(j * span, span)
            rows = lax.broadcasted_iota(jnp.int32, (span, count), 0) + base
            choose = one_hot(rows == map_ref[child])
            lx_h[child, pl.ds(base, span), :] = dot(choose, low_h[...]).astype(jnp.bfloat16)
            lx_l[child, pl.ds(base, span), :] = dot(choose, low_l[...]).astype(jnp.bfloat16)

    def split_child(child):
        if packed:
            cross_copy(child).wait_recv()
            high, low_part = parts(c_in[child])
            rest = jnp.zeros((c_h.shape[0] - cross, c_h.shape[1]), jnp.bfloat16)
            c_h[:cross] = high
            c_l[:cross] = low_part
            c_h[cross:] = rest
            c_l[cross:] = rest

        @pl.loop(0, n)
        def _(s):
            if not packed:
                high, low_part = parts(up[child, s])
                up_h[s] = high
                up_l[s] = low_part
            rows = pl.ds(pl.multiple_of(s * kr, kr), kr)
            high, low_part = parts(inv[child, s])
            inv_h[rows, :] = high
            inv_l[rows, :] = low_part

    def factor(child, columns):
        high = low_part = None
        for s in range(n // 2 if packed else n):
            choose = one_hot(columns == listed(child, first + s))
            index = (child, s) if packed else s
            a = dot(choose, up_h[index], (1, 1))
            b = dot(choose, up_l[index], (1, 1))
            high = a if high is None else high + a
            low_part = b if low_part is None else low_part + b
        if packed:
            choose = one_hot(columns == row_in[child])
            high = high + dot(choose, c_h[...])
            low_part = low_part + dot(choose, c_l[...])
        high = high.astype(jnp.bfloat16)
        low_part = low_part.astype(jnp.bfloat16)
        total = dot(high, inv_h[...], (1, 1))
        total = total + dot(low_part, inv_h[...], (1, 1))
        return total + dot(high, inv_l[...], (1, 1))

    def strip(j):
        return pl.ds(pl.multiple_of(j * chunk, chunk), chunk)

    def range_of(start):
        return lax.broadcasted_iota(jnp.int32, (chunk, 1), 0) + start

    groups = 2 if packed else chunks

    def end_copy(child, j, target):
        ref = f_buf.at[child, j]
        return pltpu.make_async_remote_copy(
            src_ref=ref, dst_ref=ref,
            send_sem=f_send.at[child, j], recv_sem=f_recv.at[child, j],
            device_id=(f, target), device_id_type=MESH,
        )

    def serve(child):
        @pl.when(middle)
        def _():
            split_child(child)

            @pl.when(server)
            def _():
                @pl.loop(0, groups)
                def _(j):
                    columns = want[child, j] if packed else range_of(end * width + j * chunk)
                    f_buf[child, j] = factor(child, columns)
                    end_copy(child, j, end).start()

            @pl.loop(0, chunks)
            def _(j):
                high, low_part = parts(factor(child, range_of(t * width + j * chunk)))
                f_h[child, strip(j), :] = high
                f_l[child, strip(j), :] = low_part

    def take_factor(child, j):
        if packed:
            fresh = at_end & (lax.rem(j, chunks // 2) == 0)
            group = lax.div(j, chunks // 2)
        else:
            fresh, group = at_end, j

        @pl.when(fresh)
        def _():
            end_copy(child, group, aside).wait_recv()
            high, low_part = parts(f_buf[child, group])
            if packed:
                rest = jnp.zeros((g_h.shape[0] - cap, g_h.shape[1]), jnp.bfloat16)
                g_h[:cap] = high
                g_l[:cap] = low_part
                g_h[cap:] = rest
                g_l[cap:] = rest
            else:
                f_h[child, strip(j), :] = high
                f_l[child, strip(j), :] = low_part

        if packed:
            @pl.when(at_end)
            def _():
                choose = one_hot(range_of(t * width + j * chunk) == row_want[child, group])
                f_h[child, strip(j), :] = dot(choose, g_h[...]).astype(jnp.bfloat16)
                f_l[child, strip(j), :] = dot(choose, g_l[...]).astype(jnp.bfloat16)

    slots = x_buf.shape[0]
    ahead = slots // 2
    tall = x_buf.shape[1]
    per = order // tall
    blocks = per * chunks

    def window(ref, i):
        rows = pl.ds(pl.multiple_of(lax.rem(i, per) * tall, tall), tall)
        return ref.at[rows, strip(lax.div(i, per))]

    def subtract(child):
        source = base_in if child == 0 else x_out

        def load(i):
            slot = lax.rem(i, slots)
            return pltpu.make_async_copy(window(source, i), x_buf.at[slot], in_sem.at[slot])

        def store(i):
            slot = lax.rem(i, slots)
            return pltpu.make_async_copy(x_buf.at[slot], window(x_out, i), out_sem.at[slot])

        for i in range(ahead):
            load(i).start()

        @pl.loop(0, blocks)
        def _(i):
            j = lax.div(i, per)

            @pl.when(lax.rem(i, per) == 0)
            def _():
                take_factor(child, j)

            @pl.when(i + ahead < blocks)
            def _():
                @pl.when(i >= slots - ahead)
                def _():
                    store(i - (slots - ahead)).wait()

                load(i + ahead).start()

            rows = pl.ds(pl.multiple_of(lax.rem(i, per) * tall, tall), tall)
            high = f_h[child, strip(j), :]
            left = lx_h[child, rows, :]
            total = dot(left, high, (1, 1))
            total = total + dot(left, f_l[child, strip(j), :], (1, 1))
            total = total + dot(lx_l[child, rows, :], high, (1, 1))
            load(i).wait()
            slot = lax.rem(i, slots)
            x_buf[slot] = x_buf[slot] - total
            store(i).start()

        for i in range(max(blocks - slots, 0), blocks):
            store(i).wait()

    for kind in (2, 1, 0):
        exchange(kind).start()
        local(kind).start()
    local(2).wait()
    send_own(2, 0)
    exchange(2).wait()
    send_own(2, 1)
    for kind in (1, 0):
        local(kind).wait()
        exchange(kind).wait()

    @pl.when(at_end)
    def _():
        for child in range(2):
            send_own(1, child)
            send_own(0, child)

    for child in range(2):
        map_ref[child] = index_ref[f if child == 0 else partner, child:child + 1, :]
    if packed:
        for child in range(2):
            tables(child)

    relay_low(0, 1)
    relay_low(1, 1)

    @pl.when(middle)
    def _():
        for kind in kinds:
            send_own(kind, 0)

    relay_low(0, 2)
    near(0)
    if packed:
        pack(0)

    @pl.when(middle)
    def _():
        for kind in kinds:
            send_own(kind, 1)

    relay_low(1, 2)

    @pl.loop(3, n - 1)
    def _(d):
        relay_low(0, d)
        relay_low(1, d)

    relay_low(0, n - 1)
    place_rows(0)
    near(1)
    if packed:
        pack(1)
    relay_low(1, n - 1)
    place_rows(1)
    far(0)
    serve(0)
    subtract(0)
    far(1)
    serve(1)
    subtract(1)

    for child in range(2):
        @pl.loop(0, n)
        def _(s):
            for side in range(2):
                for kind in range(3):
                    @pl.when(takes(kind, side) & (s <= t if side == 0 else s >= t))
                    def _():
                        hop(kind, child, s, side).wait_send()

        @pl.when(server)
        def _():
            @pl.loop(0, groups)
            def _(j):
                end_copy(child, j, aside).wait_send()

        if packed:
            @pl.when(middle)
            def _():
                cross_copy(child).wait_send()


def capacity(expected):
    return -(-math.ceil(expected + 2.8 * math.sqrt(expected)) // 16) * 16


def assembled(inverse, upper, lower, maps, base, n, limits):
    order, width = base.shape
    pivots = inverse.shape[2]
    count = maps.shape[2]
    kr, wc, lr = inverse.shape[1], upper.shape[2], lower.shape[1]
    vmem = pltpu.VMEM
    dma = pltpu.SemaphoreType.DMA
    f32, b16 = jnp.float32, jnp.bfloat16
    chunk = min(256, width)
    chunks = width // chunk
    slots = 4
    packed = limits is not None
    held, extra = n, []
    f_shape = (2, chunks, chunk, pivots)
    u_shape = (n, pivots, wc)
    if packed:
        cap, cross = limits
        cap_pad, cross_pad = -(-cap // 128) * 128, -(-cross // 128) * 128
        held = n // 2
        f_shape = (2, 2, cap, pivots)
        u_shape = (2, held, pivots, wc)
        extra = [
            vmem((2, 8, count), jnp.int32),
            vmem((2, 2, cap, 1), jnp.int32),
            vmem((2, 2, 1, cap_pad), jnp.int32),
            vmem((2, 1, cross_pad), jnp.int32),
            vmem((2, cross, pivots), f32),
            vmem((2, cross, pivots), f32),
            vmem((cross_pad, pivots), b16),
            vmem((cross_pad, pivots), b16),
            vmem((cap_pad, pivots), b16),
            vmem((cap_pad, pivots), b16),
            dma((2,)), dma((2,)),
        ]
    whole = pl.BlockSpec(memory_space=pl.ANY)
    return pl.pallas_call(
        functools.partial(front_kernel, n, limits),
        out_shape=jax.ShapeDtypeStruct((order, width), f32),
        in_specs=[whole] * 3 + [pl.BlockSpec(memory_space=vmem), whole],
        out_specs=whole,
        scratch_shapes=[
            vmem((2, 1, count), jnp.int32),
            vmem((2, held, pivots, wc), f32),
            vmem((2, n, kr, pivots), f32),
            vmem((2, n, lr, pivots), f32),
            vmem(u_shape, b16),
            vmem(u_shape, b16),
            vmem((n * kr, pivots), b16),
            vmem((n * kr, pivots), b16),
            vmem((count, pivots), b16),
            vmem((count, pivots), b16),
            vmem((2, order, pivots), b16),
            vmem((2, order, pivots), b16),
            vmem(f_shape, f32),
            vmem((2, width, pivots), b16),
            vmem((2, width, pivots), b16),
            vmem((slots, min(1024, order), chunk), f32),
            dma((3,)), dma((3,)), dma((3,)),
            dma((2, 2, n)), dma((2, n)),
            dma((2, 2, n)), dma((2, n)),
            dma((2, 2, n)), dma((2, n)),
            dma(f_shape[:2]), dma(f_shape[:2]),
            dma((slots,)), dma((slots,)),
        ] + extra,
        compiler_params=pltpu.CompilerParams(
            collective_id=int(packed), has_side_effects=True, vmem_limit_bytes=63 * 1024 * 1024
        ),
    )(inverse, upper, lower, maps, base)


def shards(pivot_inverse, panel_upper, panel_lower, index_map, parent_base):
    n = lax.axis_size("tile")
    order, width = parent_base.shape[1:]
    count = index_map.shape[2]
    operands = (pivot_inverse[0], panel_upper[0], panel_lower[0], index_map, parent_base[0])

    def run(limits, *args):
        return assembled(*args, n, limits)

    half, side = width // 2, order // 2
    cap = capacity(half * count // order)
    cross = capacity(count // 4)
    if n != 4 or cap >= half or cross >= count // 2:
        return run(None, *operands)[None]

    near = lax.broadcasted_iota(jnp.int32, index_map.shape, 2) < count // 2
    crossing = near ^ (index_map < side)
    most = [jnp.max(jnp.sum((crossing & (near ^ flip)).astype(jnp.int32), axis=2)) for flip in (False, True)]
    fits = jnp.maximum(*most) <= cross
    for part in (0, 1, 2 * n - 2, 2 * n - 1):
        inside = (index_map >= part * half) & (index_map < (part + 1) * half)
        fits &= jnp.max(jnp.sum(inside.astype(jnp.int32), axis=2)) <= cap
    return lax.cond(
        fits, functools.partial(run, (cap, cross)), functools.partial(run, None), *operands
    )[None]


def solution(mesh):
    return jax.shard_map(
        shards,
        mesh=mesh,
        in_specs=(
            P("front", None, "tile", None),
            P("front", None, None, "tile"),
            P("front", None, "tile", None),
            P(),
            P("front", None, "tile"),
        ),
        out_specs=P("front", None, "tile"),
        check_vma=False,
    )
```

```python
import functools
import math

import jax
import jax.numpy as jnp
from jax import lax
from jax.experimental import pallas as pl
from jax.experimental.pallas import tpu as pltpu
from jax.sharding import PartitionSpec as P

MESH = pl.DeviceIdType.MESH


def parts(value):
    high = value.astype(jnp.bfloat16)
    return high, (value - high.astype(jnp.float32)).astype(jnp.bfloat16)


def dot(left, right, contract=(1, 0)):
    dims = (((contract[0],), (contract[1],)), ((), ()))
    return lax.dot_general(left, right, dims, preferred_element_type=jnp.float32)


def one_hot(match):
    return match.astype(jnp.float32).astype(jnp.bfloat16)


def front_kernel(
    n, limits, inv_in, up_in, low_in, index_ref, base_in,
    x_out, high_out, low_out, last_h, last_l,
    map_ref, up, inv, low, up_h, up_l, inv_h, inv_l, low_h, low_l, lx_h, lx_l, f_buf, f_h, f_l, x_buf,
    local_sem, part_send, part_recv, up_send, up_recv, inv_send, inv_recv,
    low_send, low_recv, f_send, f_recv, in_sem, out_sem, lx_sem, *packing,
):
    packed = limits is not None
    if packed:
        ranks, want, row_want, row_in, c_out, c_in, c_h, c_l, g_h, g_l, c_send, c_recv = packing
        cap, cross = limits
        gap = -(-cap // 16) * 16
    t = lax.axis_index("tile")
    f = lax.axis_index("front")
    partner = lax.rem(f, 2) * -2 + 1 + f
    count = map_ref.shape[2]
    wc = up.shape[3]
    kr = inv.shape[2]
    lr = low.shape[2]
    order, width = x_out.shape
    chunk = min(256, width)
    chunks = width // chunk
    middle = (t >= 1) & (t <= n - 2)
    at_end = (t == 0) | (t == n - 1)
    lower = t < n // 2
    server = (t == 1) | (t == n - 2)
    end = lax.div(t - 1, n - 3) * (n - 1)
    aside = lax.rem(t + 1, n)
    first = jnp.where(lower, 0, n // 2) if packed else 0

    barrier = pltpu.get_barrier_semaphore()
    pl.semaphore_signal(barrier, inc=1, device_id=(partner, t), device_id_type=MESH)

    @pl.when(t > 0)
    def _():
        pl.semaphore_signal(barrier, inc=1, device_id=(f, t - 1), device_id_type=MESH)

    @pl.when(t < n - 1)
    def _():
        pl.semaphore_signal(barrier, inc=1, device_id=(f, t + 1), device_id_type=MESH)

    @pl.when(at_end)
    def _():
        pl.semaphore_wait(barrier, 2)

    @pl.when(middle)
    def _():
        pl.semaphore_wait(barrier, 3)

    sources = (up_in, inv_in, low_in)
    targets = (up, inv, low)

    def place(kind, child, shard):
        return targets[kind].at[child, shard - first if kind == 0 else shard]

    def local(kind):
        return pltpu.make_async_copy(sources[kind].at[0], place(kind, 0, t), local_sem.at[kind])

    def exchange(kind):
        return pltpu.make_async_remote_copy(
            src_ref=sources[kind].at[1], dst_ref=place(kind, 1, t),
            send_sem=part_send.at[kind], recv_sem=part_recv.at[kind],
            device_id=(partner, t), device_id_type=MESH,
        )

    def hop(kind, child, shard, side):
        send, recv = ((up_send, up_recv), (inv_send, inv_recv), (low_send, low_recv))[kind]
        ref = place(kind, child, shard)
        return pltpu.make_async_remote_copy(
            src_ref=ref, dst_ref=ref,
            send_sem=send.at[side, child, shard], recv_sem=recv.at[child, shard],
            device_id=(f, lax.rem(t + (1 if side == 0 else n - 1), n)), device_id_type=MESH,
        )

    def takes(kind, side):
        if kind == 2:
            return t + 1 <= n - 1 if side == 0 else t - 1 >= 0
        if kind == 0 and packed:
            return t == 0 if side == 0 else t == n - 1
        return t + 1 <= n - 2 if side == 0 else t - 1 >= 1

    def send(kind, child, shard, side):
        @pl.when(takes(kind, side))
        def _():
            hop(kind, child, shard, side).start()

    def send_own(kind, child):
        send(kind, child, t, 0)
        send(kind, child, t, 1)

    def pass_on(kinds, child, d, side, where):
        shard = t - d if side == 0 else t + d
        inside = shard >= 0 if side == 0 else shard <= n - 1

        @pl.when(inside & where)
        def _():
            for kind in kinds:
                hop(kind, child, shard, side).wait_recv()
                send(kind, child, shard, side)

    def relay_low(child, d):
        pass_on((2,), child, d, 0, t >= 0)
        pass_on((2,), child, d, 1, t >= 0)

    kinds = (1,) if packed else (1, 0)

    def near(child):
        @pl.loop(1, n)
        def _(d):
            pass_on(kinds, child, d, 0, middle & lower)
            pass_on(kinds, child, d, 1, middle & (t >= n // 2))

    def far(child):
        @pl.loop(1, n)
        def _(d):
            pass_on(kinds, child, d, 1, middle & lower)
            pass_on(kinds, child, d, 0, middle & (t >= n // 2))

    def listed(child, shard):
        return map_ref[child, :, pl.ds(pl.multiple_of(shard * wc, wc), wc)]

    def tables(child):
        row = lax.broadcasted_iota(jnp.int32, (8, 1), 0)
        side = order // 2
        tile = jnp.where(middle, end, t) * width
        ours = jnp.where(lower, 0, side)
        starts = (tile, tile, side - ours, ours)
        spans = (width, width, side, side)
        low_end = high_end = jnp.zeros((8, 1), jnp.int32)
        for q in range(4):
            low_end = jnp.where(row == q, starts[q], low_end)
            high_end = jnp.where(row == q, starts[q] + spans[q], high_end)
        before = lax.broadcasted_iota(jnp.int32, (wc, wc), 0) < lax.broadcasted_iota(jnp.int32, (wc, wc), 1)
        before = one_hot(before)
        passed = jnp.zeros((8, 1), jnp.float32)
        which = lax.broadcasted_iota(jnp.int32, (8, wc), 0)
        wants = [jnp.zeros((cap, 8), jnp.float32)] * 2
        both = jnp.zeros((8, row_want.shape[2]), jnp.float32)
        inward = jnp.zeros((8, row_in.shape[2]), jnp.float32)
        for s in range(n):
            columns = map_ref[child, :, s * wc:(s + 1) * wc]
            is_ours = (first <= s) & (s < first + n // 2)
            fits = jnp.where(lax.rem(row, 2) == 0, is_ours.astype(jnp.int32), 1 - is_ours.astype(jnp.int32)) > 0
            inside = (columns >= low_end) & (columns < high_end) & fits
            mark = one_hot(inside)
            rank = jnp.where(inside, (dot(mark, before) + passed).astype(jnp.int32), -2 * count)
            passed = passed + jnp.sum(mark.astype(jnp.float32), axis=1, keepdims=True)
            ranks[child, :, s * wc:(s + 1) * wc] = rank
            digits = jnp.where(which == 0, columns >> 7, jnp.where(which == 1, columns & 127, 1))
            digits = digits.astype(jnp.float32).astype(jnp.bfloat16)

            def pick(q, size, skip=0):
                return one_hot(lax.broadcasted_iota(jnp.int32, (size, wc), 0) - skip == rank[q:q + 1])

            for q in range(2):
                wants[q] = wants[q] + dot(pick(q, cap), digits, (1, 1))
                both = both + dot(digits, pick(q, both.shape[1], q * gap), (1, 1))
            inward = inward + dot(digits, pick(3, inward.shape[1]), (1, 1))

        def across(found):
            value = found[0:1].astype(jnp.int32) * 128 + found[1:2].astype(jnp.int32)
            return jnp.where(found[2:3] > 0, value, -1)

        for q in range(2):
            found = wants[q].astype(jnp.int32)
            want[child, q] = jnp.where(found[:, 2:3] > 0, found[:, 0:1] * 128 + found[:, 1:2], -1)
        row_want[child] = across(both)
        row_in[child] = across(inward)

    def cross_copy(child):
        return pltpu.make_async_remote_copy(
            src_ref=c_out.at[child], dst_ref=c_in.at[child],
            send_sem=c_send.at[child], recv_sem=c_recv.at[child],
            device_id=(f, n - 1 - t), device_id_type=MESH,
        )

    def pack(child):
        @pl.when(middle)
        def _():
            @pl.when(lower)
            def _():
                hop(0, child, 0, 0).wait_recv()

            @pl.when(t >= n // 2)
            def _():
                hop(0, child, n - 1, 1).wait_recv()

            for k in range(n // 2):
                high, low_part = parts(up[child, k])
                up_h[child, k] = high
                up_l[child, k] = low_part
            total = None
            for k in range(n // 2):
                shard = pl.ds(pl.multiple_of((first + k) * wc, wc), wc)
                rank = ranks[child, 2:3, shard]
                choose = one_hot(lax.broadcasted_iota(jnp.int32, (cross, wc), 0) == rank)
                piece = dot(choose, up_h[child, k], (1, 1)) + dot(choose, up_l[child, k], (1, 1))
                total = piece if total is None else total + piece
            c_out[child] = total
            cross_copy(child).start()

    def place_rows(child):
        @pl.loop(0, n)
        def _(s):
            rows = pl.ds(pl.multiple_of(s * lr, lr), lr)
            high, low_part = parts(low[child, s])
            low_h[rows, :] = high
            low_l[rows, :] = low_part

        span = min(512, order)

        @pl.loop(0, order // span)
        def _(j):
            base = pl.multiple_of(j * span, span)
            rows = lax.broadcasted_iota(jnp.int32, (span, count), 0) + base
            choose = one_hot(rows == map_ref[child])
            lx_h[child, pl.ds(base, span), :] = dot(choose, low_h[...]).astype(jnp.bfloat16)
            lx_l[child, pl.ds(base, span), :] = dot(choose, low_l[...]).astype(jnp.bfloat16)

    def split_inverse(child):
        @pl.loop(0, n)
        def _(s):
            rows = pl.ds(pl.multiple_of(s * kr, kr), kr)
            high, low_part = parts(inv[child, s])
            inv_h[rows, :] = high
            inv_l[rows, :] = low_part

    def factor(child, columns, near_side=True, far_side=True):
        terms = []
        if near_side:
            for s in range(n // 2 if packed else n):
                choose = one_hot(columns == listed(child, first + s))
                index = (child, s) if packed else s
                terms.append((dot(choose, up_h[index], (1, 1)), dot(choose, up_l[index], (1, 1))))
        if packed and far_side:
            choose = one_hot(columns == row_in[child])
            terms.append((dot(choose, c_h[...]), dot(choose, c_l[...])))
        high, low_part = terms[0]
        for a, b in terms[1:]:
            high = high + a
            low_part = low_part + b
        high = high.astype(jnp.bfloat16)
        low_part = low_part.astype(jnp.bfloat16)
        total = dot(high, inv_h[...], (1, 1))
        total = total + dot(low_part, inv_h[...], (1, 1))
        return total + dot(high, inv_l[...], (1, 1))

    def strip(j):
        return pl.ds(pl.multiple_of(j * chunk, chunk), chunk)

    def range_of(start):
        return lax.broadcasted_iota(jnp.int32, (chunk, 1), 0) + start

    groups = 2 if packed else chunks

    def end_copy(child, j, target):
        ref = f_buf.at[child, j]
        return pltpu.make_async_remote_copy(
            src_ref=ref, dst_ref=ref,
            send_sem=f_send.at[child, j], recv_sem=f_recv.at[child, j],
            device_id=(f, target), device_id_type=MESH,
        )

    def kept(child):
        return (f_h, f_l) if child == 0 else (last_h, last_l)

    def keep(child, j, value):
        for ref, part in zip(kept(child), parts(value)):
            ref[strip(j), :] = part

    def serve_near(child):
        @pl.when(middle)
        def _():
            split_inverse(child)
            f_buf[child, 0] = factor(child, want[child, 0], far_side=False)
            end_copy(child, 0, end).start()

    def serve_far(child):
        @pl.when(middle)
        def _():
            cross_copy(child).wait_recv()
            high, low_part = parts(c_in[child])
            rest = jnp.zeros((c_h.shape[0] - cross, c_h.shape[1]), jnp.bfloat16)
            c_h[:cross] = high
            c_l[:cross] = low_part
            c_h[cross:] = rest
            c_l[cross:] = rest
            f_buf[child, 1] = factor(child, want[child, 1], near_side=False)
            end_copy(child, 1, end).start()

    def serve_all(child):
        @pl.when(middle)
        def _():
            split_inverse(child)

            @pl.loop(0, n)
            def _(s):
                high, low_part = parts(up[child, s])
                up_h[s] = high
                up_l[s] = low_part

            @pl.when(server)
            def _():
                @pl.loop(0, chunks)
                def _(j):
                    f_buf[child, j] = factor(child, range_of(end * width + j * chunk))
                    end_copy(child, j, end).start()

    def serve_own(child):
        @pl.when(middle)
        def _():
            @pl.loop(0, chunks)
            def _(j):
                keep(child, j, factor(child, range_of(t * width + j * chunk)))

    def take_factor(child):
        @pl.when(at_end)
        def _():
            if packed:
                for q in range(2):
                    end_copy(child, q, aside).wait_recv()
                    high, low_part = parts(f_buf[child, q])
                    for ref, part in ((g_h, high), (g_l, low_part)):
                        ref[q * gap:q * gap + cap] = part
                        stop = gap if q == 0 else ref.shape[0]
                        if q * gap + cap < stop:
                            ref[q * gap + cap:stop] = jnp.zeros((stop - q * gap - cap, ref.shape[1]), jnp.bfloat16)

            @pl.loop(0, chunks)
            def _(j):
                if packed:
                    choose = one_hot(range_of(t * width + j * chunk) == row_want[child])
                    for ref, source in zip(kept(child), (g_h, g_l)):
                        ref[strip(j), :] = dot(choose, source[...]).astype(jnp.bfloat16)
                else:
                    end_copy(child, j, aside).wait_recv()
                    keep(child, j, f_buf[child, j])

    slots = x_buf.shape[0]
    ahead = slots // 2
    tall = x_buf.shape[1]
    per = order // tall
    blocks = per * chunks

    def window(ref, i):
        rows = pl.ds(pl.multiple_of(lax.rem(i, per) * tall, tall), tall)
        return ref.at[rows, strip(lax.div(i, per))]

    def subtract():
        def load(i):
            slot = lax.rem(i, slots)
            return pltpu.make_async_copy(window(base_in, i), x_buf.at[slot], in_sem.at[slot])

        def store(i):
            slot = lax.rem(i, slots)
            return pltpu.make_async_copy(x_buf.at[slot], window(x_out, i), out_sem.at[slot])

        for i in range(ahead):
            load(i).start()
        take_factor(0)

        @pl.loop(0, blocks)
        def _(i):
            j = lax.div(i, per)

            @pl.when(i + ahead < blocks)
            def _():
                @pl.when(i >= slots - ahead)
                def _():
                    store(i - (slots - ahead)).wait()

                load(i + ahead).start()

            rows = pl.ds(pl.multiple_of(lax.rem(i, per) * tall, tall), tall)
            high = f_h[strip(j), :]
            left = lx_h[0, rows, :]
            total = dot(left, high, (1, 1))
            total = total + dot(left, f_l[strip(j), :], (1, 1))
            total = total + dot(lx_l[0, rows, :], high, (1, 1))
            load(i).wait()
            slot = lax.rem(i, slots)
            x_buf[slot] = x_buf[slot] - total
            store(i).start()

        for i in range(max(blocks - slots, 0), blocks):
            store(i).wait()

    def hand_on(k):
        return pltpu.make_async_copy((lx_h, lx_l)[k].at[1], (high_out, low_out)[k], lx_sem.at[k])

    for kind in (2, 1, 0):
        exchange(kind).start()
        local(kind).start()
    local(2).wait()
    send_own(2, 0)
    exchange(2).wait()
    send_own(2, 1)
    for kind in (1, 0):
        local(kind).wait()
        exchange(kind).wait()

    @pl.when(at_end)
    def _():
        for kind, child in ((1, 0), (1, 1), (0, 0), (0, 1)) if packed else ((1, 0), (0, 0), (1, 1), (0, 1)):
            send_own(kind, child)

    for child in range(2):
        map_ref[child] = index_ref[f if child == 0 else partner, child:child + 1, :]
    if packed:
        for child in range(2):
            tables(child)

    relay_low(0, 1)
    relay_low(1, 1)

    @pl.when(middle)
    def _():
        for kind, child in ((1, 0), (1, 1)) if packed else ((1, 0), (0, 0)):
            send_own(kind, child)

    if packed:
        near(0)
        near(1)
        relay_low(0, 2)
        pack(0)
    else:
        relay_low(0, 2)
        near(0)

        @pl.when(middle)
        def _():
            send_own(1, 1)
            send_own(0, 1)

    relay_low(1, 2)

    @pl.loop(3, n - 1)
    def _(d):
        relay_low(0, d)
        relay_low(1, d)

    relay_low(0, n - 1)
    place_rows(0)
    if packed:
        pack(1)
    else:
        near(1)
    relay_low(1, n - 1)
    place_rows(1)
    for k in range(2):
        hand_on(k).start()
    far(0)
    if packed:
        serve_near(0)
        serve_far(0)
        serve_own(0)
        far(1)
        serve_near(1)
        subtract()
        serve_far(1)
    else:
        serve_all(0)
        serve_own(0)
        subtract()
        far(1)
        serve_all(1)
    serve_own(1)
    take_factor(1)
    for k in range(2):
        hand_on(k).wait()

    for child in range(2):
        @pl.loop(0, n)
        def _(s):
            for side in range(2):
                for kind in range(3):
                    @pl.when(takes(kind, side) & (s <= t if side == 0 else s >= t))
                    def _():
                        hop(kind, child, s, side).wait_send()

        @pl.when(server)
        def _():
            @pl.loop(0, groups)
            def _(j):
                end_copy(child, j, aside).wait_send()

        if packed:
            @pl.when(middle)
            def _():
                cross_copy(child).wait_send()


def capacity(draws, share):
    spread = math.sqrt(draws * share * (1 - share))
    return -(-math.ceil(draws * share + 4 * spread) // 8) * 8


def assembled(inverse, upper, lower, maps, base, n, limits):
    order, width = base.shape
    pivots = inverse.shape[2]
    count = maps.shape[2]
    kr, wc, lr = inverse.shape[1], upper.shape[2], lower.shape[1]
    vmem = pltpu.VMEM
    dma = pltpu.SemaphoreType.DMA
    f32, b16 = jnp.float32, jnp.bfloat16
    chunk = min(256, width)
    chunks = width // chunk
    slots = 4
    packed = limits is not None
    held, extra = n, []
    f_shape = (2, chunks, chunk, pivots)
    u_shape = (n, pivots, wc)
    if packed:
        cap, cross = limits
        cap_pad = -(-(-(-cap // 16) * 16 + cap) // 128) * 128
        cross_pad = -(-cross // 128) * 128
        held = n // 2
        f_shape = (2, 2, cap, pivots)
        u_shape = (2, held, pivots, wc)
        extra = [
            vmem((2, 8, count), jnp.int32),
            vmem((2, 2, cap, 1), jnp.int32),
            vmem((2, 1, cap_pad), jnp.int32),
            vmem((2, 1, cross_pad), jnp.int32),
            vmem((2, cross, pivots), f32),
            vmem((2, cross, pivots), f32),
            vmem((cross_pad, pivots), b16),
            vmem((cross_pad, pivots), b16),
            vmem((cap_pad, pivots), b16),
            vmem((cap_pad, pivots), b16),
            dma((2,)), dma((2,)),
        ]
    whole = pl.BlockSpec(memory_space=pl.ANY)
    return pl.pallas_call(
        functools.partial(front_kernel, n, limits),
        out_shape=[jax.ShapeDtypeStruct((order, width), f32)]
        + [jax.ShapeDtypeStruct((order, pivots), b16)] * 2
        + [jax.ShapeDtypeStruct((width, pivots), b16)] * 2,
        in_specs=[whole] * 3 + [pl.BlockSpec(memory_space=vmem), whole],
        out_specs=[whole] * 3 + [pl.BlockSpec(memory_space=vmem)] * 2,
        scratch_shapes=[
            vmem((2, 1, count), jnp.int32),
            vmem((2, held, pivots, wc), f32),
            vmem((2, n, kr, pivots), f32),
            vmem((2, n, lr, pivots), f32),
            vmem(u_shape, b16),
            vmem(u_shape, b16),
            vmem((n * kr, pivots), b16),
            vmem((n * kr, pivots), b16),
            vmem((count, pivots), b16),
            vmem((count, pivots), b16),
            vmem((2, order, pivots), b16),
            vmem((2, order, pivots), b16),
            vmem(f_shape, f32),
            vmem((width, pivots), b16),
            vmem((width, pivots), b16),
            vmem((slots, min(1024, order), chunk), f32),
            dma((3,)), dma((3,)), dma((3,)),
            dma((2, 2, n)), dma((2, n)),
            dma((2, 2, n)), dma((2, n)),
            dma((2, 2, n)), dma((2, n)),
            dma(f_shape[:2]), dma(f_shape[:2]),
            dma((slots,)), dma((slots,)), dma((2,)),
        ] + extra,
        compiler_params=pltpu.CompilerParams(
            collective_id=int(packed), has_side_effects=True, vmem_limit_bytes=63 * 1024 * 1024
        ),
    )(inverse, upper, lower, maps, base)


def finish_kernel(x_ref, high_ref, low_ref, f_h, f_l, out_ref):
    width = out_ref.shape[1]
    chunk = min(256, width)
    for j in range(width // chunk):
        columns = slice(j * chunk, (j + 1) * chunk)
        total = dot(high_ref[...], f_h[columns, :], (1, 1))
        total = total + dot(high_ref[...], f_l[columns, :], (1, 1))
        total = total + dot(low_ref[...], f_h[columns, :], (1, 1))
        out_ref[:, columns] = x_ref[:, columns] - total


def finished(x, high, low_part, f_h, f_l):
    order, width = x.shape
    rows = min(1024, order)
    tall = pl.BlockSpec((rows, width), lambda i: (i, 0))
    slim = pl.BlockSpec((rows, high.shape[1]), lambda i: (i, 0))
    fixed = pl.BlockSpec(f_h.shape, lambda i: (0, 0))
    return pl.pallas_call(
        finish_kernel,
        out_shape=jax.ShapeDtypeStruct(x.shape, x.dtype),
        grid=(order // rows,),
        in_specs=[tall, slim, slim, fixed, fixed],
        out_specs=tall,
        compiler_params=pltpu.CompilerParams(vmem_limit_bytes=40 * 1024 * 1024),
    )(x, high, low_part, f_h, f_l)


def fits_kernel(ranges, index_ref, out_ref):
    index = index_ref[...]
    early = lax.broadcasted_iota(jnp.int32, index.shape, 2) < index.shape[2] // 2
    over = None
    for start, stop, is_early, limit in ranges:
        inside = (index >= start) & (index < stop) & (early if is_early else ~early)
        extra = jnp.sum(inside.astype(jnp.int32), axis=2, keepdims=True) - limit
        over = extra if over is None else jnp.maximum(over, extra)
    out_ref[0] = (jnp.max(over) <= 0).astype(jnp.int32)


def shards(pivot_inverse, panel_upper, panel_lower, index_map, parent_base):
    n = lax.axis_size("tile")
    order, width = parent_base.shape[1:]
    count = index_map.shape[2]
    operands = (pivot_inverse[0], panel_upper[0], panel_lower[0], index_map, parent_base[0])

    def run(limits, *args):
        return tuple(assembled(*args, n, limits))

    side = order // 2
    cap = capacity(count // 2, width / order)
    cross = capacity(count // 2, 1 / 2)
    if n != 4 or 2 * cap >= width or cross >= count // 2:
        return finished(*run(None, *operands))[None]

    ranges = (
        (side, order, True, cross), (0, side, False, cross),
        (0, width, True, cap), (0, width, False, cap),
        (order - width, order, True, cap), (order - width, order, False, cap),
    )
    fits = pl.pallas_call(
        functools.partial(fits_kernel, ranges),
        out_shape=jax.ShapeDtypeStruct((1,), jnp.int32),
        in_specs=[pl.BlockSpec(memory_space=pltpu.VMEM)],
        out_specs=pl.BlockSpec(memory_space=pltpu.SMEM),
    )(index_map)[0]
    return finished(*lax.cond(
        fits > 0, functools.partial(run, (cap, cross)), functools.partial(run, None), *operands
    ))[None]


def solution(mesh):
    return jax.shard_map(
        shards,
        mesh=mesh,
        in_specs=(
            P("front", None, "tile", None),
            P("front", None, None, "tile"),
            P("front", None, "tile", None),
            P(),
            P("front", None, "tile"),
        ),
        out_specs=P("front", None, "tile"),
        check_vma=False,
    )
```

```python
import functools
import math

import jax
import jax.numpy as jnp
from jax import lax
from jax.experimental import pallas as pl
from jax.experimental.pallas import tpu as pltpu
from jax.sharding import PartitionSpec as P

MESH = pl.DeviceIdType.MESH


def parts(value):
    high = value.astype(jnp.bfloat16)
    return high, (value - high.astype(jnp.float32)).astype(jnp.bfloat16)


def spread(value, targets):
    rows = value.shape[0]
    for ref, part in zip(targets, parts(value)):
        ref[:rows] = part
        if rows < ref.shape[0]:
            ref[rows:] = jnp.zeros((ref.shape[0] - rows, ref.shape[1]), jnp.bfloat16)


def dot(left, right, contract=(1, 0)):
    dims = (((contract[0],), (contract[1],)), ((), ()))
    return lax.dot_general(left, right, dims, preferred_element_type=jnp.float32)


def one_hot(match):
    return match.astype(jnp.float32).astype(jnp.bfloat16)


def front_kernel(
    n, limits, inv_in, up_in, low_in, index_ref, base_in,
    x_out, high_out, low_out, last_h_out, last_l_out, raw_out, slot_out,
    map_ref, up, inv, low, up_h, up_l, inv_h, inv_l, low_h, low_l, lx_h, lx_l, f_buf, f_h, f_l, last_h, last_l, x_buf,
    local_sem, part_send, part_recv, up_send, up_recv, inv_send, inv_recv,
    low_send, low_recv, f_send, f_recv, in_sem, out_sem, lx_sem, *packing,
):
    packed = limits is not None
    if packed:
        ranks, want, row_want, row_in, c_out, c_in, c_h, c_l, g_h, g_l, c_send, c_recv = packing
        total_cap, far_cap, cross = limits
        split = total_cap - far_cap
    t = lax.axis_index("tile")
    f = lax.axis_index("front")
    partner = lax.rem(f, 2) * -2 + 1 + f
    count = map_ref.shape[2]
    wc = up.shape[3]
    kr = inv.shape[2]
    lr = low.shape[2]
    order, width = x_out.shape
    chunk = min(256, width)
    chunks = width // chunk
    middle = (t >= 1) & (t <= n - 2)
    at_end = (t == 0) | (t == n - 1)
    lower = t < n // 2
    server = (t == 1) | (t == n - 2)
    end = lax.div(t - 1, n - 3) * (n - 1)
    aside = lax.rem(t + 1, n)
    first = jnp.where(lower, 0, n // 2) if packed else 0

    barrier = pltpu.get_barrier_semaphore()
    pl.semaphore_signal(barrier, inc=1, device_id=(partner, t), device_id_type=MESH)

    @pl.when(t > 0)
    def _():
        pl.semaphore_signal(barrier, inc=1, device_id=(f, t - 1), device_id_type=MESH)

    @pl.when(t < n - 1)
    def _():
        pl.semaphore_signal(barrier, inc=1, device_id=(f, t + 1), device_id_type=MESH)

    @pl.when(at_end)
    def _():
        pl.semaphore_wait(barrier, 2)

    @pl.when(middle)
    def _():
        pl.semaphore_wait(barrier, 3)

    sources = (up_in, inv_in, low_in)
    targets = (up, inv, low)

    def place(kind, child, shard):
        return targets[kind].at[child, shard - first if kind == 0 else shard]

    def local(kind):
        return pltpu.make_async_copy(sources[kind].at[0], place(kind, 0, t), local_sem.at[kind])

    def exchange(kind):
        return pltpu.make_async_remote_copy(
            src_ref=sources[kind].at[1], dst_ref=place(kind, 1, t),
            send_sem=part_send.at[kind], recv_sem=part_recv.at[kind],
            device_id=(partner, t), device_id_type=MESH,
        )

    def hop(kind, child, shard, side, source=None):
        send, recv = ((up_send, up_recv), (inv_send, inv_recv), (low_send, low_recv))[kind]
        ref = place(kind, child, shard)
        return pltpu.make_async_remote_copy(
            src_ref=ref if source is None else source, dst_ref=ref,
            send_sem=send.at[side, child, shard], recv_sem=recv.at[child, shard],
            device_id=(f, lax.rem(t + (1 if side == 0 else n - 1), n)), device_id_type=MESH,
        )

    def takes(kind, side):
        if kind == 2:
            return t + 1 <= n - 1 if side == 0 else t - 1 >= 0
        if kind == 0 and packed:
            return t == 0 if side == 0 else t == n - 1
        return t + 1 <= n - 2 if side == 0 else t - 1 >= 1

    def send(kind, child, shard, side, source=None):
        @pl.when(takes(kind, side))
        def _():
            hop(kind, child, shard, side, source).start()

    def send_own(kind, child, source=None):
        send(kind, child, t, 0, source)
        send(kind, child, t, 1, source)

    def pass_on(kinds, child, d, side, where):
        shard = t - d if side == 0 else t + d
        inside = shard >= 0 if side == 0 else shard <= n - 1

        @pl.when(inside & where)
        def _():
            for kind in kinds:
                hop(kind, child, shard, side).wait_recv()
                send(kind, child, shard, side)

    def relay_low(child, d):
        pass_on((2,), child, d, 0, t >= 0)
        pass_on((2,), child, d, 1, t >= 0)

    kinds = (1,) if packed else (1, 0)

    def near(child):
        @pl.loop(1, n)
        def _(d):
            pass_on(kinds, child, d, 0, middle & lower)
            pass_on(kinds, child, d, 1, middle & (t >= n // 2))

    def far(child):
        @pl.loop(1, n)
        def _(d):
            pass_on(kinds, child, d, 1, middle & lower)
            pass_on(kinds, child, d, 0, middle & (t >= n // 2))

    def listed(child, shard):
        return map_ref[child, :, pl.ds(pl.multiple_of(shard * wc, wc), wc)]

    def tables(child):
        row = lax.broadcasted_iota(jnp.int32, (8, 1), 0)
        side = order // 2
        tile = jnp.where(middle, end, t) * width
        ours = jnp.where(lower, 0, side)
        starts = (tile, tile, side - ours, ours)
        spans = (width, width, side, side)
        low_end = high_end = jnp.zeros((8, 1), jnp.int32)
        for q in range(4):
            low_end = jnp.where(row == q, starts[q], low_end)
            high_end = jnp.where(row == q, starts[q] + spans[q], high_end)
        before = lax.broadcasted_iota(jnp.int32, (wc, wc), 0) < lax.broadcasted_iota(jnp.int32, (wc, wc), 1)
        before = one_hot(before)
        passed = jnp.zeros((8, 1), jnp.float32)
        which = lax.broadcasted_iota(jnp.int32, (8, wc), 0)
        wants = jnp.zeros((total_cap, 8), jnp.float32)
        both = jnp.zeros((8, row_want.shape[2]), jnp.float32)
        inward = jnp.zeros((8, row_in.shape[2]), jnp.float32)
        for s in range(n):
            columns = map_ref[child, :, s * wc:(s + 1) * wc]
            is_ours = (first <= s) & (s < first + n // 2)
            fits = jnp.where(lax.rem(row, 2) == 0, is_ours.astype(jnp.int32), 1 - is_ours.astype(jnp.int32)) > 0
            inside = (columns >= low_end) & (columns < high_end) & fits
            mark = one_hot(inside)
            rank = jnp.where(inside, (dot(mark, before) + passed).astype(jnp.int32), -2 * count)
            passed = passed + jnp.sum(mark.astype(jnp.float32), axis=1, keepdims=True)
            ranks[child, :, s * wc:(s + 1) * wc] = rank
            digits = jnp.where(which == 0, columns >> 7, jnp.where(which == 1, columns & 127, 1))
            digits = digits.astype(jnp.float32).astype(jnp.bfloat16)

            def pick(q, size):
                slot = lax.broadcasted_iota(jnp.int32, (size, wc), 0)
                return one_hot((total_cap - 1 - slot if q == 1 else slot) == rank[q:q + 1])

            for q in range(2):
                wants = wants + dot(pick(q, total_cap), digits, (1, 1))
                both = both + dot(digits, pick(q, both.shape[1]), (1, 1))
            inward = inward + dot(digits, pick(3, inward.shape[1]), (1, 1))

        def across(found):
            value = found[0:1].astype(jnp.int32) * 128 + found[1:2].astype(jnp.int32)
            return jnp.where(found[2:3] > 0, value, -1)

        found = wants.astype(jnp.int32)
        want[child] = jnp.where(found[:, 2:3] > 0, found[:, 0:1] * 128 + found[:, 1:2], -1)
        row_want[child] = across(both)
        row_in[child] = across(inward)

    def cross_copy(child):
        return pltpu.make_async_remote_copy(
            src_ref=c_out.at[child], dst_ref=c_in.at[child],
            send_sem=c_send.at[child], recv_sem=c_recv.at[child],
            device_id=(f, n - 1 - t), device_id_type=MESH,
        )

    def pack(child):
        @pl.when(middle)
        def _():
            @pl.when(lower)
            def _():
                hop(0, child, 0, 0).wait_recv()

            @pl.when(t >= n // 2)
            def _():
                hop(0, child, n - 1, 1).wait_recv()

            for k in range(n // 2):
                high, low_part = parts(up[child, k])
                up_h[child, k] = high
                up_l[child, k] = low_part
            total = None
            for k in range(n // 2):
                shard = pl.ds(pl.multiple_of((first + k) * wc, wc), wc)
                rank = ranks[child, 2:3, shard]
                choose = one_hot(lax.broadcasted_iota(jnp.int32, (cross, wc), 0) == rank)
                piece = dot(choose, up_h[child, k], (1, 1)) + dot(choose, up_l[child, k], (1, 1))
                total = piece if total is None else total + piece
            c_out[child] = total
            cross_copy(child).start()

    def place_rows(child):
        @pl.loop(0, n)
        def _(s):
            rows = pl.ds(pl.multiple_of(s * lr, lr), lr)
            high, low_part = parts(low[child, s])
            low_h[rows, :] = high
            low_l[rows, :] = low_part

        span = min(512, order)

        @pl.loop(0, order // span)
        def _(j):
            base = pl.multiple_of(j * span, span)
            rows = lax.broadcasted_iota(jnp.int32, (span, count), 0) + base
            choose = one_hot(rows == map_ref[child])
            lx_h[child, pl.ds(base, span), :] = dot(choose, low_h[...]).astype(jnp.bfloat16)
            lx_l[child, pl.ds(base, span), :] = dot(choose, low_l[...]).astype(jnp.bfloat16)

    def split_inverse(child):
        @pl.loop(0, n)
        def _(s):
            rows = pl.ds(pl.multiple_of(s * kr, kr), kr)
            high, low_part = parts(inv[child, s])
            inv_h[rows, :] = high
            inv_l[rows, :] = low_part

    def factor(child, columns, near_side=True, far_side=True):
        terms = []
        if near_side:
            for s in range(n // 2 if packed else n):
                choose = one_hot(columns == listed(child, first + s))
                index = (child, s) if packed else s
                terms.append((dot(choose, up_h[index], (1, 1)), dot(choose, up_l[index], (1, 1))))
        if packed and far_side:
            choose = one_hot(columns == row_in[child])
            terms.append((dot(choose, c_h[...]), dot(choose, c_l[...])))
        high, low_part = terms[0]
        for a, b in terms[1:]:
            high = high + a
            low_part = low_part + b
        high = high.astype(jnp.bfloat16)
        low_part = low_part.astype(jnp.bfloat16)
        total = dot(high, inv_h[...], (1, 1))
        total = total + dot(low_part, inv_h[...], (1, 1))
        return total + dot(high, inv_l[...], (1, 1))

    def strip(j):
        return pl.ds(pl.multiple_of(j * chunk, chunk), chunk)

    def range_of(start):
        return lax.broadcasted_iota(jnp.int32, (chunk, 1), 0) + start

    def slots_of(j):
        return slice(0, split) if j == 0 else slice(split, total_cap)

    def end_copy(child, j, target):
        if packed:
            ref = f_buf.at[child, slots_of(j)]
            into = raw_out.at[slots_of(j)] if child == 1 else ref
        else:
            ref = into = f_buf.at[child, j]
        return pltpu.make_async_remote_copy(
            src_ref=ref, dst_ref=into,
            send_sem=f_send.at[child, j], recv_sem=f_recv.at[child, j],
            device_id=(f, target), device_id_type=MESH,
        )

    def kept(child):
        return (f_h, f_l) if child == 0 else (last_h, last_l)

    def keep(child, j, value):
        for ref, part in zip(kept(child), parts(value)):
            ref[strip(j), :] = part

    def serve_near(child):
        @pl.when(middle)
        def _():
            split_inverse(child)
            f_buf[child, slots_of(0)] = factor(child, want[child, slots_of(0)], far_side=False)
            end_copy(child, 0, end).start()

    def serve_far(child):
        @pl.when(middle)
        def _():
            cross_copy(child).wait_recv()
            high, low_part = parts(c_in[child])
            rest = jnp.zeros((c_h.shape[0] - cross, c_h.shape[1]), jnp.bfloat16)
            c_h[:cross] = high
            c_l[:cross] = low_part
            c_h[cross:] = rest
            c_l[cross:] = rest
            f_buf[child, slots_of(1)] = factor(child, want[child, slots_of(1)])
            end_copy(child, 1, end).start()

    def serve_all(child):
        @pl.when(middle)
        def _():
            split_inverse(child)

            @pl.loop(0, n)
            def _(s):
                high, low_part = parts(up[child, s])
                up_h[s] = high
                up_l[s] = low_part

            @pl.when(server)
            def _():
                @pl.loop(0, chunks)
                def _(j):
                    f_buf[child, j] = factor(child, range_of(end * width + j * chunk))
                    end_copy(child, j, end).start()

    def serve_own(child):
        @pl.when(middle)
        def _():
            @pl.loop(0, chunks)
            def _(j):
                keep(child, j, factor(child, range_of(t * width + j * chunk)))

    def take_factor(child):
        @pl.when(at_end)
        def _():
            if packed:
                for q in range(2):
                    end_copy(child, q, aside).wait_recv()
                if child == 1:
                    return
                spread(f_buf[child], (g_h, g_l))

            @pl.loop(0, chunks)
            def _(j):
                if packed:
                    choose = one_hot(range_of(t * width + j * chunk) == row_want[child])
                    for ref, source in zip(kept(child), (g_h, g_l)):
                        ref[strip(j), :] = dot(choose, source[...]).astype(jnp.bfloat16)
                else:
                    end_copy(child, j, aside).wait_recv()
                    keep(child, j, f_buf[child, j])

    slots = x_buf.shape[0]
    ahead = slots // 2
    tall = x_buf.shape[1]
    per = order // tall
    blocks = per * chunks

    def window(ref, i):
        rows = pl.ds(pl.multiple_of(lax.rem(i, per) * tall, tall), tall)
        return ref.at[rows, strip(lax.div(i, per))]

    def subtract(begin, stop):
        def load(i):
            slot = lax.rem(i, slots)
            return pltpu.make_async_copy(window(base_in, i), x_buf.at[slot], in_sem.at[slot])

        def store(i):
            slot = lax.rem(i, slots)
            return pltpu.make_async_copy(x_buf.at[slot], window(x_out, i), out_sem.at[slot])

        for i in range(begin, min(begin + ahead, stop)):
            load(i).start()
        if begin == 0:
            take_factor(0)

        @pl.loop(begin, stop)
        def _(i):
            j = lax.div(i, per)

            @pl.when(i + ahead < stop)
            def _():
                @pl.when(i >= begin + slots - ahead)
                def _():
                    store(i - (slots - ahead)).wait()

                load(i + ahead).start()

            rows = pl.ds(pl.multiple_of(lax.rem(i, per) * tall, tall), tall)
            high = f_h[strip(j), :]
            left = lx_h[0, rows, :]
            total = dot(left, high, (1, 1))
            total = total + dot(left, f_l[strip(j), :], (1, 1))
            total = total + dot(lx_l[0, rows, :], high, (1, 1))
            load(i).wait()
            slot = lax.rem(i, slots)
            x_buf[slot] = x_buf[slot] - total
            store(i).start()

        for i in range(max(stop - slots, begin), stop):
            store(i).wait()

    def hand_on(k):
        if k < 2:
            return pltpu.make_async_copy((lx_h, lx_l)[k].at[1], (high_out, low_out)[k], lx_sem.at[k])
        if k < 4:
            return pltpu.make_async_copy((last_h, last_l)[k - 2], (last_h_out, last_l_out)[k - 2], lx_sem.at[k])
        return pltpu.make_async_copy(row_want.at[1], slot_out, lx_sem.at[k])

    send_own(2, 0, low_in.at[0])
    for kind in (2, 1, 0):
        exchange(kind).start()
        local(kind).start()
    exchange(2).wait()
    send_own(2, 1)
    local(2).wait()
    for kind in (1, 0):
        local(kind).wait()
        exchange(kind).wait()

    @pl.when(at_end)
    def _():
        for kind, child in ((1, 0), (1, 1), (0, 0), (0, 1)) if packed else ((1, 0), (0, 0), (1, 1), (0, 1)):
            send_own(kind, child)

    for child in range(2):
        map_ref[child] = index_ref[f if child == 0 else partner, child:child + 1, :]
    if packed:
        for child in range(2):
            tables(child)
        hand_on(4).start()

    relay_low(0, 1)
    relay_low(1, 1)

    @pl.when(middle)
    def _():
        for kind, child in ((1, 0), (1, 1)) if packed else ((1, 0), (0, 0)):
            send_own(kind, child)

    if packed:
        near(0)
        near(1)
        relay_low(0, 2)
        pack(0)
    else:
        relay_low(0, 2)
        near(0)

        @pl.when(middle)
        def _():
            send_own(1, 1)
            send_own(0, 1)

    relay_low(1, 2)

    @pl.loop(3, n - 1)
    def _(d):
        relay_low(0, d)
        relay_low(1, d)

    relay_low(0, n - 1)
    place_rows(0)
    if packed:
        pack(1)
    else:
        near(1)
    relay_low(1, n - 1)
    place_rows(1)
    for k in range(2):
        hand_on(k).start()
    far(0)
    if packed:
        serve_near(0)
        serve_far(0)
        serve_own(0)
        far(1)
        serve_near(1)
        subtract(0, blocks // 2)
        serve_far(1)
        subtract(blocks // 2, blocks)
        keeps = middle
    else:
        serve_all(0)
        serve_own(0)
        subtract(0, blocks)
        far(1)
        serve_all(1)
        keeps = t >= 0
    serve_own(1)
    take_factor(1)

    @pl.when(keeps)
    def _():
        for k in (2, 3):
            hand_on(k).start()
        for k in (2, 3):
            hand_on(k).wait()

    for k in (0, 1, 4) if packed else (0, 1):
        hand_on(k).wait()

    for child in range(2):
        @pl.loop(0, n)
        def _(s):
            for side in range(2):
                for kind in range(3):
                    @pl.when(takes(kind, side) & (s <= t if side == 0 else s >= t))
                    def _():
                        hop(kind, child, s, side).wait_send()

        @pl.when(server)
        def _():
            if packed:
                for j in range(2):
                    end_copy(child, j, aside).wait_send()
            else:
                @pl.loop(0, chunks)
                def _(j):
                    end_copy(child, j, aside).wait_send()

        if packed:
            @pl.when(middle)
            def _():
                cross_copy(child).wait_send()


def capacity(draws, share, order):
    spread_of = math.sqrt(draws * share * (1 - share) * (1 - draws / order))
    return -(-math.ceil(draws * share + 4.5 * spread_of) // 8) * 8


def padded(rows):
    return -(-rows // 128) * 128


def assembled(inverse, upper, lower, maps, base, n, limits, raw_rows):
    order, width = base.shape
    pivots = inverse.shape[2]
    count = maps.shape[2]
    kr, wc, lr = inverse.shape[1], upper.shape[2], lower.shape[1]
    vmem = pltpu.VMEM
    dma = pltpu.SemaphoreType.DMA
    f32, b16 = jnp.float32, jnp.bfloat16
    chunk = min(256, width)
    chunks = width // chunk
    slots = 4
    packed = limits is not None
    held, extra = n, []
    f_shape, f_sems = (2, chunks, chunk, pivots), (2, chunks)
    u_shape = (n, pivots, wc)
    if packed:
        total_cap, _, cross = limits
        cap_pad, cross_pad = padded(total_cap), padded(cross)
        held = n // 2
        f_shape, f_sems = (2, total_cap, pivots), (2, 2)
        u_shape = (2, held, pivots, wc)
        extra = [
            vmem((2, 8, count), jnp.int32),
            vmem((2, total_cap, 1), jnp.int32),
            vmem((2, 1, cap_pad), jnp.int32),
            vmem((2, 1, cross_pad), jnp.int32),
            vmem((2, cross, pivots), f32),
            vmem((2, cross, pivots), f32),
            vmem((cross_pad, pivots), b16),
            vmem((cross_pad, pivots), b16),
            vmem((cap_pad, pivots), b16),
            vmem((cap_pad, pivots), b16),
            dma((2,)), dma((2,)),
        ]
    whole = pl.BlockSpec(memory_space=pl.ANY)
    return pl.pallas_call(
        functools.partial(front_kernel, n, limits),
        out_shape=[jax.ShapeDtypeStruct((order, width), f32)]
        + [jax.ShapeDtypeStruct((order, pivots), b16)] * 2
        + [jax.ShapeDtypeStruct((width, pivots), b16)] * 2
        + [jax.ShapeDtypeStruct((raw_rows, pivots), f32), jax.ShapeDtypeStruct((1, padded(raw_rows)), jnp.int32)],
        in_specs=[whole] * 3 + [pl.BlockSpec(memory_space=vmem), whole],
        out_specs=[whole] * 7,
        scratch_shapes=[
            vmem((2, 1, count), jnp.int32),
            vmem((2, held, pivots, wc), f32),
            vmem((2, n, kr, pivots), f32),
            vmem((2, n, lr, pivots), f32),
            vmem(u_shape, b16),
            vmem(u_shape, b16),
            vmem((n * kr, pivots), b16),
            vmem((n * kr, pivots), b16),
            vmem((count, pivots), b16),
            vmem((count, pivots), b16),
            vmem((2, order, pivots), b16),
            vmem((2, order, pivots), b16),
            vmem(f_shape, f32),
            vmem((width, pivots), b16),
            vmem((width, pivots), b16),
            vmem((width, pivots), b16),
            vmem((width, pivots), b16),
            vmem((slots, min(1024, order), chunk), f32),
            dma((3,)), dma((3,)), dma((3,)),
            dma((2, 2, n)), dma((2, n)),
            dma((2, 2, n)), dma((2, n)),
            dma((2, 2, n)), dma((2, n)),
            dma(f_sems), dma(f_sems),
            dma((slots,)), dma((slots,)), dma((5,)),
        ] + extra,
        compiler_params=pltpu.CompilerParams(
            collective_id=int(packed), has_side_effects=True, vmem_limit_bytes=63 * 1024 * 1024
        ),
    )(inverse, upper, lower, maps, base)


def finish_kernel(
    n, fits_ref, slot_ref, x_in, high_in, low_in, last_h, last_l, raw_in, out,
    x_buf, high, low, f_h, f_l, raw, g_h, g_l, x_sem, high_sem, low_sem, out_sem, f_sem,
):
    t = lax.axis_index("tile")
    slots, rows, width = x_buf.shape
    blocks = out.shape[0] // rows
    ahead = slots // 2
    chunk = min(256, width)
    expand = (fits_ref[0] > 0) & ((t == 0) | (t == n - 1))

    def loads(i):
        slot = lax.rem(i, slots)
        window = pl.ds(pl.multiple_of(i * rows, rows), rows)
        return [
            pltpu.make_async_copy(source.at[window], target.at[slot], sem.at[slot])
            for source, target, sem in ((high_in, high, high_sem), (low_in, low, low_sem), (x_in, x_buf, x_sem))
        ]

    def store(i):
        slot = lax.rem(i, slots)
        window = pl.ds(pl.multiple_of(i * rows, rows), rows)
        return pltpu.make_async_copy(x_buf.at[slot], out.at[window], out_sem.at[slot])

    packed_copy = pltpu.make_async_copy(raw_in, raw, f_sem.at[0])
    high_copy = pltpu.make_async_copy(last_h, f_h, f_sem.at[1])
    low_copy = pltpu.make_async_copy(last_l, f_l, f_sem.at[2])

    @pl.when(expand)
    def _():
        packed_copy.start()

    @pl.when(~expand)
    def _():
        high_copy.start()
        low_copy.start()

    for i in range(min(ahead, blocks)):
        for copy in loads(i):
            copy.start()

    @pl.when(expand)
    def _():
        packed_copy.wait()
        spread(raw[...], (g_h, g_l))

        @pl.loop(0, width // chunk)
        def _(j):
            base = pl.multiple_of(j * chunk, chunk)
            columns = lax.broadcasted_iota(jnp.int32, (chunk, 1), 0) + (t * width + base)
            choose = one_hot(columns == slot_ref[...])
            f_h[pl.ds(base, chunk), :] = dot(choose, g_h[...]).astype(jnp.bfloat16)
            f_l[pl.ds(base, chunk), :] = dot(choose, g_l[...]).astype(jnp.bfloat16)

    @pl.when(~expand)
    def _():
        high_copy.wait()
        low_copy.wait()

    @pl.loop(0, blocks)
    def _(i):
        @pl.when(i + ahead < blocks)
        def _():
            @pl.when(i >= slots - ahead)
            def _():
                store(i - (slots - ahead)).wait()

            for copy in loads(i + ahead):
                copy.start()

        for copy in loads(i):
            copy.wait()
        slot = lax.rem(i, slots)
        for j in range(width // chunk):
            columns = slice(j * chunk, (j + 1) * chunk)
            total = dot(high[slot], f_h[columns, :], (1, 1))
            total = total + dot(high[slot], f_l[columns, :], (1, 1))
            total = total + dot(low[slot], f_h[columns, :], (1, 1))
            x_buf[slot, :, columns] = x_buf[slot, :, columns] - total
        store(i).start()

    for i in range(max(blocks - slots, 0), blocks):
        store(i).wait()


def finished(n, fits, x, high, low_part, f_h, f_l, raw, slot):
    order, width = x.shape
    pivots = high.shape[1]
    rows, slots = min(512, order), 4
    vmem, dma, b16 = pltpu.VMEM, pltpu.SemaphoreType.DMA, jnp.bfloat16
    whole = pl.BlockSpec(memory_space=pl.ANY)
    return pl.pallas_call(
        functools.partial(finish_kernel, n),
        out_shape=jax.ShapeDtypeStruct(x.shape, x.dtype),
        in_specs=[pl.BlockSpec(memory_space=pltpu.SMEM), pl.BlockSpec(memory_space=vmem)] + [whole] * 6,
        out_specs=whole,
        scratch_shapes=[
            vmem((slots, rows, width), x.dtype),
            vmem((slots, rows, pivots), b16),
            vmem((slots, rows, pivots), b16),
            vmem((width, pivots), b16),
            vmem((width, pivots), b16),
            vmem(raw.shape, raw.dtype),
            vmem((padded(raw.shape[0]), pivots), b16),
            vmem((padded(raw.shape[0]), pivots), b16),
            dma((slots,)), dma((slots,)), dma((slots,)), dma((slots,)), dma((3,)),
        ],
        compiler_params=pltpu.CompilerParams(vmem_limit_bytes=60 * 1024 * 1024),
    )(fits, slot, x, high, low_part, f_h, f_l, raw)


def fits_kernel(ranges, index_ref, out_ref):
    index = index_ref[...]
    early = lax.broadcasted_iota(jnp.int32, index.shape, 2) < index.shape[2] // 2
    over = None
    for start, stop, is_early, limit in ranges:
        inside = (index >= start) & (index < stop)
        if is_early is not None:
            inside &= early if is_early else ~early
        extra = jnp.sum(inside.astype(jnp.int32), axis=2, keepdims=True) - limit
        over = extra if over is None else jnp.maximum(over, extra)
    out_ref[0] = (jnp.max(over) <= 0).astype(jnp.int32)


def shards(pivot_inverse, panel_upper, panel_lower, index_map, parent_base):
    n = lax.axis_size("tile")
    order, width = parent_base.shape[1:]
    count = index_map.shape[2]
    operands = (pivot_inverse[0], panel_upper[0], panel_lower[0], index_map, parent_base[0])

    side = order // 2
    total = capacity(count, width / order, order)
    far = capacity(count // 2, width / order, order)
    cross = capacity(count // 2, 1 / 2, order)

    def run(limits, *args):
        return tuple(assembled(*args, n, limits, total))

    if n != 4 or total >= width or cross >= count // 2:
        return finished(n, jnp.zeros((1,), jnp.int32), *run(None, *operands))[None]

    ranges = (
        (side, order, True, cross), (0, side, False, cross),
        (0, width, None, total), (0, width, False, far),
        (order - width, order, None, total), (order - width, order, True, far),
    )
    fits = pl.pallas_call(
        functools.partial(fits_kernel, ranges),
        out_shape=jax.ShapeDtypeStruct((1,), jnp.int32),
        in_specs=[pl.BlockSpec(memory_space=pltpu.VMEM)],
        out_specs=pl.BlockSpec(memory_space=pltpu.SMEM),
    )(index_map)
    return finished(n, fits, *lax.cond(
        fits[0] > 0, functools.partial(run, (total, far, cross)), functools.partial(run, None), *operands
    ))[None]


def solution(mesh):
    return jax.shard_map(
        shards,
        mesh=mesh,
        in_specs=(
            P("front", None, "tile", None),
            P("front", None, None, "tile"),
            P("front", None, "tile", None),
            P(),
            P("front", None, "tile"),
        ),
        out_specs=P("front", None, "tile"),
        check_vma=False,
    )
```

```python
import functools
import math

import jax
import jax.numpy as jnp
from jax import lax
from jax.experimental import pallas as pl
from jax.experimental.pallas import tpu as pltpu
from jax.sharding import PartitionSpec as P

MESH = pl.DeviceIdType.MESH


def parts(value):
    high = value.astype(jnp.bfloat16)
    return high, (value - high.astype(jnp.float32)).astype(jnp.bfloat16)


def spread(value, targets):
    rows = value.shape[0]
    for ref, part in zip(targets, parts(value)):
        ref[:rows] = part
        if rows < ref.shape[0]:
            ref[rows:] = jnp.zeros((ref.shape[0] - rows, ref.shape[1]), jnp.bfloat16)


def dot(left, right, contract=(1, 0)):
    dims = (((contract[0],), (contract[1],)), ((), ()))
    return lax.dot_general(left, right, dims, preferred_element_type=jnp.float32)


def one_hot(match):
    return match.astype(jnp.float32).astype(jnp.bfloat16)


def front_kernel(
    n, limits, inv_in, up_in, low_in, index_ref, base_in,
    x_out, last_h_out, last_l_out, late_out,
    map_ref, up, inv, low, up_h, up_l, inv_h, inv_l, low_h, low_l, lx_h, lx_l, f_buf, f_h, f_l, x_buf,
    local_sem, part_send, part_recv, up_send, up_recv, inv_send, inv_recv,
    low_send, low_recv, f_send, f_recv, in_sem, out_sem, out_copy_sem, *packing,
):
    packed = limits is not None
    if packed:
        ranks, want, row_want, row_in, c_out, c_in, c_h, c_l, g_h, g_l, c_send, c_recv = packing
        total_cap, far_cap, cross = limits
        split = total_cap - far_cap
    t = lax.axis_index("tile")
    f = lax.axis_index("front")
    partner = lax.rem(f, 2) * -2 + 1 + f
    count = map_ref.shape[2]
    wc = up.shape[3]
    kr = inv.shape[2]
    lr = low.shape[2]
    order, width = x_out.shape
    chunk = min(256, width)
    chunks = width // chunk
    middle = (t >= 1) & (t <= n - 2)
    at_end = (t == 0) | (t == n - 1)
    lower = t < n // 2
    server = (t == 1) | (t == n - 2)
    end = lax.div(t - 1, n - 3) * (n - 1)
    aside = lax.rem(t + 1, n)
    first = jnp.where(lower, 0, n // 2) if packed else 0

    barrier = pltpu.get_barrier_semaphore()
    pl.semaphore_signal(barrier, inc=1, device_id=(partner, t), device_id_type=MESH)

    @pl.when(t > 0)
    def _():
        pl.semaphore_signal(barrier, inc=1, device_id=(f, t - 1), device_id_type=MESH)

    @pl.when(t < n - 1)
    def _():
        pl.semaphore_signal(barrier, inc=1, device_id=(f, t + 1), device_id_type=MESH)

    @pl.when(at_end)
    def _():
        pl.semaphore_wait(barrier, 2)

    @pl.when(middle)
    def _():
        pl.semaphore_wait(barrier, 3)

    sources = (up_in, inv_in, low_in)
    targets = (up, inv, low)

    def place(kind, child, shard):
        return targets[kind].at[child, shard - first if kind == 0 else shard]

    def local(kind):
        return pltpu.make_async_copy(sources[kind].at[0], place(kind, 0, t), local_sem.at[kind])

    def exchange(kind):
        return pltpu.make_async_remote_copy(
            src_ref=sources[kind].at[1], dst_ref=place(kind, 1, t),
            send_sem=part_send.at[kind], recv_sem=part_recv.at[kind],
            device_id=(partner, t), device_id_type=MESH,
        )

    def hop(kind, child, shard, side, source=None):
        send, recv = ((up_send, up_recv), (inv_send, inv_recv), (low_send, low_recv))[kind]
        ref = place(kind, child, shard)
        return pltpu.make_async_remote_copy(
            src_ref=ref if source is None else source, dst_ref=ref,
            send_sem=send.at[side, child, shard], recv_sem=recv.at[child, shard],
            device_id=(f, lax.rem(t + (1 if side == 0 else n - 1), n)), device_id_type=MESH,
        )

    def takes(kind, side):
        if kind == 2:
            return t + 1 <= n - 1 if side == 0 else t - 1 >= 0
        if kind == 0 and packed:
            return t == 0 if side == 0 else t == n - 1
        return t + 1 <= n - 2 if side == 0 else t - 1 >= 1

    def send(kind, child, shard, side, source=None):
        @pl.when(takes(kind, side))
        def _():
            hop(kind, child, shard, side, source).start()

    def send_own(kind, child, source=None):
        send(kind, child, t, 0, source)
        send(kind, child, t, 1, source)

    def pass_on(kinds, child, d, side, where):
        shard = t - d if side == 0 else t + d
        inside = shard >= 0 if side == 0 else shard <= n - 1

        @pl.when(inside & where)
        def _():
            for kind in kinds:
                hop(kind, child, shard, side).wait_recv()
                send(kind, child, shard, side)

    def relay_low(child, d):
        pass_on((2,), child, d, 0, t >= 0)
        pass_on((2,), child, d, 1, t >= 0)

    def inner(child, d, where):
        pass_on((2,), child, d, 1, where & lower)
        pass_on((2,), child, d, 0, where & (t >= n // 2))

    def outer(child, d):
        pass_on((2,), child, d, 0, middle & lower)
        pass_on((2,), child, d, 1, middle & (t >= n // 2))

    kinds = (1,) if packed else (1, 0)

    def near(child):
        @pl.loop(1, n)
        def _(d):
            pass_on(kinds, child, d, 0, middle & lower)
            pass_on(kinds, child, d, 1, middle & (t >= n // 2))

    def far(child):
        @pl.loop(1, n)
        def _(d):
            pass_on(kinds, child, d, 1, middle & lower)
            pass_on(kinds, child, d, 0, middle & (t >= n // 2))

    def listed(child, shard):
        return map_ref[child, :, pl.ds(pl.multiple_of(shard * wc, wc), wc)]

    def tables(child):
        row = lax.broadcasted_iota(jnp.int32, (8, 1), 0)
        side = order // 2
        tile = jnp.where(middle, end, t) * width
        ours = jnp.where(lower, 0, side)
        starts = (tile, tile, side - ours, ours)
        spans = (width, width, side, side)
        low_end = high_end = jnp.zeros((8, 1), jnp.int32)
        for q in range(4):
            low_end = jnp.where(row == q, starts[q], low_end)
            high_end = jnp.where(row == q, starts[q] + spans[q], high_end)
        before = lax.broadcasted_iota(jnp.int32, (wc, wc), 0) < lax.broadcasted_iota(jnp.int32, (wc, wc), 1)
        before = one_hot(before)
        passed = jnp.zeros((8, 1), jnp.float32)
        which = lax.broadcasted_iota(jnp.int32, (8, wc), 0)
        wants = jnp.zeros((total_cap, 8), jnp.float32)
        both = jnp.zeros((8, row_want.shape[2]), jnp.float32)
        inward = jnp.zeros((8, row_in.shape[2]), jnp.float32)
        for s in range(n):
            columns = map_ref[child, :, s * wc:(s + 1) * wc]
            is_ours = (first <= s) & (s < first + n // 2)
            fits = jnp.where(lax.rem(row, 2) == 0, is_ours.astype(jnp.int32), 1 - is_ours.astype(jnp.int32)) > 0
            inside = (columns >= low_end) & (columns < high_end) & fits
            mark = one_hot(inside)
            rank = jnp.where(inside, (dot(mark, before) + passed).astype(jnp.int32), -2 * count)
            passed = passed + jnp.sum(mark.astype(jnp.float32), axis=1, keepdims=True)
            ranks[child, :, s * wc:(s + 1) * wc] = rank
            digits = jnp.where(which == 0, columns >> 7, jnp.where(which == 1, columns & 127, 1))
            digits = digits.astype(jnp.float32).astype(jnp.bfloat16)

            def pick(q, size):
                slot = lax.broadcasted_iota(jnp.int32, (size, wc), 0)
                return one_hot((total_cap - 1 - slot if q == 1 else slot) == rank[q:q + 1])

            for q in range(2):
                wants = wants + dot(pick(q, total_cap), digits, (1, 1))
                both = both + dot(digits, pick(q, both.shape[1]), (1, 1))
            inward = inward + dot(digits, pick(3, inward.shape[1]), (1, 1))

        def across(found):
            value = found[0:1].astype(jnp.int32) * 128 + found[1:2].astype(jnp.int32)
            return jnp.where(found[2:3] > 0, value, -1)

        found = wants.astype(jnp.int32)
        want[child] = jnp.where(found[:, 2:3] > 0, found[:, 0:1] * 128 + found[:, 1:2], -1)
        row_want[child] = across(both)
        row_in[child] = across(inward)

    def cross_copy(child):
        return pltpu.make_async_remote_copy(
            src_ref=c_out.at[child], dst_ref=c_in.at[child],
            send_sem=c_send.at[child], recv_sem=c_recv.at[child],
            device_id=(f, n - 1 - t), device_id_type=MESH,
        )

    def pack(child):
        @pl.when(middle)
        def _():
            @pl.when(lower)
            def _():
                hop(0, child, 0, 0).wait_recv()

            @pl.when(t >= n // 2)
            def _():
                hop(0, child, n - 1, 1).wait_recv()

            for k in range(n // 2):
                high, low_part = parts(up[child, k])
                up_h[child, k] = high
                up_l[child, k] = low_part
            total = None
            for k in range(n // 2):
                shard = pl.ds(pl.multiple_of((first + k) * wc, wc), wc)
                rank = ranks[child, 2:3, shard]
                choose = one_hot(lax.broadcasted_iota(jnp.int32, (cross, wc), 0) == rank)
                piece = dot(choose, up_h[child, k], (1, 1)) + dot(choose, up_l[child, k], (1, 1))
                total = piece if total is None else total + piece
            c_out[child] = total
            cross_copy(child).start()

    def place_rows(child):
        held = (n - 1 if packed and child == 1 else n) * lr
        from_shard = jnp.where(lower, 0, 1) if packed and child == 1 else 0
        used = pl.ds(pl.multiple_of(from_shard * lr, lr), held)

        @pl.loop(from_shard, from_shard + held // lr)
        def _(s):
            rows = pl.ds(pl.multiple_of(s * lr, lr), lr)
            high, low_part = parts(low[child, s])
            low_h[rows, :] = high
            low_l[rows, :] = low_part

        span = min(512, order)

        @pl.loop(0, order // span)
        def _(j):
            base = pl.multiple_of(j * span, span)
            rows = lax.broadcasted_iota(jnp.int32, (span, held), 0) + base
            choose = one_hot(rows == map_ref[child, :, used])
            lx_h[child, pl.ds(base, span), :] = dot(choose, low_h[used, :]).astype(jnp.bfloat16)
            lx_l[child, pl.ds(base, span), :] = dot(choose, low_l[used, :]).astype(jnp.bfloat16)

    def split_inverse(child):
        @pl.loop(0, n)
        def _(s):
            rows = pl.ds(pl.multiple_of(s * kr, kr), kr)
            high, low_part = parts(inv[child, s])
            inv_h[rows, :] = high
            inv_l[rows, :] = low_part

    def factor(child, columns, near_side=True, far_side=True):
        terms = []
        if near_side:
            for s in range(n // 2 if packed else n):
                choose = one_hot(columns == listed(child, first + s))
                index = (child, s) if packed else s
                terms.append((dot(choose, up_h[index], (1, 1)), dot(choose, up_l[index], (1, 1))))
        if packed and far_side:
            choose = one_hot(columns == row_in[child])
            terms.append((dot(choose, c_h[...]), dot(choose, c_l[...])))
        high, low_part = terms[0]
        for a, b in terms[1:]:
            high = high + a
            low_part = low_part + b
        high = high.astype(jnp.bfloat16)
        low_part = low_part.astype(jnp.bfloat16)
        total = dot(high, inv_h[...], (1, 1))
        total = total + dot(low_part, inv_h[...], (1, 1))
        return total + dot(high, inv_l[...], (1, 1))

    def strip(j):
        return pl.ds(pl.multiple_of(j * chunk, chunk), chunk)

    def range_of(start):
        return lax.broadcasted_iota(jnp.int32, (chunk, 1), 0) + start

    def slots_of(j):
        return slice(0, split) if j == 0 else slice(split, total_cap)

    def end_copy(child, j, target):
        if packed:
            ref = f_buf.at[child, slots_of(j)]
        else:
            ref = f_buf.at[child, j]
        return pltpu.make_async_remote_copy(
            src_ref=ref, dst_ref=ref,
            send_sem=f_send.at[child, j], recv_sem=f_recv.at[child, j],
            device_id=(f, target), device_id_type=MESH,
        )

    def keep(child, j, value):
        for ref, part in zip((f_h, f_l), parts(value)):
            ref[child, strip(j), :] = part

    def serve_near(child):
        @pl.when(middle)
        def _():
            split_inverse(child)
            f_buf[child, slots_of(0)] = factor(child, want[child, slots_of(0)], far_side=False)
            end_copy(child, 0, end).start()

    def serve_far(child):
        @pl.when(middle)
        def _():
            cross_copy(child).wait_recv()
            high, low_part = parts(c_in[child])
            rest = jnp.zeros((c_h.shape[0] - cross, c_h.shape[1]), jnp.bfloat16)
            c_h[:cross] = high
            c_l[:cross] = low_part
            c_h[cross:] = rest
            c_l[cross:] = rest
            f_buf[child, slots_of(1)] = factor(child, want[child, slots_of(1)])
            end_copy(child, 1, end).start()

    def serve_all(child):
        @pl.when(middle)
        def _():
            split_inverse(child)

            @pl.loop(0, n)
            def _(s):
                high, low_part = parts(up[child, s])
                up_h[s] = high
                up_l[s] = low_part

            @pl.when(server)
            def _():
                @pl.loop(0, chunks)
                def _(j):
                    f_buf[child, j] = factor(child, range_of(end * width + j * chunk))
                    end_copy(child, j, end).start()

    def serve_own(child):
        @pl.when(middle)
        def _():
            @pl.loop(0, chunks)
            def _(j):
                keep(child, j, factor(child, range_of(t * width + j * chunk)))

    def take_factor(child):
        @pl.when(at_end)
        def _():
            if packed:
                for q in range(2):
                    end_copy(child, q, aside).wait_recv()
                spread(f_buf[child], (g_h, g_l))

            @pl.loop(0, chunks)
            def _(j):
                if packed:
                    choose = one_hot(range_of(t * width + j * chunk) == row_want[child])
                    for ref, source in ((f_h, g_h), (f_l, g_l)):
                        ref[child, strip(j), :] = dot(choose, source[...]).astype(jnp.bfloat16)
                else:
                    end_copy(child, j, aside).wait_recv()
                    keep(child, j, f_buf[child, j])

    slots = x_buf.shape[0]
    ahead = slots // 2
    tall = x_buf.shape[1]
    per = order // tall
    blocks = per * chunks

    def window(ref, i):
        rows = pl.ds(pl.multiple_of(lax.rem(i, per) * tall, tall), tall)
        return ref.at[rows, strip(lax.div(i, per))]

    def subtract(child, begin, stop):
        source = base_in if child == 0 else x_out

        def load(i):
            slot = lax.rem(i, slots)
            return pltpu.make_async_copy(window(source, i), x_buf.at[slot], in_sem.at[slot])

        def store(i):
            slot = lax.rem(i, slots)
            return pltpu.make_async_copy(x_buf.at[slot], window(x_out, i), out_sem.at[slot])

        for i in range(begin, min(begin + ahead, stop)):
            load(i).start()
        if begin == 0:
            take_factor(child)

        @pl.loop(begin, stop)
        def _(i):
            j = lax.div(i, per)

            @pl.when(i + ahead < stop)
            def _():
                @pl.when(i >= begin + slots - ahead)
                def _():
                    store(i - (slots - ahead)).wait()

                load(i + ahead).start()

            rows = pl.ds(pl.multiple_of(lax.rem(i, per) * tall, tall), tall)
            high = f_h[child, strip(j), :]
            left = lx_h[child, rows, :]
            total = dot(left, high, (1, 1))
            total = total + dot(left, f_l[child, strip(j), :], (1, 1))
            total = total + dot(lx_l[child, rows, :], high, (1, 1))
            load(i).wait()
            slot = lax.rem(i, slots)
            x_buf[slot] = x_buf[slot] - total
            store(i).start()

        for i in range(max(stop - slots, begin), stop):
            store(i).wait()

    def hand_on(k):
        if k < 2:
            return pltpu.make_async_copy((f_h, f_l)[k].at[1], (last_h_out, last_l_out)[k], out_copy_sem.at[k])
        return pltpu.make_async_copy(low.at[1, late], late_out, out_copy_sem.at[k])

    late = jnp.where(lower, n - 1, 0) if packed else 0
    send_own(2, 0, low_in.at[0])
    for kind in (2, 1, 0):
        exchange(kind).start()
        local(kind).start()
    exchange(2).wait()

    @pl.when(middle if packed else t >= 0)
    def _():
        send_own(2, 1)

    local(2).wait()
    for kind in (1, 0):
        local(kind).wait()
        exchange(kind).wait()

    @pl.when(at_end)
    def _():
        for child in range(2):
            for kind in (1, 0):
                send_own(kind, child)
        if packed:
            send_own(2, 1)

    for child in range(2):
        map_ref[child] = index_ref[f if child == 0 else partner, child:child + 1, :]
    if packed:
        for child in range(2):
            tables(child)

        @pl.when(middle)
        def _():
            outer(0, 1)
            inner(0, 1, middle)
            send_own(1, 0)
            near(0)
            inner(1, 1, middle)
            pack(0)
            send_own(1, 1)
            near(1)
            inner(0, 2, middle)

        @pl.when(at_end)
        def _():
            for child, d in ((0, 1), (1, 1), (0, 2), (1, 2), (0, 3)):
                inner(child, d, at_end)

        place_rows(0)

        @pl.when(middle)
        def _():
            pack(1)
            far(0)
            serve_near(0)
            outer(1, 1)
            serve_far(0)
            serve_own(0)

        place_rows(1)

        @pl.when(middle)
        def _():
            far(1)
            serve_near(1)

        subtract(0, 0, blocks // 2)

        @pl.when(middle)
        def _():
            serve_far(1)
            serve_own(1)

        subtract(0, blocks // 2, blocks)
        inner(1, 2, middle)
        subtract(1, 0, blocks)
        for k in range(2):
            hand_on(k).start()
        inner(1, 3, at_end)
        hand_on(2).start()
        for k in range(3):
            hand_on(k).wait()
    else:
        relay_low(0, 1)
        relay_low(1, 1)

        @pl.when(middle)
        def _():
            send_own(1, 0)
            send_own(0, 0)

        relay_low(0, 2)
        near(0)

        @pl.when(middle)
        def _():
            send_own(1, 1)
            send_own(0, 1)

        relay_low(1, 2)

        @pl.loop(3, n)
        def _(d):
            relay_low(0, d)
            relay_low(1, d)

        near(1)
        place_rows(0)
        place_rows(1)
        for child in range(2):
            far(child)
            serve_all(child)
            serve_own(child)
            subtract(child, 0, blocks)
        for k in range(2):
            hand_on(k).start()
            hand_on(k).wait()

    for child in range(2):
        @pl.loop(0, n)
        def _(s):
            for side in range(2):
                for kind in range(3):
                    @pl.when(takes(kind, side) & (s <= t if side == 0 else s >= t))
                    def _():
                        hop(kind, child, s, side).wait_send()

        @pl.when(server)
        def _():
            if packed:
                for j in range(2):
                    end_copy(child, j, aside).wait_send()
            else:
                @pl.loop(0, chunks)
                def _(j):
                    end_copy(child, j, aside).wait_send()

        if packed:
            @pl.when(middle)
            def _():
                cross_copy(child).wait_send()

    if not packed:
        low[1, late] = jnp.zeros(late_out.shape, jnp.float32)
        hand_on(2).start()
        hand_on(2).wait()


def capacity(draws, share, order):
    spread_of = math.sqrt(draws * share * (1 - share) * (1 - draws / order))
    return -(-math.ceil(draws * share + 4.5 * spread_of) // 8) * 8


def padded(rows):
    return -(-rows // 128) * 128


def assembled(inverse, upper, lower, maps, base, n, limits):
    order, width = base.shape
    pivots = inverse.shape[2]
    count = maps.shape[2]
    kr, wc, lr = inverse.shape[1], upper.shape[2], lower.shape[1]
    vmem = pltpu.VMEM
    dma = pltpu.SemaphoreType.DMA
    f32, b16 = jnp.float32, jnp.bfloat16
    chunk = min(256, width)
    chunks = width // chunk
    slots = 4
    packed = limits is not None
    held, extra = n, []
    f_shape, f_sems = (2, chunks, chunk, pivots), (2, chunks)
    u_shape = (n, pivots, wc)
    if packed:
        total_cap, _, cross = limits
        cap_pad, cross_pad = padded(total_cap), padded(cross)
        held = n // 2
        f_shape, f_sems = (2, total_cap, pivots), (2, 2)
        u_shape = (2, held, pivots, wc)
        extra = [
            vmem((2, 8, count), jnp.int32),
            vmem((2, total_cap, 1), jnp.int32),
            vmem((2, 1, cap_pad), jnp.int32),
            vmem((2, 1, cross_pad), jnp.int32),
            vmem((2, cross, pivots), f32),
            vmem((2, cross, pivots), f32),
            vmem((cross_pad, pivots), b16),
            vmem((cross_pad, pivots), b16),
            vmem((cap_pad, pivots), b16),
            vmem((cap_pad, pivots), b16),
            dma((2,)), dma((2,)),
        ]
    whole = pl.BlockSpec(memory_space=pl.ANY)
    return pl.pallas_call(
        functools.partial(front_kernel, n, limits),
        out_shape=[jax.ShapeDtypeStruct((order, width), f32)]
        + [jax.ShapeDtypeStruct((width, pivots), b16)] * 2
        + [jax.ShapeDtypeStruct((lr, pivots), f32)],
        in_specs=[whole] * 3 + [pl.BlockSpec(memory_space=vmem), whole],
        out_specs=[whole] * 4,
        scratch_shapes=[
            vmem((2, 1, count), jnp.int32),
            vmem((2, held, pivots, wc), f32),
            vmem((2, n, kr, pivots), f32),
            vmem((2, n, lr, pivots), f32),
            vmem(u_shape, b16),
            vmem(u_shape, b16),
            vmem((n * kr, pivots), b16),
            vmem((n * kr, pivots), b16),
            vmem((count, pivots), b16),
            vmem((count, pivots), b16),
            vmem((2, order, pivots), b16),
            vmem((2, order, pivots), b16),
            vmem(f_shape, f32),
            vmem((2, width, pivots), b16),
            vmem((2, width, pivots), b16),
            vmem((slots, min(1024, order), chunk), f32),
            dma((3,)), dma((3,)), dma((3,)),
            dma((2, 2, n)), dma((2, n)),
            dma((2, 2, n)), dma((2, n)),
            dma((2, 2, n)), dma((2, n)),
            dma(f_sems), dma(f_sems),
            dma((slots,)), dma((slots,)), dma((3,)),
        ] + extra,
        compiler_params=pltpu.CompilerParams(
            collective_id=int(packed), has_side_effects=True, vmem_limit_bytes=63 * 1024 * 1024
        ),
    )(inverse, upper, lower, maps, base)


def finish_kernel(
    n, index_ref, x_in, last_h, last_l, late_in, out,
    x_buf, f_h, f_l, late, u_h, u_l, x_sem, out_sem, f_sem,
):
    t = lax.axis_index("tile")
    f = lax.axis_index("front")
    partner = lax.rem(f, 2) * -2 + 1 + f
    slots, rows, width = x_buf.shape
    lr = late.shape[0]
    blocks = out.shape[0] // rows
    ahead = slots // 2
    chunk = min(256, width)
    shard = jnp.where(t < n // 2, n - 1, 0)
    places = index_ref[partner, 1:2, pl.ds(pl.multiple_of(shard * lr, lr), lr)]

    def window(i):
        return pl.ds(pl.multiple_of(i * rows, rows), rows)

    def load(i):
        slot = lax.rem(i, slots)
        return pltpu.make_async_copy(x_in.at[window(i)], x_buf.at[slot], x_sem.at[slot])

    def store(i):
        slot = lax.rem(i, slots)
        return pltpu.make_async_copy(x_buf.at[slot], out.at[window(i)], out_sem.at[slot])

    first = [
        pltpu.make_async_copy(source, target, f_sem.at[k])
        for k, (source, target) in enumerate(((late_in, late), (last_h, f_h), (last_l, f_l)))
    ]
    for copy in first:
        copy.start()
    for i in range(min(ahead, blocks)):
        load(i).start()
    for copy in first:
        copy.wait()
    left = parts(late[...])
    for j in range(width // chunk):
        columns = slice(j * chunk, (j + 1) * chunk)
        total = dot(left[0], f_h[columns, :], (1, 1))
        total = total + dot(left[0], f_l[columns, :], (1, 1))
        total = total + dot(left[1], f_h[columns, :], (1, 1))
        u_h[:, columns], u_l[:, columns] = parts(total)

    @pl.loop(0, blocks)
    def _(i):
        @pl.when(i + ahead < blocks)
        def _():
            @pl.when(i >= slots - ahead)
            def _():
                store(i - (slots - ahead)).wait()

            load(i + ahead).start()

        choose = one_hot(lax.broadcasted_iota(jnp.int32, (rows, lr), 0) + i * rows == places)
        load(i).wait()
        slot = lax.rem(i, slots)
        for j in range(width // chunk):
            columns = slice(j * chunk, (j + 1) * chunk)
            total = dot(choose, u_h[:, columns]) + dot(choose, u_l[:, columns])
            x_buf[slot, :, columns] = x_buf[slot, :, columns] - total
        store(i).start()

    for i in range(max(blocks - slots, 0), blocks):
        store(i).wait()


def finished(n, index_map, x, f_h, f_l, late):
    order, width = x.shape
    rows, slots = min(512, order), 4
    vmem, dma, b16 = pltpu.VMEM, pltpu.SemaphoreType.DMA, jnp.bfloat16
    whole = pl.BlockSpec(memory_space=pl.ANY)
    return pl.pallas_call(
        functools.partial(finish_kernel, n),
        out_shape=jax.ShapeDtypeStruct(x.shape, x.dtype),
        in_specs=[pl.BlockSpec(memory_space=vmem)] + [whole] * 4,
        out_specs=whole,
        scratch_shapes=[
            vmem((slots, rows, width), x.dtype),
            vmem(f_h.shape, b16),
            vmem(f_h.shape, b16),
            vmem(late.shape, late.dtype),
            vmem((late.shape[0], width), b16),
            vmem((late.shape[0], width), b16),
            dma((slots,)), dma((slots,)), dma((3,)),
        ],
        compiler_params=pltpu.CompilerParams(vmem_limit_bytes=60 * 1024 * 1024),
    )(index_map, x, f_h, f_l, late)


def fits_kernel(ranges, index_ref, out_ref):
    index = index_ref[...]
    early = lax.broadcasted_iota(jnp.int32, index.shape, 2) < index.shape[2] // 2
    over = None
    for start, stop, is_early, limit in ranges:
        inside = (index >= start) & (index < stop)
        if is_early is not None:
            inside &= early if is_early else ~early
        extra = jnp.sum(inside.astype(jnp.int32), axis=2, keepdims=True) - limit
        over = extra if over is None else jnp.maximum(over, extra)
    out_ref[0] = (jnp.max(over) <= 0).astype(jnp.int32)


def shards(pivot_inverse, panel_upper, panel_lower, index_map, parent_base):
    n = lax.axis_size("tile")
    order, width = parent_base.shape[1:]
    count = index_map.shape[2]
    operands = (pivot_inverse[0], panel_upper[0], panel_lower[0], index_map, parent_base[0])

    side = order // 2
    total = capacity(count, width / order, order)
    far = capacity(count // 2, width / order, order)
    cross = capacity(count // 2, 1 / 2, order)

    def run(limits, *args):
        return tuple(assembled(*args, n, limits))

    if n != 4 or total >= width or cross >= count // 2:
        return finished(n, index_map, *run(None, *operands))[None]

    ranges = (
        (side, order, True, cross), (0, side, False, cross),
        (0, width, None, total), (0, width, False, far),
        (order - width, order, None, total), (order - width, order, True, far),
    )
    fits = pl.pallas_call(
        functools.partial(fits_kernel, ranges),
        out_shape=jax.ShapeDtypeStruct((1,), jnp.int32),
        in_specs=[pl.BlockSpec(memory_space=pltpu.VMEM)],
        out_specs=pl.BlockSpec(memory_space=pltpu.SMEM),
    )(index_map)
    return finished(n, index_map, *lax.cond(
        fits[0] > 0, functools.partial(run, (total, far, cross)), functools.partial(run, None), *operands
    ))[None]


def solution(mesh):
    return jax.shard_map(
        shards,
        mesh=mesh,
        in_specs=(
            P("front", None, "tile", None),
            P("front", None, None, "tile"),
            P("front", None, "tile", None),
            P(),
            P("front", None, "tile"),
        ),
        out_specs=P("front", None, "tile"),
        check_vma=False,
    )
```

```python
import functools
import math

import jax
import jax.numpy as jnp
from jax import lax
from jax.experimental import pallas as pl
from jax.experimental.pallas import tpu as pltpu
from jax.sharding import PartitionSpec as P

MESH = pl.DeviceIdType.MESH


def parts(value):
    high = value.astype(jnp.bfloat16)
    return high, (value - high.astype(jnp.float32)).astype(jnp.bfloat16)


def spread(value, targets):
    rows = value.shape[0]
    for ref, part in zip(targets, parts(value)):
        ref[:rows] = part
        if rows < ref.shape[0]:
            ref[rows:] = jnp.zeros((ref.shape[0] - rows, ref.shape[1]), jnp.bfloat16)


def dot(left, right, contract=(1, 0)):
    dims = (((contract[0],), (contract[1],)), ((), ()))
    return lax.dot_general(left, right, dims, preferred_element_type=jnp.float32)


def one_hot(match):
    return match.astype(jnp.float32).astype(jnp.bfloat16)


def front_kernel(
    n, limits, inv_in, up_in, low_in, index_ref, base_in,
    x_out, last_h_out, last_l_out, late_out,
    map_ref, up, inv, low, up_h, up_l, inv_h, inv_l, low_h, low_l, lx_h, lx_l, f_buf, f_h, f_l, x_buf,
    local_sem, part_send, part_recv, up_send, up_recv, inv_send, inv_recv,
    low_send, low_recv, f_send, f_recv, in_sem, out_sem, out_copy_sem, *packing,
):
    packed = limits is not None
    if packed:
        ranks, want, row_want, row_in, c_out, c_in, c_h, c_l, g_h, g_l, c_send, c_recv = packing
        total_cap, far_cap, cross = limits
        split = total_cap - far_cap
    t = lax.axis_index("tile")
    f = lax.axis_index("front")
    partner = lax.rem(f, 2) * -2 + 1 + f
    count = map_ref.shape[2]
    wc = up.shape[3]
    kr = inv.shape[2]
    lr = low.shape[2]
    order, width = x_out.shape
    chunk = min(256, width)
    chunks = width // chunk
    middle = (t >= 1) & (t <= n - 2)
    at_end = (t == 0) | (t == n - 1)
    lower = t < n // 2
    server = (t == 1) | (t == n - 2)
    end = lax.div(t - 1, n - 3) * (n - 1)
    aside = lax.rem(t + 1, n)
    first = jnp.where(lower, 0, n // 2) if packed else 0

    barrier = pltpu.get_barrier_semaphore()
    pl.semaphore_signal(barrier, inc=1, device_id=(partner, t), device_id_type=MESH)

    @pl.when(t > 0)
    def _():
        pl.semaphore_signal(barrier, inc=1, device_id=(f, t - 1), device_id_type=MESH)

    @pl.when(t < n - 1)
    def _():
        pl.semaphore_signal(barrier, inc=1, device_id=(f, t + 1), device_id_type=MESH)

    @pl.when(at_end)
    def _():
        pl.semaphore_wait(barrier, 2)

    @pl.when(middle)
    def _():
        pl.semaphore_wait(barrier, 3)

    sources = (up_in, inv_in, low_in)
    targets = (up, inv, low)

    def place(kind, child, shard):
        return targets[kind].at[child, shard - first if kind == 0 else shard]

    def local(kind):
        return pltpu.make_async_copy(sources[kind].at[0], place(kind, 0, t), local_sem.at[kind])

    def exchange(kind):
        return pltpu.make_async_remote_copy(
            src_ref=sources[kind].at[1], dst_ref=place(kind, 1, t),
            send_sem=part_send.at[kind], recv_sem=part_recv.at[kind],
            device_id=(partner, t), device_id_type=MESH,
        )

    def hop(kind, child, shard, side, source=None):
        send, recv = ((up_send, up_recv), (inv_send, inv_recv), (low_send, low_recv))[kind]
        ref = place(kind, child, shard)
        return pltpu.make_async_remote_copy(
            src_ref=ref if source is None else source, dst_ref=ref,
            send_sem=send.at[side, child, shard], recv_sem=recv.at[child, shard],
            device_id=(f, lax.rem(t + (1 if side == 0 else n - 1), n)), device_id_type=MESH,
        )

    def takes(kind, side):
        if kind == 2:
            return t + 1 <= n - 1 if side == 0 else t - 1 >= 0
        if kind == 0 and packed:
            return t == 0 if side == 0 else t == n - 1
        return t + 1 <= n - 2 if side == 0 else t - 1 >= 1

    def send(kind, child, shard, side, source=None):
        @pl.when(takes(kind, side))
        def _():
            hop(kind, child, shard, side, source).start()

    def send_own(kind, child, source=None):
        send(kind, child, t, 0, source)
        send(kind, child, t, 1, source)

    def pass_on(kinds, child, d, side, where):
        shard = t - d if side == 0 else t + d
        inside = shard >= 0 if side == 0 else shard <= n - 1

        @pl.when(inside & where)
        def _():
            for kind in kinds:
                hop(kind, child, shard, side).wait_recv()
                send(kind, child, shard, side)

    def relay_low(child, d):
        pass_on((2,), child, d, 0, t >= 0)
        pass_on((2,), child, d, 1, t >= 0)

    def inner(child, d, where):
        pass_on((2,), child, d, 1, where & lower)
        pass_on((2,), child, d, 0, where & (t >= n // 2))

    def outer(child, d):
        pass_on((2,), child, d, 0, middle & lower)
        pass_on((2,), child, d, 1, middle & (t >= n // 2))

    kinds = (1,) if packed else (1, 0)

    def near(child):
        @pl.loop(1, n)
        def _(d):
            pass_on(kinds, child, d, 0, middle & lower)
            pass_on(kinds, child, d, 1, middle & (t >= n // 2))

    def far(child):
        @pl.loop(1, n)
        def _(d):
            pass_on(kinds, child, d, 1, middle & lower)
            pass_on(kinds, child, d, 0, middle & (t >= n // 2))

    def listed(child, shard):
        return map_ref[child, :, pl.ds(pl.multiple_of(shard * wc, wc), wc)]

    def tables(child):
        row = lax.broadcasted_iota(jnp.int32, (8, 1), 0)
        side = order // 2
        tile = jnp.where(middle, end, t) * width
        ours = jnp.where(lower, 0, side)
        starts = (tile, tile, side - ours, ours)
        spans = (width, width, side, side)
        low_end = high_end = jnp.zeros((8, 1), jnp.int32)
        for q in range(4):
            low_end = jnp.where(row == q, starts[q], low_end)
            high_end = jnp.where(row == q, starts[q] + spans[q], high_end)
        before = lax.broadcasted_iota(jnp.int32, (wc, wc), 0) < lax.broadcasted_iota(jnp.int32, (wc, wc), 1)
        before = one_hot(before)
        passed = jnp.zeros((8, 1), jnp.float32)
        which = lax.broadcasted_iota(jnp.int32, (8, wc), 0)
        wants = jnp.zeros((total_cap, 8), jnp.float32)
        both = jnp.zeros((8, row_want.shape[2]), jnp.float32)
        inward = jnp.zeros((8, row_in.shape[2]), jnp.float32)
        for s in range(n):
            columns = map_ref[child, :, s * wc:(s + 1) * wc]
            is_ours = (first <= s) & (s < first + n // 2)
            fits = jnp.where(lax.rem(row, 2) == 0, is_ours.astype(jnp.int32), 1 - is_ours.astype(jnp.int32)) > 0
            inside = (columns >= low_end) & (columns < high_end) & fits
            mark = one_hot(inside)
            rank = jnp.where(inside, (dot(mark, before) + passed).astype(jnp.int32), -2 * count)
            passed = passed + jnp.sum(mark.astype(jnp.float32), axis=1, keepdims=True)
            ranks[child, :, s * wc:(s + 1) * wc] = rank
            digits = jnp.where(which == 0, columns >> 7, jnp.where(which == 1, columns & 127, 1))
            digits = digits.astype(jnp.float32).astype(jnp.bfloat16)

            def pick(q, size):
                slot = lax.broadcasted_iota(jnp.int32, (size, wc), 0)
                return one_hot((total_cap - 1 - slot if q == 1 else slot) == rank[q:q + 1])

            for q in range(2):
                wants = wants + dot(pick(q, total_cap), digits, (1, 1))
                both = both + dot(digits, pick(q, both.shape[1]), (1, 1))
            inward = inward + dot(digits, pick(3, inward.shape[1]), (1, 1))

        def across(found):
            value = found[0:1].astype(jnp.int32) * 128 + found[1:2].astype(jnp.int32)
            return jnp.where(found[2:3] > 0, value, -1)

        found = wants.astype(jnp.int32)
        want[child] = jnp.where(found[:, 2:3] > 0, found[:, 0:1] * 128 + found[:, 1:2], -1)
        row_want[child] = across(both)
        row_in[child] = across(inward)

    def cross_copy(child):
        return pltpu.make_async_remote_copy(
            src_ref=c_out.at[child], dst_ref=c_in.at[child],
            send_sem=c_send.at[child], recv_sem=c_recv.at[child],
            device_id=(f, n - 1 - t), device_id_type=MESH,
        )

    def pack(child):
        @pl.when(middle)
        def _():
            @pl.when(lower)
            def _():
                hop(0, child, 0, 0).wait_recv()

            @pl.when(t >= n // 2)
            def _():
                hop(0, child, n - 1, 1).wait_recv()

            for k in range(n // 2):
                high, low_part = parts(up[child, k])
                up_h[child, k] = high
                up_l[child, k] = low_part
            step = cross // 4 if cross % 32 == 0 else cross

            @pl.loop(0, cross // step)
            def _(j):
                base = pl.multiple_of(j * step, 8)
                total = None
                for k in range(n // 2):
                    shard = pl.ds(pl.multiple_of((first + k) * wc, wc), wc)
                    rank = ranks[child, 2:3, shard] - base
                    choose = one_hot(lax.broadcasted_iota(jnp.int32, (step, wc), 0) == rank)
                    piece = dot(choose, up_h[child, k], (1, 1)) + dot(choose, up_l[child, k], (1, 1))
                    total = piece if total is None else total + piece
                c_out[child, pl.ds(base, step), :] = total

            cross_copy(child).start()

    def place_rows(child):
        held = (n - 1 if packed and child == 1 else n) * lr
        from_shard = jnp.where(lower, 0, 1) if packed and child == 1 else 0
        used = pl.ds(pl.multiple_of(from_shard * lr, lr), held)

        @pl.loop(from_shard, from_shard + held // lr)
        def _(s):
            rows = pl.ds(pl.multiple_of(s * lr, lr), lr)
            high, low_part = parts(low[child, s])
            low_h[rows, :] = high
            low_l[rows, :] = low_part

        span = min(512, order)

        @pl.loop(0, order // span)
        def _(j):
            base = pl.multiple_of(j * span, span)
            rows = lax.broadcasted_iota(jnp.int32, (span, held), 0) + base
            choose = one_hot(rows == map_ref[child, :, used])
            lx_h[child, pl.ds(base, span), :] = dot(choose, low_h[used, :]).astype(jnp.bfloat16)
            lx_l[child, pl.ds(base, span), :] = dot(choose, low_l[used, :]).astype(jnp.bfloat16)

    def split_inverse(child):
        @pl.loop(0, n)
        def _(s):
            rows = pl.ds(pl.multiple_of(s * kr, kr), kr)
            high, low_part = parts(inv[child, s])
            inv_h[rows, :] = high
            inv_l[rows, :] = low_part

    def factor(child, columns, near_side=True, far_side=True):
        terms = []
        if near_side:
            for s in range(n // 2 if packed else n):
                choose = one_hot(columns == listed(child, first + s))
                index = (child, s) if packed else s
                terms.append((dot(choose, up_h[index], (1, 1)), dot(choose, up_l[index], (1, 1))))
        if packed and far_side:
            choose = one_hot(columns == row_in[child])
            terms.append((dot(choose, c_h[...]), dot(choose, c_l[...])))
        high, low_part = terms[0]
        for a, b in terms[1:]:
            high = high + a
            low_part = low_part + b
        high = high.astype(jnp.bfloat16)
        low_part = low_part.astype(jnp.bfloat16)
        total = dot(high, inv_h[...], (1, 1))
        total = total + dot(low_part, inv_h[...], (1, 1))
        return total + dot(high, inv_l[...], (1, 1))

    def strip(j):
        return pl.ds(pl.multiple_of(j * chunk, chunk), chunk)

    def range_of(start):
        return lax.broadcasted_iota(jnp.int32, (chunk, 1), 0) + start

    def slots_of(j):
        return slice(0, split) if j == 0 else slice(split, total_cap)

    def end_copy(child, j, target):
        if packed:
            ref = f_buf.at[child, slots_of(j)]
        else:
            ref = f_buf.at[child, j]
        return pltpu.make_async_remote_copy(
            src_ref=ref, dst_ref=ref,
            send_sem=f_send.at[child, j], recv_sem=f_recv.at[child, j],
            device_id=(f, target), device_id_type=MESH,
        )

    def keep(child, j, value):
        for ref, part in zip((f_h, f_l), parts(value)):
            ref[child, strip(j), :] = part

    def serve_near(child):
        @pl.when(middle)
        def _():
            split_inverse(child)
            f_buf[child, slots_of(0)] = factor(child, want[child, slots_of(0)], far_side=False)
            end_copy(child, 0, end).start()

    def serve_far(child):
        @pl.when(middle)
        def _():
            cross_copy(child).wait_recv()
            high, low_part = parts(c_in[child])
            rest = jnp.zeros((c_h.shape[0] - cross, c_h.shape[1]), jnp.bfloat16)
            c_h[:cross] = high
            c_l[:cross] = low_part
            c_h[cross:] = rest
            c_l[cross:] = rest
            f_buf[child, slots_of(1)] = factor(child, want[child, slots_of(1)])
            end_copy(child, 1, end).start()

    def serve_all(child):
        @pl.when(middle)
        def _():
            split_inverse(child)

            @pl.loop(0, n)
            def _(s):
                high, low_part = parts(up[child, s])
                up_h[s] = high
                up_l[s] = low_part

            @pl.when(server)
            def _():
                @pl.loop(0, chunks)
                def _(j):
                    f_buf[child, j] = factor(child, range_of(end * width + j * chunk))
                    end_copy(child, j, end).start()

    def serve_own(child):
        @pl.when(middle)
        def _():
            @pl.loop(0, chunks)
            def _(j):
                keep(child, j, factor(child, range_of(t * width + j * chunk)))

    def take_factor(child):
        @pl.when(at_end)
        def _():
            if packed:
                for q in range(2):
                    end_copy(child, q, aside).wait_recv()
                spread(f_buf[child], (g_h, g_l))

            @pl.loop(0, chunks)
            def _(j):
                if packed:
                    choose = one_hot(range_of(t * width + j * chunk) == row_want[child])
                    for ref, source in ((f_h, g_h), (f_l, g_l)):
                        ref[child, strip(j), :] = dot(choose, source[...]).astype(jnp.bfloat16)
                else:
                    end_copy(child, j, aside).wait_recv()
                    keep(child, j, f_buf[child, j])

    slots = x_buf.shape[0]
    ahead = slots // 2
    tall = x_buf.shape[1]
    per = order // tall
    blocks = per * chunks

    def window(ref, i):
        rows = pl.ds(pl.multiple_of(lax.rem(i, per) * tall, tall), tall)
        return ref.at[rows, strip(lax.div(i, per))]

    def subtract(child, begin, stop):
        source = base_in if child == 0 else x_out

        def load(i):
            slot = lax.rem(i, slots)
            return pltpu.make_async_copy(window(source, i), x_buf.at[slot], in_sem.at[slot])

        def store(i):
            slot = lax.rem(i, slots)
            return pltpu.make_async_copy(x_buf.at[slot], window(x_out, i), out_sem.at[slot])

        for i in range(begin, min(begin + ahead, stop)):
            load(i).start()
        if begin == 0:
            take_factor(child)

        @pl.loop(begin, stop)
        def _(i):
            j = lax.div(i, per)

            @pl.when(i + ahead < stop)
            def _():
                @pl.when(i >= begin + slots - ahead)
                def _():
                    store(i - (slots - ahead)).wait()

                load(i + ahead).start()

            rows = pl.ds(pl.multiple_of(lax.rem(i, per) * tall, tall), tall)
            high = f_h[child, strip(j), :]
            left = lx_h[child, rows, :]
            total = dot(left, high, (1, 1))
            total = total + dot(left, f_l[child, strip(j), :], (1, 1))
            total = total + dot(lx_l[child, rows, :], high, (1, 1))
            load(i).wait()
            slot = lax.rem(i, slots)
            x_buf[slot] = x_buf[slot] - total
            store(i).start()

        for i in range(max(stop - slots, begin), stop):
            store(i).wait()

    def hand_on(k):
        if k < 2:
            return pltpu.make_async_copy((f_h, f_l)[k].at[1], (last_h_out, last_l_out)[k], out_copy_sem.at[k])
        return pltpu.make_async_copy(low.at[1, late], late_out, out_copy_sem.at[k])

    late = jnp.where(lower, n - 1, 0) if packed else 0
    send_own(2, 0, low_in.at[0])
    for kind in (2, 1, 0):
        exchange(kind).start()
        local(kind).start()
    exchange(2).wait()

    @pl.when(middle if packed else t >= 0)
    def _():
        send_own(2, 1)

    local(2).wait()
    for kind in (1, 0):
        local(kind).wait()
        exchange(kind).wait()

    @pl.when(at_end)
    def _():
        for child in range(2):
            for kind in (1, 0):
                send_own(kind, child)
        if packed:
            send_own(2, 1)

    for child in range(2):
        map_ref[child] = index_ref[f if child == 0 else partner, child:child + 1, :]
    if packed:
        pl.loop(0, 2)(tables)

        @pl.when(middle)
        def _():
            outer(0, 1)
            inner(0, 1, middle)
            send_own(1, 0)
            near(0)
            inner(1, 1, middle)
            pack(0)
            send_own(1, 1)
            near(1)
            inner(0, 2, middle)

        @pl.when(at_end)
        def _():
            for child, d in ((0, 1), (1, 1), (0, 2), (1, 2)):
                inner(child, d, at_end)
            place_rows(1)
            inner(0, 3, at_end)

        place_rows(0)

        @pl.when(middle)
        def _():
            pack(1)
            far(0)
            serve_near(0)
            outer(1, 1)
            serve_far(0)
            serve_own(0)
            place_rows(1)
            far(1)
            serve_near(1)

        subtract(0, 0, blocks // 2)

        @pl.when(middle)
        def _():
            serve_far(1)
            serve_own(1)

        subtract(0, blocks // 2, blocks)
        inner(1, 2, middle)
        subtract(1, 0, blocks)
        for k in range(2):
            hand_on(k).start()
        inner(1, 3, at_end)
        hand_on(2).start()
        for k in range(3):
            hand_on(k).wait()
    else:
        relay_low(0, 1)
        relay_low(1, 1)

        @pl.when(middle)
        def _():
            send_own(1, 0)
            send_own(0, 0)

        relay_low(0, 2)
        near(0)

        @pl.when(middle)
        def _():
            send_own(1, 1)
            send_own(0, 1)

        relay_low(1, 2)

        @pl.loop(3, n)
        def _(d):
            relay_low(0, d)
            relay_low(1, d)

        near(1)
        place_rows(0)
        place_rows(1)
        for child in range(2):
            far(child)
            serve_all(child)
            serve_own(child)
            subtract(child, 0, blocks)
        for k in range(2):
            hand_on(k).start()
            hand_on(k).wait()

    for child in range(2):
        @pl.loop(0, n)
        def _(s):
            for side in range(2):
                for kind in range(3):
                    @pl.when(takes(kind, side) & (s <= t if side == 0 else s >= t))
                    def _():
                        hop(kind, child, s, side).wait_send()

        @pl.when(server)
        def _():
            if packed:
                for j in range(2):
                    end_copy(child, j, aside).wait_send()
            else:
                @pl.loop(0, chunks)
                def _(j):
                    end_copy(child, j, aside).wait_send()

        if packed:
            @pl.when(middle)
            def _():
                cross_copy(child).wait_send()

    if not packed:
        low[1, late] = jnp.zeros(late_out.shape, jnp.float32)
        hand_on(2).start()
        hand_on(2).wait()


def capacity(draws, share, order):
    spread_of = math.sqrt(draws * share * (1 - share) * (1 - draws / order))
    return -(-math.ceil(draws * share + 4.5 * spread_of) // 8) * 8


def padded(rows):
    return -(-rows // 128) * 128


def assembled(inverse, upper, lower, maps, base, n, limits):
    order, width = base.shape
    pivots = inverse.shape[2]
    count = maps.shape[2]
    kr, wc, lr = inverse.shape[1], upper.shape[2], lower.shape[1]
    vmem = pltpu.VMEM
    dma = pltpu.SemaphoreType.DMA
    f32, b16 = jnp.float32, jnp.bfloat16
    chunk = min(256, width)
    chunks = width // chunk
    slots = 4
    packed = limits is not None
    held, extra = n, []
    f_shape, f_sems = (2, chunks, chunk, pivots), (2, chunks)
    u_shape = (n, pivots, wc)
    if packed:
        total_cap, _, cross = limits
        cap_pad, cross_pad = padded(total_cap), padded(cross)
        held = n // 2
        f_shape, f_sems = (2, total_cap, pivots), (2, 2)
        u_shape = (2, held, pivots, wc)
        extra = [
            vmem((2, 8, count), jnp.int32),
            vmem((2, total_cap, 1), jnp.int32),
            vmem((2, 1, cap_pad), jnp.int32),
            vmem((2, 1, cross_pad), jnp.int32),
            vmem((2, cross, pivots), f32),
            vmem((2, cross, pivots), f32),
            vmem((cross_pad, pivots), b16),
            vmem((cross_pad, pivots), b16),
            vmem((cap_pad, pivots), b16),
            vmem((cap_pad, pivots), b16),
            dma((2,)), dma((2,)),
        ]
    whole = pl.BlockSpec(memory_space=pl.ANY)
    return pl.pallas_call(
        functools.partial(front_kernel, n, limits),
        out_shape=[jax.ShapeDtypeStruct((order, width), f32)]
        + [jax.ShapeDtypeStruct((width, pivots), b16)] * 2
        + [jax.ShapeDtypeStruct((lr, pivots), f32)],
        in_specs=[whole] * 3 + [pl.BlockSpec(memory_space=vmem), whole],
        out_specs=[whole] * 4,
        scratch_shapes=[
            vmem((2, 1, count), jnp.int32),
            vmem((2, held, pivots, wc), f32),
            vmem((2, n, kr, pivots), f32),
            vmem((2, n, lr, pivots), f32),
            vmem(u_shape, b16),
            vmem(u_shape, b16),
            vmem((n * kr, pivots), b16),
            vmem((n * kr, pivots), b16),
            vmem((count, pivots), b16),
            vmem((count, pivots), b16),
            vmem((2, order, pivots), b16),
            vmem((2, order, pivots), b16),
            vmem(f_shape, f32),
            vmem((2, width, pivots), b16),
            vmem((2, width, pivots), b16),
            vmem((slots, min(1024, order), chunk), f32),
            dma((3,)), dma((3,)), dma((3,)),
            dma((2, 2, n)), dma((2, n)),
            dma((2, 2, n)), dma((2, n)),
            dma((2, 2, n)), dma((2, n)),
            dma(f_sems), dma(f_sems),
            dma((slots,)), dma((slots,)), dma((3,)),
        ] + extra,
        compiler_params=pltpu.CompilerParams(
            collective_id=int(packed), has_side_effects=True, vmem_limit_bytes=63 * 1024 * 1024
        ),
    )(inverse, upper, lower, maps, base)


def finish_kernel(
    n, index_ref, x_in, last_h, last_l, late_in, out,
    x_buf, f_h, f_l, late, u_h, u_l, x_sem, out_sem, f_sem,
):
    t = lax.axis_index("tile")
    f = lax.axis_index("front")
    partner = lax.rem(f, 2) * -2 + 1 + f
    slots, rows, width = x_buf.shape
    lr = late.shape[0]
    blocks = out.shape[0] // rows
    ahead = slots // 2
    chunk = min(256, width)
    shard = jnp.where(t < n // 2, n - 1, 0)
    places = index_ref[partner, 1:2, pl.ds(pl.multiple_of(shard * lr, lr), lr)]

    def window(i):
        return pl.ds(pl.multiple_of(i * rows, rows), rows)

    def load(i):
        slot = lax.rem(i, slots)
        return pltpu.make_async_copy(x_in.at[window(i)], x_buf.at[slot], x_sem.at[slot])

    def store(i):
        slot = lax.rem(i, slots)
        return pltpu.make_async_copy(x_buf.at[slot], out.at[window(i)], out_sem.at[slot])

    first = [
        pltpu.make_async_copy(source, target, f_sem.at[k])
        for k, (source, target) in enumerate(((late_in, late), (last_h, f_h), (last_l, f_l)))
    ]
    for copy in first:
        copy.start()
    for copy in first:
        copy.wait()
    for i in range(min(ahead, blocks)):
        load(i).start()
    left = parts(late[...])
    for j in range(width // chunk):
        columns = slice(j * chunk, (j + 1) * chunk)
        total = dot(left[0], f_h[columns, :], (1, 1))
        total = total + dot(left[0], f_l[columns, :], (1, 1))
        total = total + dot(left[1], f_h[columns, :], (1, 1))
        u_h[:, columns], u_l[:, columns] = parts(total)

    @pl.loop(0, blocks)
    def _(i):
        @pl.when(i + ahead < blocks)
        def _():
            @pl.when(i >= slots - ahead)
            def _():
                store(i - (slots - ahead)).wait()

            load(i + ahead).start()

        choose = one_hot(lax.broadcasted_iota(jnp.int32, (rows, lr), 0) + i * rows == places)
        load(i).wait()
        slot = lax.rem(i, slots)
        for j in range(width // chunk):
            columns = slice(j * chunk, (j + 1) * chunk)
            total = dot(choose, u_h[:, columns]) + dot(choose, u_l[:, columns])
            x_buf[slot, :, columns] = x_buf[slot, :, columns] - total
        store(i).start()

    for i in range(max(blocks - slots, 0), blocks):
        store(i).wait()


def finished(n, index_map, x, f_h, f_l, late):
    order, width = x.shape
    rows, slots = min(512, order), 4
    vmem, dma, b16 = pltpu.VMEM, pltpu.SemaphoreType.DMA, jnp.bfloat16
    whole = pl.BlockSpec(memory_space=pl.ANY)
    return pl.pallas_call(
        functools.partial(finish_kernel, n),
        out_shape=jax.ShapeDtypeStruct(x.shape, x.dtype),
        in_specs=[pl.BlockSpec(memory_space=vmem)] + [whole] * 4,
        out_specs=whole,
        scratch_shapes=[
            vmem((slots, rows, width), x.dtype),
            vmem(f_h.shape, b16),
            vmem(f_h.shape, b16),
            vmem(late.shape, late.dtype),
            vmem((late.shape[0], width), b16),
            vmem((late.shape[0], width), b16),
            dma((slots,)), dma((slots,)), dma((3,)),
        ],
        compiler_params=pltpu.CompilerParams(vmem_limit_bytes=60 * 1024 * 1024),
    )(index_map, x, f_h, f_l, late)


def fits_kernel(ranges, index_ref, out_ref):
    index = index_ref[...]
    early = lax.broadcasted_iota(jnp.int32, index.shape, 2) < index.shape[2] // 2
    over = None
    for start, stop, is_early, limit in ranges:
        inside = (index >= start) & (index < stop)
        if is_early is not None:
            inside &= early if is_early else ~early
        extra = jnp.sum(inside.astype(jnp.int32), axis=2, keepdims=True) - limit
        over = extra if over is None else jnp.maximum(over, extra)
    out_ref[0] = (jnp.max(over) <= 0).astype(jnp.int32)


def shards(pivot_inverse, panel_upper, panel_lower, index_map, parent_base):
    n = lax.axis_size("tile")
    order, width = parent_base.shape[1:]
    count = index_map.shape[2]
    operands = (pivot_inverse[0], panel_upper[0], panel_lower[0], index_map, parent_base[0])

    side = order // 2
    total = capacity(count, width / order, order)
    far = capacity(count // 2, width / order, order)
    cross = capacity(count // 2, 1 / 2, order)

    def run(limits, *args):
        return tuple(assembled(*args, n, limits))

    if n != 4 or total >= width or cross >= count // 2:
        return finished(n, index_map, *run(None, *operands))[None]

    ranges = (
        (side, order, True, cross), (0, side, False, cross),
        (0, width, None, total), (0, width, False, far),
        (order - width, order, None, total), (order - width, order, True, far),
    )
    fits = pl.pallas_call(
        functools.partial(fits_kernel, ranges),
        out_shape=jax.ShapeDtypeStruct((1,), jnp.int32),
        in_specs=[pl.BlockSpec(memory_space=pltpu.VMEM)],
        out_specs=pl.BlockSpec(memory_space=pltpu.SMEM),
    )(index_map)
    return finished(n, index_map, *lax.cond(
        fits[0] > 0, functools.partial(run, (total, far, cross)), functools.partial(run, None), *operands
    ))[None]


def solution(mesh):
    return jax.shard_map(
        shards,
        mesh=mesh,
        in_specs=(
            P("front", None, "tile", None),
            P("front", None, None, "tile"),
            P("front", None, "tile", None),
            P(),
            P("front", None, "tile"),
        ),
        out_specs=P("front", None, "tile"),
        check_vma=False,
    )
```

```python
import functools
import math

import jax
import jax.numpy as jnp
from jax import lax
from jax.experimental import pallas as pl
from jax.experimental.pallas import tpu as pltpu
from jax.sharding import PartitionSpec as P

MESH = pl.DeviceIdType.MESH


def parts(value):
    high = value.astype(jnp.bfloat16)
    return high, (value - high.astype(jnp.float32)).astype(jnp.bfloat16)


def spread(value, targets):
    rows = value.shape[0]
    for ref, part in zip(targets, parts(value)):
        ref[:rows] = part
        if rows < ref.shape[0]:
            ref[rows:] = jnp.zeros((ref.shape[0] - rows, ref.shape[1]), jnp.bfloat16)


def dot(left, right, contract=(1, 0)):
    dims = (((contract[0],), (contract[1],)), ((), ()))
    return lax.dot_general(left, right, dims, preferred_element_type=jnp.float32)


def one_hot(match):
    return match.astype(jnp.float32).astype(jnp.bfloat16)


def counts_fit(index_ref, order, width, limits):
    total_cap, far_cap, cross = limits
    half = index_ref.shape[2] // 2

    def number(early, test):
        part = index_ref[:, :, :half] if early else index_ref[:, :, half:]
        return jnp.sum(test(part).astype(jnp.int32), axis=2, keepdims=True)

    def first(m):
        return m < width

    def last(m):
        return m >= order - width

    over = number(True, lambda m: m >= order // 2) - cross
    over = jnp.maximum(over, number(False, lambda m: m < order // 2) - cross)
    for test, far_early in ((first, False), (last, True)):
        far = number(far_early, test)
        over = jnp.maximum(over, far - far_cap)
        over = jnp.maximum(over, far + number(not far_early, test) - total_cap)
    return (jnp.max(over) <= 0).astype(jnp.int32)


def front_kernel(
    n, limits, inv_in, up_in, low_in, index_ref, base_in,
    x_out, u_h_out, u_l_out, fits_out,
    map_ref, up, inv, low, up_h, up_l, inv_h, inv_l, low_h, low_l, lx_h, lx_l, f_buf, f_h, f_l, u_h, u_l, x_buf,
    local_sem, part_send, part_recv, up_send, up_recv, inv_send, inv_recv,
    low_send, low_recv, f_send, f_recv, in_sem, out_sem, out_copy_sem, *packing,
):
    packed = limits is not None
    if packed:
        ranks, want, row_want, row_in, c_out, c_in, c_h, c_l, g_h, g_l, c_send, c_recv, late_send, late_recv = packing
        total_cap, far_cap, cross = limits
        split = total_cap - far_cap
    t = lax.axis_index("tile")
    f = lax.axis_index("front")
    partner = lax.rem(f, 2) * -2 + 1 + f
    count = map_ref.shape[2]
    wc = up.shape[3]
    kr = inv.shape[2]
    lr = low.shape[2]
    order, width = x_out.shape
    chunk = min(256, width)
    chunks = width // chunk
    middle = (t >= 1) & (t <= n - 2)
    at_end = (t == 0) | (t == n - 1)
    lower = t < n // 2
    server = (t == 1) | (t == n - 2)
    end = lax.div(t - 1, n - 3) * (n - 1)
    aside = lax.rem(t + 1, n)
    first = jnp.where(lower, 0, n // 2) if packed else 0

    barrier = pltpu.get_barrier_semaphore()
    pl.semaphore_signal(barrier, inc=1, device_id=(partner, t), device_id_type=MESH)

    @pl.when(t > 0)
    def _():
        pl.semaphore_signal(barrier, inc=1, device_id=(f, t - 1), device_id_type=MESH)

    @pl.when(t < n - 1)
    def _():
        pl.semaphore_signal(barrier, inc=1, device_id=(f, t + 1), device_id_type=MESH)

    @pl.when(at_end)
    def _():
        pl.semaphore_wait(barrier, 2)

    @pl.when(middle)
    def _():
        pl.semaphore_wait(barrier, 3)

    sources = (up_in, inv_in, low_in)
    targets = (up, inv, low)

    def place(kind, child, shard):
        return targets[kind].at[child, shard - first if kind == 0 else shard]

    def local(kind):
        return pltpu.make_async_copy(sources[kind].at[0], place(kind, 0, t), local_sem.at[kind])

    def exchange(kind):
        return pltpu.make_async_remote_copy(
            src_ref=sources[kind].at[1], dst_ref=place(kind, 1, t),
            send_sem=part_send.at[kind], recv_sem=part_recv.at[kind],
            device_id=(partner, t), device_id_type=MESH,
        )

    def hop(kind, child, shard, side, source=None):
        send, recv = ((up_send, up_recv), (inv_send, inv_recv), (low_send, low_recv))[kind]
        ref = place(kind, child, shard)
        return pltpu.make_async_remote_copy(
            src_ref=ref if source is None else source, dst_ref=ref,
            send_sem=send.at[side, child, shard], recv_sem=recv.at[child, shard],
            device_id=(f, lax.rem(t + (1 if side == 0 else n - 1), n)), device_id_type=MESH,
        )

    def takes(kind, side):
        if kind == 2:
            return t + 1 <= n - 1 if side == 0 else t - 1 >= 0
        if kind == 0 and packed:
            return t == 0 if side == 0 else t == n - 1
        return t + 1 <= n - 2 if side == 0 else t - 1 >= 1

    def send(kind, child, shard, side, source=None):
        @pl.when(takes(kind, side))
        def _():
            hop(kind, child, shard, side, source).start()

    def send_own(kind, child, source=None):
        send(kind, child, t, 0, source)
        send(kind, child, t, 1, source)

    def pass_on(kinds, child, d, side, where):
        shard = t - d if side == 0 else t + d
        inside = shard >= 0 if side == 0 else shard <= n - 1

        @pl.when(inside & where)
        def _():
            for kind in kinds:
                hop(kind, child, shard, side).wait_recv()
                send(kind, child, shard, side)

    def relay_low(child, d):
        pass_on((2,), child, d, 0, t >= 0)
        pass_on((2,), child, d, 1, t >= 0)

    def inner(child, d, where):
        pass_on((2,), child, d, 1, where & lower)
        pass_on((2,), child, d, 0, where & (t >= n // 2))

    def outer(child, d):
        pass_on((2,), child, d, 0, middle & lower)
        pass_on((2,), child, d, 1, middle & (t >= n // 2))

    kinds = (1,) if packed else (1, 0)

    def near(child):
        @pl.loop(1, n)
        def _(d):
            pass_on(kinds, child, d, 0, middle & lower)
            pass_on(kinds, child, d, 1, middle & (t >= n // 2))

    def far(child):
        @pl.loop(1, n)
        def _(d):
            pass_on(kinds, child, d, 1, middle & lower)
            pass_on(kinds, child, d, 0, middle & (t >= n // 2))

    def listed(child, shard):
        return map_ref[child, :, pl.ds(pl.multiple_of(shard * wc, wc), wc)]

    def tables(child):
        row = lax.broadcasted_iota(jnp.int32, (8, 1), 0)
        side = order // 2
        tile = jnp.where(middle, end, t) * width
        ours = jnp.where(lower, 0, side)
        starts = (tile, tile, side - ours, ours)
        spans = (width, width, side, side)
        low_end = high_end = jnp.zeros((8, 1), jnp.int32)
        for q in range(4):
            low_end = jnp.where(row == q, starts[q], low_end)
            high_end = jnp.where(row == q, starts[q] + spans[q], high_end)
        before = lax.broadcasted_iota(jnp.int32, (wc, wc), 0) < lax.broadcasted_iota(jnp.int32, (wc, wc), 1)
        before = one_hot(before)
        passed = jnp.zeros((8, 1), jnp.float32)
        which = lax.broadcasted_iota(jnp.int32, (8, wc), 0)
        wants = jnp.zeros((total_cap, 8), jnp.float32)
        both = jnp.zeros((8, row_want.shape[2]), jnp.float32)
        inward = jnp.zeros((8, row_in.shape[2]), jnp.float32)
        for s in range(n):
            columns = map_ref[child, :, s * wc:(s + 1) * wc]
            is_ours = (first <= s) & (s < first + n // 2)
            fits = jnp.where(lax.rem(row, 2) == 0, is_ours.astype(jnp.int32), 1 - is_ours.astype(jnp.int32)) > 0
            inside = (columns >= low_end) & (columns < high_end) & fits
            mark = one_hot(inside)
            rank = jnp.where(inside, (dot(mark, before) + passed).astype(jnp.int32), -2 * count)
            passed = passed + jnp.sum(mark.astype(jnp.float32), axis=1, keepdims=True)
            ranks[child, :, s * wc:(s + 1) * wc] = rank
            digits = jnp.where(which == 0, columns >> 7, jnp.where(which == 1, columns & 127, 1))
            digits = digits.astype(jnp.float32).astype(jnp.bfloat16)

            def pick(q, size):
                slot = lax.broadcasted_iota(jnp.int32, (size, wc), 0)
                return one_hot((total_cap - 1 - slot if q == 1 else slot) == rank[q:q + 1])

            for q in range(2):
                wants = wants + dot(pick(q, total_cap), digits, (1, 1))
                both = both + dot(digits, pick(q, both.shape[1]), (1, 1))
            inward = inward + dot(digits, pick(3, inward.shape[1]), (1, 1))

        def across(found):
            value = found[0:1].astype(jnp.int32) * 128 + found[1:2].astype(jnp.int32)
            return jnp.where(found[2:3] > 0, value, -1)

        found = wants.astype(jnp.int32)
        want[child] = jnp.where(found[:, 2:3] > 0, found[:, 0:1] * 128 + found[:, 1:2], -1)
        row_want[child] = across(both)
        row_in[child] = across(inward)

    def cross_copy(child):
        return pltpu.make_async_remote_copy(
            src_ref=c_out.at[child], dst_ref=c_in.at[child],
            send_sem=c_send.at[child], recv_sem=c_recv.at[child],
            device_id=(f, n - 1 - t), device_id_type=MESH,
        )

    def pack(child):
        @pl.when(middle)
        def _():
            @pl.when(lower)
            def _():
                hop(0, child, 0, 0).wait_recv()

            @pl.when(t >= n // 2)
            def _():
                hop(0, child, n - 1, 1).wait_recv()

            for k in range(n // 2):
                high, low_part = parts(up[child, k])
                up_h[child, k] = high
                up_l[child, k] = low_part
            step = cross // 4 if cross % 32 == 0 else cross

            @pl.loop(0, cross // step)
            def _(j):
                base = pl.multiple_of(j * step, 8)
                total = None
                for k in range(n // 2):
                    shard = pl.ds(pl.multiple_of((first + k) * wc, wc), wc)
                    rank = ranks[child, 2:3, shard] - base
                    choose = one_hot(lax.broadcasted_iota(jnp.int32, (step, wc), 0) == rank)
                    piece = dot(choose, up_h[child, k], (1, 1)) + dot(choose, up_l[child, k], (1, 1))
                    total = piece if total is None else total + piece
                c_out[child, pl.ds(base, step), :] = total

            cross_copy(child).start()

    def place_rows(child):
        held = (n - 1 if packed and child == 1 else n) * lr
        from_shard = jnp.where(lower, 0, 1) if packed and child == 1 else 0
        used = pl.ds(pl.multiple_of(from_shard * lr, lr), held)

        @pl.loop(from_shard, from_shard + held // lr)
        def _(s):
            rows = pl.ds(pl.multiple_of(s * lr, lr), lr)
            high, low_part = parts(low[child, s])
            low_h[rows, :] = high
            low_l[rows, :] = low_part

        span = min(512, order)

        @pl.loop(0, order // span)
        def _(j):
            base = pl.multiple_of(j * span, span)
            rows = lax.broadcasted_iota(jnp.int32, (span, held), 0) + base
            choose = one_hot(rows == map_ref[child, :, used])
            lx_h[child, pl.ds(base, span), :] = dot(choose, low_h[used, :]).astype(jnp.bfloat16)
            lx_l[child, pl.ds(base, span), :] = dot(choose, low_l[used, :]).astype(jnp.bfloat16)

    def split_inverse(child):
        @pl.loop(0, n)
        def _(s):
            rows = pl.ds(pl.multiple_of(s * kr, kr), kr)
            high, low_part = parts(inv[child, s])
            inv_h[rows, :] = high
            inv_l[rows, :] = low_part

    def factor(child, columns, near_side=True, far_side=True):
        terms = []
        if near_side:
            for s in range(n // 2 if packed else n):
                choose = one_hot(columns == listed(child, first + s))
                index = (child, s) if packed else s
                terms.append((dot(choose, up_h[index], (1, 1)), dot(choose, up_l[index], (1, 1))))
        if packed and far_side:
            choose = one_hot(columns == row_in[child])
            terms.append((dot(choose, c_h[...]), dot(choose, c_l[...])))
        high, low_part = terms[0]
        for a, b in terms[1:]:
            high = high + a
            low_part = low_part + b
        high = high.astype(jnp.bfloat16)
        low_part = low_part.astype(jnp.bfloat16)
        total = dot(high, inv_h[...], (1, 1))
        total = total + dot(low_part, inv_h[...], (1, 1))
        return total + dot(high, inv_l[...], (1, 1))

    def strip(j):
        return pl.ds(pl.multiple_of(j * chunk, chunk), chunk)

    def range_of(start):
        return lax.broadcasted_iota(jnp.int32, (chunk, 1), 0) + start

    def slots_of(j):
        return slice(0, split) if j == 0 else slice(split, total_cap)

    def end_copy(child, j, target):
        if packed:
            ref = f_buf.at[child, slots_of(j)]
        else:
            ref = f_buf.at[child, j]
        return pltpu.make_async_remote_copy(
            src_ref=ref, dst_ref=ref,
            send_sem=f_send.at[child, j], recv_sem=f_recv.at[child, j],
            device_id=(f, target), device_id_type=MESH,
        )

    def keep(child, j, value):
        for ref, part in zip((f_h, f_l), parts(value)):
            ref[child, strip(j), :] = part

    def serve_near(child):
        @pl.when(middle)
        def _():
            split_inverse(child)
            f_buf[child, slots_of(0)] = factor(child, want[child, slots_of(0)], far_side=False)
            end_copy(child, 0, end).start()

    def serve_far(child):
        @pl.when(middle)
        def _():
            cross_copy(child).wait_recv()
            high, low_part = parts(c_in[child])
            rest = jnp.zeros((c_h.shape[0] - cross, c_h.shape[1]), jnp.bfloat16)
            c_h[:cross] = high
            c_l[:cross] = low_part
            c_h[cross:] = rest
            c_l[cross:] = rest
            f_buf[child, slots_of(1)] = factor(child, want[child, slots_of(1)])
            end_copy(child, 1, end).start()

    def serve_all(child):
        @pl.when(middle)
        def _():
            split_inverse(child)

            @pl.loop(0, n)
            def _(s):
                high, low_part = parts(up[child, s])
                up_h[s] = high
                up_l[s] = low_part

            @pl.when(server)
            def _():
                @pl.loop(0, chunks)
                def _(j):
                    f_buf[child, j] = factor(child, range_of(end * width + j * chunk))
                    end_copy(child, j, end).start()

    def serve_own(child):
        @pl.when(middle)
        def _():
            @pl.loop(0, chunks)
            def _(j):
                keep(child, j, factor(child, range_of(t * width + j * chunk)))

    def take_factor(child):
        @pl.when(at_end)
        def _():
            if packed:
                for q in range(2):
                    end_copy(child, q, aside).wait_recv()
                spread(f_buf[child], (g_h, g_l))

            @pl.loop(0, chunks)
            def _(j):
                if packed:
                    choose = one_hot(range_of(t * width + j * chunk) == row_want[child])
                    for ref, source in ((f_h, g_h), (f_l, g_l)):
                        ref[child, strip(j), :] = dot(choose, source[...]).astype(jnp.bfloat16)
                else:
                    end_copy(child, j, aside).wait_recv()
                    keep(child, j, f_buf[child, j])

    slots = x_buf.shape[0]
    ahead = slots // 2
    tall = x_buf.shape[1]
    per = order // tall
    blocks = per * chunks

    def window(ref, i):
        rows = pl.ds(pl.multiple_of(lax.rem(i, per) * tall, tall), tall)
        return ref.at[rows, strip(lax.div(i, per))]

    def subtract(child, begin, stop):
        source = base_in if child == 0 else x_out

        def load(i):
            slot = lax.rem(i, slots)
            return pltpu.make_async_copy(window(source, i), x_buf.at[slot], in_sem.at[slot])

        def store(i):
            slot = lax.rem(i, slots)
            return pltpu.make_async_copy(x_buf.at[slot], window(x_out, i), out_sem.at[slot])

        for i in range(begin, min(begin + ahead, stop)):
            load(i).start()
        if begin == 0:
            take_factor(child)

        @pl.loop(begin, stop)
        def _(i):
            j = lax.div(i, per)

            @pl.when(i + ahead < stop)
            def _():
                @pl.when(i >= begin + slots - ahead)
                def _():
                    store(i - (slots - ahead)).wait()

                load(i + ahead).start()

            rows = pl.ds(pl.multiple_of(lax.rem(i, per) * tall, tall), tall)
            high = f_h[child, strip(j), :]
            left = lx_h[child, rows, :]
            total = dot(left, high, (1, 1))
            total = total + dot(left, f_l[child, strip(j), :], (1, 1))
            total = total + dot(lx_l[child, rows, :], high, (1, 1))
            load(i).wait()
            slot = lax.rem(i, slots)
            x_buf[slot] = x_buf[slot] - total
            store(i).start()

        for i in range(max(stop - slots, begin), stop):
            store(i).wait()

    def hand_on(k):
        return pltpu.make_async_copy((u_h, u_l)[k], (u_h_out, u_l_out)[k], out_copy_sem.at[k])

    late = jnp.where(lower, n - 1, 0)

    def late_rows(k):
        return slice(k * (lr // 2), (k + 1) * (lr // 2))

    def late_copy(k, target):
        ref = low.at[1, late, late_rows(k)]
        return pltpu.make_async_remote_copy(
            src_ref=ref, dst_ref=ref, send_sem=late_send.at[k], recv_sem=late_recv.at[k],
            device_id=(f, target), device_id_type=MESH,
        )

    def take_late():
        @pl.when(middle)
        def _():
            @pl.when(lower)
            def _():
                hop(2, 1, n - 1, 1).wait_recv()

            @pl.when(t >= n // 2)
            def _():
                hop(2, 1, 0, 0).wait_recv()

            for k in range(2):
                late_copy(k, end).start()

    def last_update():
        @pl.loop(0, 2)
        def _(k):
            @pl.when(at_end)
            def _():
                for q in range(2):
                    @pl.when(k == q)
                    def _():
                        late_copy(q, aside).wait_recv()

            rows = pl.ds(pl.multiple_of(k * (lr // 2), lr // 2), lr // 2)
            left = parts(low[1, late, rows, :])
            for j in range(chunks):
                columns = slice(j * chunk, (j + 1) * chunk)
                total = dot(left[0], f_h[1, columns, :], (1, 1))
                total = total + dot(left[0], f_l[1, columns, :], (1, 1))
                total = total + dot(left[1], f_h[1, columns, :], (1, 1))
                u_h[rows, columns], u_l[rows, columns] = parts(total)
    send_own(2, 0, low_in.at[0])
    for kind in (2, 1, 0):
        exchange(kind).start()
        local(kind).start()
    exchange(2).wait()

    @pl.when(middle if packed else t >= 0)
    def _():
        send_own(2, 1)

    local(2).wait()
    for kind in (1, 0):
        local(kind).wait()
        exchange(kind).wait()

    @pl.when(at_end)
    def _():
        for child in range(2):
            for kind in (1, 0):
                send_own(kind, child)
        if packed:
            send_own(2, 1)

    for child in range(2):
        map_ref[child] = index_ref[f if child == 0 else partner, child:child + 1, :]
    if packed:
        pl.loop(0, 2)(tables)
        fits_out[0] = counts_fit(index_ref, order, width, limits)

        @pl.when(middle)
        def _():
            outer(0, 1)
            inner(0, 1, middle)
            send_own(1, 0)
            near(0)
            inner(1, 1, middle)
            pack(0)
            send_own(1, 1)
            near(1)
            inner(0, 2, middle)

        @pl.when(at_end)
        def _():
            for child, d in ((0, 1), (1, 1), (0, 2), (1, 2)):
                inner(child, d, at_end)
            place_rows(1)
            inner(0, 3, at_end)

        place_rows(0)

        @pl.when(middle)
        def _():
            pack(1)
            far(0)
            serve_near(0)
            outer(1, 1)
            serve_far(0)
            serve_own(0)
            place_rows(1)
            far(1)
            serve_near(1)

        subtract(0, 0, blocks // 2)

        @pl.when(middle)
        def _():
            serve_far(1)
            serve_own(1)

        subtract(0, blocks // 2, blocks)
        take_late()
        subtract(1, 0, blocks)
        last_update()
        for k in range(2):
            hand_on(k).start()
        for k in range(2):
            hand_on(k).wait()
    else:
        relay_low(0, 1)
        relay_low(1, 1)

        @pl.when(middle)
        def _():
            send_own(1, 0)
            send_own(0, 0)

        relay_low(0, 2)
        near(0)

        @pl.when(middle)
        def _():
            send_own(1, 1)
            send_own(0, 1)

        relay_low(1, 2)

        @pl.loop(3, n)
        def _(d):
            relay_low(0, d)
            relay_low(1, d)

        near(1)
        place_rows(0)
        place_rows(1)
        for child in range(2):
            far(child)
            serve_all(child)
            serve_own(child)
            subtract(child, 0, blocks)
        for k, ref in enumerate((u_h, u_l)):
            ref[...] = jnp.zeros_like(ref)
            hand_on(k).start()
            hand_on(k).wait()
        fits_out[0] = 1

    for child in range(2):
        @pl.loop(0, n)
        def _(s):
            for side in range(2):
                for kind in range(3):
                    whole = ~(middle & (s == late)) if packed and (kind, child) == (2, 1) else t >= 0

                    @pl.when(takes(kind, side) & (s <= t if side == 0 else s >= t) & whole)
                    def _():
                        hop(kind, child, s, side).wait_send()

        @pl.when(server)
        def _():
            if packed:
                for j in range(2):
                    end_copy(child, j, aside).wait_send()
            else:
                @pl.loop(0, chunks)
                def _(j):
                    end_copy(child, j, aside).wait_send()

        if packed:
            @pl.when(middle)
            def _():
                cross_copy(child).wait_send()

            @pl.when(server)
            def _():
                if child == 1:
                    for k in range(2):
                        late_copy(k, aside).wait_send()


def capacity(draws, share, order):
    spread_of = math.sqrt(draws * share * (1 - share) * (1 - draws / order))
    return -(-math.ceil(draws * share + 4.5 * spread_of) // 8) * 8


def padded(rows):
    return -(-rows // 128) * 128


def assembled(inverse, upper, lower, maps, base, n, limits):
    order, width = base.shape
    pivots = inverse.shape[2]
    count = maps.shape[2]
    kr, wc, lr = inverse.shape[1], upper.shape[2], lower.shape[1]
    vmem = pltpu.VMEM
    dma = pltpu.SemaphoreType.DMA
    f32, b16 = jnp.float32, jnp.bfloat16
    chunk = min(256, width)
    chunks = width // chunk
    slots = 4
    packed = limits is not None
    held, extra = n, []
    f_shape, f_sems = (2, chunks, chunk, pivots), (2, chunks)
    u_shape = (n, pivots, wc)
    if packed:
        total_cap, _, cross = limits
        cap_pad, cross_pad = padded(total_cap), padded(cross)
        held = n // 2
        f_shape, f_sems = (2, total_cap, pivots), (2, 2)
        u_shape = (2, held, pivots, wc)
        extra = [
            vmem((2, 8, count), jnp.int32),
            vmem((2, total_cap, 1), jnp.int32),
            vmem((2, 1, cap_pad), jnp.int32),
            vmem((2, 1, cross_pad), jnp.int32),
            vmem((2, cross, pivots), f32),
            vmem((2, cross, pivots), f32),
            vmem((cross_pad, pivots), b16),
            vmem((cross_pad, pivots), b16),
            vmem((cap_pad, pivots), b16),
            vmem((cap_pad, pivots), b16),
            dma((2,)), dma((2,)), dma((2,)), dma((2,)),
        ]
    whole = pl.BlockSpec(memory_space=pl.ANY)
    return pl.pallas_call(
        functools.partial(front_kernel, n, limits),
        out_shape=[jax.ShapeDtypeStruct((order, width), f32)]
        + [jax.ShapeDtypeStruct((lr, width), b16)] * 2
        + [jax.ShapeDtypeStruct((1,), jnp.int32)],
        in_specs=[whole] * 3 + [pl.BlockSpec(memory_space=vmem), whole],
        out_specs=[whole] * 3 + [pl.BlockSpec(memory_space=pltpu.SMEM)],
        scratch_shapes=[
            vmem((2, 1, count), jnp.int32),
            vmem((2, held, pivots, wc), f32),
            vmem((2, n, kr, pivots), f32),
            vmem((2, n, lr, pivots), f32),
            vmem(u_shape, b16),
            vmem(u_shape, b16),
            vmem((n * kr, pivots), b16),
            vmem((n * kr, pivots), b16),
            vmem((count, pivots), b16),
            vmem((count, pivots), b16),
            vmem((2, order, pivots), b16),
            vmem((2, order, pivots), b16),
            vmem(f_shape, f32),
            vmem((2, width, pivots), b16),
            vmem((2, width, pivots), b16),
            vmem((lr, width), b16),
            vmem((lr, width), b16),
            vmem((slots, min(1024, order), chunk), f32),
            dma((3,)), dma((3,)), dma((3,)),
            dma((2, 2, n)), dma((2, n)),
            dma((2, 2, n)), dma((2, n)),
            dma((2, 2, n)), dma((2, n)),
            dma(f_sems), dma(f_sems),
            dma((slots,)), dma((slots,)), dma((2,)),
        ] + extra,
        compiler_params=pltpu.CompilerParams(
            collective_id=int(packed), has_side_effects=True, vmem_limit_bytes=63 * 1024 * 1024
        ),
    )(inverse, upper, lower, maps, base)


def finish_kernel(
    n, index_ref, x_in, u_h_in, u_l_in, out,
    x_buf, u_h, u_l, x_sem, out_sem, u_sem,
):
    t = lax.axis_index("tile")
    f = lax.axis_index("front")
    partner = lax.rem(f, 2) * -2 + 1 + f
    slots, rows, width = x_buf.shape
    lr = u_h.shape[0]
    blocks = out.shape[0] // rows
    ahead = slots // 2
    chunk = min(256, width)
    shard = jnp.where(t < n // 2, n - 1, 0)
    places = index_ref[partner, 1:2, pl.ds(pl.multiple_of(shard * lr, lr), lr)]

    def window(i):
        return pl.ds(pl.multiple_of(i * rows, rows), rows)

    def load(i):
        slot = lax.rem(i, slots)
        return pltpu.make_async_copy(x_in.at[window(i)], x_buf.at[slot], x_sem.at[slot])

    def store(i):
        slot = lax.rem(i, slots)
        return pltpu.make_async_copy(x_buf.at[slot], out.at[window(i)], out_sem.at[slot])

    first = [
        pltpu.make_async_copy(source, target, u_sem.at[k])
        for k, (source, target) in enumerate(((u_h_in, u_h), (u_l_in, u_l)))
    ]
    for copy in first:
        copy.start()
    for i in range(min(ahead, blocks)):
        load(i).start()
    for copy in first:
        copy.wait()

    @pl.loop(0, blocks)
    def _(i):
        @pl.when(i + ahead < blocks)
        def _():
            @pl.when(i >= slots - ahead)
            def _():
                store(i - (slots - ahead)).wait()

            load(i + ahead).start()

        choose = one_hot(lax.broadcasted_iota(jnp.int32, (rows, lr), 0) + i * rows == places)
        load(i).wait()
        slot = lax.rem(i, slots)
        for j in range(width // chunk):
            columns = slice(j * chunk, (j + 1) * chunk)
            total = dot(choose, u_h[:, columns]) + dot(choose, u_l[:, columns])
            x_buf[slot, :, columns] = x_buf[slot, :, columns] - total
        store(i).start()

    for i in range(max(blocks - slots, 0), blocks):
        store(i).wait()


def finished(n, index_map, x, u_h, u_l):
    order, width = x.shape
    rows, slots = min(512, order), 6
    vmem, dma, b16 = pltpu.VMEM, pltpu.SemaphoreType.DMA, jnp.bfloat16
    whole = pl.BlockSpec(memory_space=pl.ANY)
    return pl.pallas_call(
        functools.partial(finish_kernel, n),
        out_shape=jax.ShapeDtypeStruct(x.shape, x.dtype),
        in_specs=[pl.BlockSpec(memory_space=vmem)] + [whole] * 3,
        out_specs=whole,
        scratch_shapes=[
            vmem((slots, rows, width), x.dtype),
            vmem(u_h.shape, b16),
            vmem(u_h.shape, b16),
            dma((slots,)), dma((slots,)), dma((2,)),
        ],
        compiler_params=pltpu.CompilerParams(vmem_limit_bytes=60 * 1024 * 1024),
    )(index_map, x, u_h, u_l)


def shards(pivot_inverse, panel_upper, panel_lower, index_map, parent_base):
    n = lax.axis_size("tile")
    order, width = parent_base.shape[1:]
    count = index_map.shape[2]
    operands = (pivot_inverse[0], panel_upper[0], panel_lower[0], index_map, parent_base[0])

    side = order // 2
    total = capacity(count, width / order, order)
    far = capacity(count // 2, width / order, order)
    cross = capacity(count // 2, 1 / 2, order)

    def run(limits, *args):
        return tuple(assembled(*args, n, limits))

    def whole_transfers():
        return finished(n, index_map, *run(None, *operands)[:3])

    if n != 4 or total >= width or cross >= count // 2:
        return whole_transfers()[None]

    x, u_h, u_l, fits = run((total, far, cross), *operands)
    return lax.cond(fits[0] > 0, lambda: finished(n, index_map, x, u_h, u_l), whole_transfers)[None]


def solution(mesh):
    return jax.shard_map(
        shards,
        mesh=mesh,
        in_specs=(
            P("front", None, "tile", None),
            P("front", None, None, "tile"),
            P("front", None, "tile", None),
            P(),
            P("front", None, "tile"),
        ),
        out_specs=P("front", None, "tile"),
        check_vma=False,
    )
```

```python
import functools
import math

import jax
import jax.numpy as jnp
from jax import lax
from jax.experimental import pallas as pl
from jax.experimental.pallas import tpu as pltpu
from jax.sharding import PartitionSpec as P

MESH = pl.DeviceIdType.MESH


def parts(value):
    high = value.astype(jnp.bfloat16)
    return high, (value - high.astype(jnp.float32)).astype(jnp.bfloat16)


def dot(left, right, contract=(1, 0)):
    dims = (((contract[0],), (contract[1],)), ((), ()))
    return lax.dot_general(left, right, dims, preferred_element_type=jnp.float32)


def one_hot(match):
    return match.astype(jnp.float32).astype(jnp.bfloat16)


def counts_fit(index_ref, order, width, limits):
    total_cap, far_cap, cross = limits
    half = index_ref.shape[2] // 2

    def number(early, test):
        part = index_ref[:, :, :half] if early else index_ref[:, :, half:]
        return jnp.sum(test(part).astype(jnp.int32), axis=2, keepdims=True)

    def first(m):
        return m < width

    def last(m):
        return m >= order - width

    over = number(True, lambda m: m >= order // 2) - cross
    over = jnp.maximum(over, number(False, lambda m: m < order // 2) - cross)
    for test, far_early in ((first, False), (last, True)):
        far = number(far_early, test)
        over = jnp.maximum(over, far - far_cap)
        over = jnp.maximum(over, far + number(not far_early, test) - total_cap)
    return (jnp.max(over) <= 0).astype(jnp.int32)


def front_kernel(
    n, limits, inv_in, up_in, low_in, index_ref, base_in,
    x_out, u_h_out, u_l_out, fits_out,
    map_ref, up, inv, low, up_h, up_l, inv_h, inv_l, low_h, low_l, lx_h, lx_l, f_buf, f_h, f_l, u_h, u_l, x_buf,
    local_sem, part_send, part_recv, up_send, up_recv, inv_send, inv_recv,
    low_send, low_recv, f_send, f_recv, in_sem, out_sem, out_copy_sem, *packing,
):
    packed = limits is not None
    if packed:
        ranks, want, row_want, row_in, c_out, c_in, c_h, c_l, g_h, g_l, c_send, c_recv, late_send, late_recv = packing
        total_cap, far_cap, cross = limits
        split = total_cap - far_cap
    t = lax.axis_index("tile")
    f = lax.axis_index("front")
    partner = lax.rem(f, 2) * -2 + 1 + f
    count = map_ref.shape[2]
    wc = up.shape[3]
    kr = inv.shape[2]
    lr = low.shape[2]
    order, width = x_out.shape
    chunk = min(256, width)
    chunks = width // chunk
    middle = (t >= 1) & (t <= n - 2)
    at_end = (t == 0) | (t == n - 1)
    lower = t < n // 2
    server = (t == 1) | (t == n - 2)
    end = lax.div(t - 1, n - 3) * (n - 1)
    aside = lax.rem(t + 1, n)
    first = jnp.where(lower, 0, n // 2) if packed else 0

    barrier = pltpu.get_barrier_semaphore()
    pl.semaphore_signal(barrier, inc=1, device_id=(partner, t), device_id_type=MESH)

    @pl.when(t > 0)
    def _():
        pl.semaphore_signal(barrier, inc=1, device_id=(f, t - 1), device_id_type=MESH)

    @pl.when(t < n - 1)
    def _():
        pl.semaphore_signal(barrier, inc=1, device_id=(f, t + 1), device_id_type=MESH)

    @pl.when(at_end)
    def _():
        pl.semaphore_wait(barrier, 2)

    @pl.when(middle)
    def _():
        pl.semaphore_wait(barrier, 3)

    sources = (up_in, inv_in, low_in)
    targets = (up, inv, low)

    def place(kind, child, shard):
        return targets[kind].at[child, shard - first if kind == 0 else shard]

    def local(kind):
        return pltpu.make_async_copy(sources[kind].at[0], place(kind, 0, t), local_sem.at[kind])

    def exchange(kind):
        return pltpu.make_async_remote_copy(
            src_ref=sources[kind].at[1], dst_ref=place(kind, 1, t),
            send_sem=part_send.at[kind], recv_sem=part_recv.at[kind],
            device_id=(partner, t), device_id_type=MESH,
        )

    def hop(kind, child, shard, side, source=None):
        send, recv = ((up_send, up_recv), (inv_send, inv_recv), (low_send, low_recv))[kind]
        ref = place(kind, child, shard)
        return pltpu.make_async_remote_copy(
            src_ref=ref if source is None else source, dst_ref=ref,
            send_sem=send.at[side, child, shard], recv_sem=recv.at[child, shard],
            device_id=(f, lax.rem(t + (1 if side == 0 else n - 1), n)), device_id_type=MESH,
        )

    def takes(kind, side):
        if kind == 2:
            return t + 1 <= n - 1 if side == 0 else t - 1 >= 0
        if kind == 0 and packed:
            return t == 0 if side == 0 else t == n - 1
        return t + 1 <= n - 2 if side == 0 else t - 1 >= 1

    def send(kind, child, shard, side, source=None):
        @pl.when(takes(kind, side))
        def _():
            hop(kind, child, shard, side, source).start()

    def send_own(kind, child, source=None):
        send(kind, child, t, 0, source)
        send(kind, child, t, 1, source)

    def pass_on(kinds, child, d, side, where):
        shard = t - d if side == 0 else t + d
        inside = shard >= 0 if side == 0 else shard <= n - 1

        @pl.when(inside & where)
        def _():
            for kind in kinds:
                hop(kind, child, shard, side).wait_recv()
                send(kind, child, shard, side)

    def relay_low(child, d):
        pass_on((2,), child, d, 0, t >= 0)
        pass_on((2,), child, d, 1, t >= 0)

    def inner(child, d, where):
        pass_on((2,), child, d, 1, where & lower)
        pass_on((2,), child, d, 0, where & (t >= n // 2))

    def outer(child, d):
        pass_on((2,), child, d, 0, middle & lower)
        pass_on((2,), child, d, 1, middle & (t >= n // 2))

    kinds = (1,) if packed else (1, 0)

    def near(child):
        @pl.loop(1, n)
        def _(d):
            pass_on(kinds, child, d, 0, middle & lower)
            pass_on(kinds, child, d, 1, middle & (t >= n // 2))

    def far(child):
        @pl.loop(1, n)
        def _(d):
            pass_on(kinds, child, d, 1, middle & lower)
            pass_on(kinds, child, d, 0, middle & (t >= n // 2))

    def listed(child, shard):
        return map_ref[child, :, pl.ds(pl.multiple_of(shard * wc, wc), wc)]

    def tables(child):
        row = lax.broadcasted_iota(jnp.int32, (8, 1), 0)
        side = order // 2
        tile = jnp.where(middle, end, t) * width
        ours = jnp.where(lower, 0, side)
        starts = (tile, tile, side - ours, ours)
        spans = (width, width, side, side)
        low_end = high_end = jnp.zeros((8, 1), jnp.int32)
        for q in range(4):
            low_end = jnp.where(row == q, starts[q], low_end)
            high_end = jnp.where(row == q, starts[q] + spans[q], high_end)
        before = lax.broadcasted_iota(jnp.int32, (wc, wc), 0) < lax.broadcasted_iota(jnp.int32, (wc, wc), 1)
        before = one_hot(before)
        passed = jnp.zeros((8, 1), jnp.float32)
        which = lax.broadcasted_iota(jnp.int32, (8, wc), 0)
        wants = jnp.zeros((total_cap, 8), jnp.float32)
        both = jnp.zeros((8, row_want.shape[2]), jnp.float32)
        inward = jnp.zeros((8, row_in.shape[2]), jnp.float32)
        for s in range(n):
            columns = map_ref[child, :, s * wc:(s + 1) * wc]
            is_ours = (first <= s) & (s < first + n // 2)
            fits = jnp.where(lax.rem(row, 2) == 0, is_ours.astype(jnp.int32), 1 - is_ours.astype(jnp.int32)) > 0
            inside = (columns >= low_end) & (columns < high_end) & fits
            mark = one_hot(inside)
            rank = jnp.where(inside, (dot(mark, before) + passed).astype(jnp.int32), -2 * count)
            passed = passed + jnp.sum(mark.astype(jnp.float32), axis=1, keepdims=True)
            ranks[child, :, s * wc:(s + 1) * wc] = rank
            digits = jnp.where(which == 0, columns >> 7, jnp.where(which == 1, columns & 127, 1))
            digits = digits.astype(jnp.float32).astype(jnp.bfloat16)

            def pick(q, size):
                slot = lax.broadcasted_iota(jnp.int32, (size, wc), 0)
                return one_hot((total_cap - 1 - slot if q == 1 else slot) == rank[q:q + 1])

            for q in range(2):
                wants = wants + dot(pick(q, total_cap), digits, (1, 1))
                both = both + dot(digits, pick(q, both.shape[1]), (1, 1))
            inward = inward + dot(digits, pick(3, inward.shape[1]), (1, 1))

        def across(found):
            value = found[0:1].astype(jnp.int32) * 128 + found[1:2].astype(jnp.int32)
            return jnp.where(found[2:3] > 0, value, -1)

        found = wants.astype(jnp.int32)
        want[child] = jnp.where(found[:, 2:3] > 0, found[:, 0:1] * 128 + found[:, 1:2], -1)
        row_want[child] = across(both)
        row_in[child] = across(inward)

    def cross_copy(child):
        return pltpu.make_async_remote_copy(
            src_ref=c_out.at[child], dst_ref=c_in.at[child],
            send_sem=c_send.at[child], recv_sem=c_recv.at[child],
            device_id=(f, n - 1 - t), device_id_type=MESH,
        )

    def pack(child):
        @pl.when(middle)
        def _():
            @pl.when(lower)
            def _():
                hop(0, child, 0, 0).wait_recv()

            @pl.when(t >= n // 2)
            def _():
                hop(0, child, n - 1, 1).wait_recv()

            for k in range(n // 2):
                high, low_part = parts(up[child, k])
                up_h[child, k] = high
                up_l[child, k] = low_part
            step = cross // 4 if cross % 32 == 0 else cross

            @pl.loop(0, cross // step)
            def _(j):
                base = pl.multiple_of(j * step, 8)
                total = None
                for k in range(n // 2):
                    shard = pl.ds(pl.multiple_of((first + k) * wc, wc), wc)
                    rank = ranks[child, 2:3, shard] - base
                    choose = one_hot(lax.broadcasted_iota(jnp.int32, (step, wc), 0) == rank)
                    piece = dot(choose, up_h[child, k], (1, 1)) + dot(choose, up_l[child, k], (1, 1))
                    total = piece if total is None else total + piece
                c_out[child, pl.ds(base, step), :] = total

            cross_copy(child).start()

    def place_rows(child):
        held = (n - 1 if packed and child == 1 else n) * lr
        from_shard = jnp.where(lower, 0, 1) if packed and child == 1 else 0
        used = pl.ds(pl.multiple_of(from_shard * lr, lr), held)

        @pl.loop(from_shard, from_shard + held // lr)
        def _(s):
            rows = pl.ds(pl.multiple_of(s * lr, lr), lr)
            high, low_part = parts(low[child, s])
            low_h[rows, :] = high
            low_l[rows, :] = low_part

        span = min(512, order)

        @pl.loop(0, order // span)
        def _(j):
            base = pl.multiple_of(j * span, span)
            rows = lax.broadcasted_iota(jnp.int32, (span, held), 0) + base
            choose = one_hot(rows == map_ref[child, :, used])
            lx_h[child, pl.ds(base, span), :] = dot(choose, low_h[used, :]).astype(jnp.bfloat16)
            lx_l[child, pl.ds(base, span), :] = dot(choose, low_l[used, :]).astype(jnp.bfloat16)

    def split_inverse(child):
        @pl.loop(0, n)
        def _(s):
            rows = pl.ds(pl.multiple_of(s * kr, kr), kr)
            high, low_part = parts(inv[child, s])
            inv_h[rows, :] = high
            inv_l[rows, :] = low_part

    def factor(child, columns, near_side=True, far_side=True):
        terms = []
        if near_side:
            for s in range(n // 2 if packed else n):
                choose = one_hot(columns == listed(child, first + s))
                index = (child, s) if packed else s
                terms.append((dot(choose, up_h[index], (1, 1)), dot(choose, up_l[index], (1, 1))))
        if packed and far_side:
            choose = one_hot(columns == row_in[child])
            terms.append((dot(choose, c_h[...]), dot(choose, c_l[...])))
        high, low_part = terms[0]
        for a, b in terms[1:]:
            high = high + a
            low_part = low_part + b
        high = high.astype(jnp.bfloat16)
        low_part = low_part.astype(jnp.bfloat16)
        total = dot(high, inv_h[...], (1, 1))
        total = total + dot(low_part, inv_h[...], (1, 1))
        return total + dot(high, inv_l[...], (1, 1))

    def strip(j):
        return pl.ds(pl.multiple_of(j * chunk, chunk), chunk)

    def range_of(start):
        return lax.broadcasted_iota(jnp.int32, (chunk, 1), 0) + start

    def slots_of(j):
        return slice(0, split) if j == 0 else slice(split, total_cap)

    def end_copy(child, j, target):
        if packed:
            ref = f_buf.at[child, slots_of(j)]
        else:
            ref = f_buf.at[child, j]
        return pltpu.make_async_remote_copy(
            src_ref=ref, dst_ref=ref,
            send_sem=f_send.at[child, j], recv_sem=f_recv.at[child, j],
            device_id=(f, target), device_id_type=MESH,
        )

    def keep(child, j, value):
        for ref, part in zip((f_h, f_l), parts(value)):
            ref[child, strip(j), :] = part

    def serve_near(child):
        @pl.when(middle)
        def _():
            split_inverse(child)
            f_buf[child, slots_of(0)] = factor(child, want[child, slots_of(0)], far_side=False)
            end_copy(child, 0, end).start()

    def serve_far(child):
        @pl.when(middle)
        def _():
            cross_copy(child).wait_recv()
            high, low_part = parts(c_in[child])
            rest = jnp.zeros((c_h.shape[0] - cross, c_h.shape[1]), jnp.bfloat16)
            c_h[:cross] = high
            c_l[:cross] = low_part
            c_h[cross:] = rest
            c_l[cross:] = rest
            f_buf[child, slots_of(1)] = factor(child, want[child, slots_of(1)])
            end_copy(child, 1, end).start()

    def serve_all(child):
        @pl.when(middle)
        def _():
            split_inverse(child)

            @pl.loop(0, n)
            def _(s):
                high, low_part = parts(up[child, s])
                up_h[s] = high
                up_l[s] = low_part

            @pl.when(server)
            def _():
                @pl.loop(0, chunks)
                def _(j):
                    f_buf[child, j] = factor(child, range_of(end * width + j * chunk))
                    end_copy(child, j, end).start()

    def serve_own(child):
        @pl.when(middle)
        def _():
            @pl.loop(0, chunks)
            def _(j):
                keep(child, j, factor(child, range_of(t * width + j * chunk)))

    def expand(child, begin, stop, stop_pad):
        value = f_buf[child, begin:stop]
        for ref, part in zip((g_h, g_l), parts(value)):
            ref[begin:stop] = part
            if stop < stop_pad:
                ref[stop:stop_pad] = jnp.zeros((stop_pad - stop, ref.shape[1]), jnp.bfloat16)

        @pl.loop(0, chunks)
        def _(j):
            choose = one_hot(range_of(t * width + j * chunk) == row_want[child, :, begin:stop_pad])
            for ref, source in ((f_h, g_h), (f_l, g_l)):
                found = dot(choose, source[begin:stop_pad, :]).astype(jnp.bfloat16)
                ref[child, strip(j), :] = found if begin == 0 else ref[child, strip(j), :] + found

    def take_first(child):
        @pl.when(at_end)
        def _():
            end_copy(child, 0, aside).wait_recv()
            expand(child, 0, split // 128 * 128, split // 128 * 128)

    def take_factor(child):
        @pl.when(at_end)
        def _():
            if packed:
                end_copy(child, 1, aside).wait_recv()
                expand(child, split // 128 * 128, total_cap, g_h.shape[0])
            else:
                @pl.loop(0, chunks)
                def _(j):
                    end_copy(child, j, aside).wait_recv()
                    keep(child, j, f_buf[child, j])

    slots = x_buf.shape[0]
    ahead = slots // 2
    tall = x_buf.shape[1]
    per = order // tall
    blocks = per * chunks

    def window(ref, i):
        rows = pl.ds(pl.multiple_of(lax.rem(i, per) * tall, tall), tall)
        return ref.at[rows, strip(lax.div(i, per))]

    def store(i):
        slot = lax.rem(i, slots)
        return pltpu.make_async_copy(x_buf.at[slot], window(x_out, i), out_sem.at[slot])

    def settle(begin, stop):
        for i in range(max(stop - slots, begin), stop):
            store(i).wait()

    def subtract(child, begin, stop):
        source = base_in if child == 0 else x_out

        def load(i):
            slot = lax.rem(i, slots)
            return pltpu.make_async_copy(window(source, i), x_buf.at[slot], in_sem.at[slot])

        for i in range(begin, min(begin + ahead, stop)):
            load(i).start()
        if begin == 0:
            take_factor(child)

        @pl.loop(begin, stop)
        def _(i):
            j = lax.div(i, per)

            @pl.when(i + ahead < stop)
            def _():
                @pl.when(i >= begin + slots - ahead)
                def _():
                    store(i - (slots - ahead)).wait()

                load(i + ahead).start()

            rows = pl.ds(pl.multiple_of(lax.rem(i, per) * tall, tall), tall)
            high = f_h[child, strip(j), :]
            left = lx_h[child, rows, :]
            total = dot(left, high, (1, 1))
            total = total + dot(left, f_l[child, strip(j), :], (1, 1))
            total = total + dot(lx_l[child, rows, :], high, (1, 1))
            load(i).wait()
            slot = lax.rem(i, slots)
            x_buf[slot] = x_buf[slot] - total
            store(i).start()

    def hand_on(k, q):
        return pltpu.make_async_copy(
            (u_h, u_l)[k].at[late_rows(q)], (u_h_out, u_l_out)[k].at[late_rows(q)], out_copy_sem.at[k, q]
        )

    late = jnp.where(lower, n - 1, 0)

    def late_rows(k):
        return slice(k * (lr // 2), (k + 1) * (lr // 2))

    def late_copy(k, target):
        ref = low.at[1, late, late_rows(k)]
        return pltpu.make_async_remote_copy(
            src_ref=ref, dst_ref=ref, send_sem=late_send.at[k], recv_sem=late_recv.at[k],
            device_id=(f, target), device_id_type=MESH,
        )

    def take_late():
        @pl.when(middle)
        def _():
            @pl.when(lower)
            def _():
                hop(2, 1, n - 1, 1).wait_recv()

            @pl.when(t >= n // 2)
            def _():
                hop(2, 1, 0, 0).wait_recv()

            for k in range(2):
                late_copy(k, end).start()

    def last_update():
        @pl.loop(0, 2)
        def _(k):
            @pl.when(at_end)
            def _():
                for q in range(2):
                    @pl.when(k == q)
                    def _():
                        late_copy(q, aside).wait_recv()

            rows = pl.ds(pl.multiple_of(k * (lr // 2), lr // 2), lr // 2)
            left = parts(low[1, late, rows, :])
            for j in range(chunks):
                columns = slice(j * chunk, (j + 1) * chunk)
                total = dot(left[0], f_h[1, columns, :], (1, 1))
                total = total + dot(left[0], f_l[1, columns, :], (1, 1))
                total = total + dot(left[1], f_h[1, columns, :], (1, 1))
                u_h[rows, columns], u_l[rows, columns] = parts(total)

            for q in range(2):
                @pl.when(k == q)
                def _():
                    for m in range(2):
                        hand_on(m, q).start()
    send_own(2, 0, low_in.at[0])
    for kind in (2, 1, 0):
        exchange(kind).start()
        local(kind).start()
    exchange(2).wait()

    @pl.when(middle if packed else t >= 0)
    def _():
        send_own(2, 1)

    local(2).wait()
    for kind in (1, 0):
        local(kind).wait()
        exchange(kind).wait()

    @pl.when(at_end)
    def _():
        for child in range(2):
            for kind in (1, 0):
                send_own(kind, child)
        if packed:
            send_own(2, 1)

    for child in range(2):
        map_ref[child] = index_ref[f if child == 0 else partner, child:child + 1, :]
    if packed:
        pl.loop(0, 2)(tables)
        fits_out[0] = counts_fit(index_ref, order, width, limits)

        @pl.when(middle)
        def _():
            outer(0, 1)
            inner(0, 1, middle)
            send_own(1, 0)
            near(0)
            inner(1, 1, middle)
            pack(0)
            send_own(1, 1)
            near(1)
            inner(0, 2, middle)

        @pl.when(at_end)
        def _():
            for child, d in ((0, 1), (1, 1), (0, 2), (1, 2)):
                inner(child, d, at_end)
            place_rows(1)
            inner(0, 3, at_end)

        place_rows(0)

        @pl.when(middle)
        def _():
            pack(1)
            far(0)
            serve_near(0)
            outer(1, 1)
            serve_far(0)
            serve_own(0)
            place_rows(1)
            far(1)
            serve_near(1)

        take_first(0)
        subtract(0, 0, blocks // 2)
        settle(0, blocks // 2)

        @pl.when(middle)
        def _():
            serve_far(1)
            serve_own(1)

        subtract(0, blocks // 2, blocks)
        settle(blocks // 2, blocks)
        take_first(1)
        take_late()
        subtract(1, 0, blocks)
        last_update()
        settle(0, blocks)
        for m in range(2):
            for q in range(2):
                hand_on(m, q).wait()
    else:
        relay_low(0, 1)
        relay_low(1, 1)

        @pl.when(middle)
        def _():
            send_own(1, 0)
            send_own(0, 0)

        relay_low(0, 2)
        near(0)

        @pl.when(middle)
        def _():
            send_own(1, 1)
            send_own(0, 1)

        relay_low(1, 2)

        @pl.loop(3, n)
        def _(d):
            relay_low(0, d)
            relay_low(1, d)

        near(1)
        place_rows(0)
        place_rows(1)
        for child in range(2):
            far(child)
            serve_all(child)
            serve_own(child)
            subtract(child, 0, blocks)
            settle(0, blocks)
        for m, ref in enumerate((u_h, u_l)):
            ref[...] = jnp.zeros_like(ref)
            for q in range(2):
                hand_on(m, q).start()
                hand_on(m, q).wait()
        fits_out[0] = 1

    for child in range(2):
        @pl.loop(0, n)
        def _(s):
            for side in range(2):
                for kind in range(3):
                    whole = ~(middle & (s == late)) if packed and (kind, child) == (2, 1) else t >= 0

                    @pl.when(takes(kind, side) & (s <= t if side == 0 else s >= t) & whole)
                    def _():
                        hop(kind, child, s, side).wait_send()

        @pl.when(server)
        def _():
            if packed:
                for j in range(2):
                    end_copy(child, j, aside).wait_send()
            else:
                @pl.loop(0, chunks)
                def _(j):
                    end_copy(child, j, aside).wait_send()

        if packed:
            @pl.when(middle)
            def _():
                cross_copy(child).wait_send()

            @pl.when(server)
            def _():
                if child == 1:
                    for k in range(2):
                        late_copy(k, aside).wait_send()


def capacity(draws, share, order):
    spread_of = math.sqrt(draws * share * (1 - share) * (1 - draws / order))
    return -(-math.ceil(draws * share + 4.5 * spread_of) // 8) * 8


def padded(rows):
    return -(-rows // 128) * 128


def assembled(inverse, upper, lower, maps, base, n, limits):
    order, width = base.shape
    pivots = inverse.shape[2]
    count = maps.shape[2]
    kr, wc, lr = inverse.shape[1], upper.shape[2], lower.shape[1]
    vmem = pltpu.VMEM
    dma = pltpu.SemaphoreType.DMA
    f32, b16 = jnp.float32, jnp.bfloat16
    chunk = min(256, width)
    chunks = width // chunk
    slots = 4
    packed = limits is not None
    held, extra = n, []
    f_shape, f_sems = (2, chunks, chunk, pivots), (2, chunks)
    u_shape = (n, pivots, wc)
    if packed:
        total_cap, _, cross = limits
        cap_pad, cross_pad = padded(total_cap), padded(cross)
        held = n // 2
        f_shape, f_sems = (2, total_cap, pivots), (2, 2)
        u_shape = (2, held, pivots, wc)
        extra = [
            vmem((2, 8, count), jnp.int32),
            vmem((2, total_cap, 1), jnp.int32),
            vmem((2, 1, cap_pad), jnp.int32),
            vmem((2, 1, cross_pad), jnp.int32),
            vmem((2, cross, pivots), f32),
            vmem((2, cross, pivots), f32),
            vmem((cross_pad, pivots), b16),
            vmem((cross_pad, pivots), b16),
            vmem((cap_pad, pivots), b16),
            vmem((cap_pad, pivots), b16),
            dma((2,)), dma((2,)), dma((2,)), dma((2,)),
        ]
    whole = pl.BlockSpec(memory_space=pl.ANY)
    return pl.pallas_call(
        functools.partial(front_kernel, n, limits),
        out_shape=[jax.ShapeDtypeStruct((order, width), f32)]
        + [jax.ShapeDtypeStruct((lr, width), b16)] * 2
        + [jax.ShapeDtypeStruct((1,), jnp.int32)],
        in_specs=[whole] * 3 + [pl.BlockSpec(memory_space=vmem), whole],
        out_specs=[whole] * 3 + [pl.BlockSpec(memory_space=pltpu.SMEM)],
        scratch_shapes=[
            vmem((2, 1, count), jnp.int32),
            vmem((2, held, pivots, wc), f32),
            vmem((2, n, kr, pivots), f32),
            vmem((2, n, lr, pivots), f32),
            vmem(u_shape, b16),
            vmem(u_shape, b16),
            vmem((n * kr, pivots), b16),
            vmem((n * kr, pivots), b16),
            vmem((count, pivots), b16),
            vmem((count, pivots), b16),
            vmem((2, order, pivots), b16),
            vmem((2, order, pivots), b16),
            vmem(f_shape, f32),
            vmem((2, width, pivots), b16),
            vmem((2, width, pivots), b16),
            vmem((lr, width), b16),
            vmem((lr, width), b16),
            vmem((slots, min(1024, order), chunk), f32),
            dma((3,)), dma((3,)), dma((3,)),
            dma((2, 2, n)), dma((2, n)),
            dma((2, 2, n)), dma((2, n)),
            dma((2, 2, n)), dma((2, n)),
            dma(f_sems), dma(f_sems),
            dma((slots,)), dma((slots,)), dma((2, 2)),
        ] + extra,
        compiler_params=pltpu.CompilerParams(
            collective_id=int(packed), has_side_effects=True, vmem_limit_bytes=63 * 1024 * 1024
        ),
    )(inverse, upper, lower, maps, base)


def finish_kernel(
    n, index_ref, x_in, u_h_in, u_l_in, out,
    x_buf, u_h, u_l, x_sem, out_sem, u_sem,
):
    t = lax.axis_index("tile")
    f = lax.axis_index("front")
    partner = lax.rem(f, 2) * -2 + 1 + f
    slots, rows, width = x_buf.shape
    lr = u_h.shape[0]
    blocks = out.shape[0] // rows
    ahead = slots // 2
    chunk = min(256, width)
    shard = jnp.where(t < n // 2, n - 1, 0)
    places = index_ref[partner, 1:2, pl.ds(pl.multiple_of(shard * lr, lr), lr)]

    def window(i):
        return pl.ds(pl.multiple_of(i * rows, rows), rows)

    def load(i):
        slot = lax.rem(i, slots)
        return pltpu.make_async_copy(x_in.at[window(i)], x_buf.at[slot], x_sem.at[slot])

    def store(i):
        slot = lax.rem(i, slots)
        return pltpu.make_async_copy(x_buf.at[slot], out.at[window(i)], out_sem.at[slot])

    first = [
        pltpu.make_async_copy(source, target, u_sem.at[k])
        for k, (source, target) in enumerate(((u_h_in, u_h), (u_l_in, u_l)))
    ]
    for copy in first:
        copy.start()
    for i in range(min(ahead, blocks)):
        load(i).start()
    for copy in first:
        copy.wait()

    @pl.loop(0, blocks)
    def _(i):
        @pl.when(i + ahead < blocks)
        def _():
            @pl.when(i >= slots - ahead)
            def _():
                store(i - (slots - ahead)).wait()

            load(i + ahead).start()

        choose = one_hot(lax.broadcasted_iota(jnp.int32, (rows, lr), 0) + i * rows == places)
        load(i).wait()
        slot = lax.rem(i, slots)
        for j in range(width // chunk):
            columns = slice(j * chunk, (j + 1) * chunk)
            total = dot(choose, u_h[:, columns]) + dot(choose, u_l[:, columns])
            x_buf[slot, :, columns] = x_buf[slot, :, columns] - total
        store(i).start()

    for i in range(max(blocks - slots, 0), blocks):
        store(i).wait()


def finished(n, index_map, x, u_h, u_l):
    order, width = x.shape
    rows, slots = min(512, order), 6
    vmem, dma, b16 = pltpu.VMEM, pltpu.SemaphoreType.DMA, jnp.bfloat16
    whole = pl.BlockSpec(memory_space=pl.ANY)
    return pl.pallas_call(
        functools.partial(finish_kernel, n),
        out_shape=jax.ShapeDtypeStruct(x.shape, x.dtype),
        in_specs=[pl.BlockSpec(memory_space=vmem)] + [whole] * 3,
        out_specs=whole,
        scratch_shapes=[
            vmem((slots, rows, width), x.dtype),
            vmem(u_h.shape, b16),
            vmem(u_h.shape, b16),
            dma((slots,)), dma((slots,)), dma((2,)),
        ],
        compiler_params=pltpu.CompilerParams(vmem_limit_bytes=60 * 1024 * 1024),
    )(index_map, x, u_h, u_l)


def shards(pivot_inverse, panel_upper, panel_lower, index_map, parent_base):
    n = lax.axis_size("tile")
    order, width = parent_base.shape[1:]
    count = index_map.shape[2]
    operands = (pivot_inverse[0], panel_upper[0], panel_lower[0], index_map, parent_base[0])

    side = order // 2
    total = capacity(count, width / order, order)
    far = capacity(count // 2, width / order, order)
    cross = capacity(count // 2, 1 / 2, order)

    def run(limits, *args):
        return tuple(assembled(*args, n, limits))

    def whole_transfers():
        return finished(n, index_map, *run(None, *operands)[:3])

    if n != 4 or total >= width or total - far < 128 or cross >= count // 2:
        return whole_transfers()[None]

    x, u_h, u_l, fits = run((total, far, cross), *operands)
    return lax.cond(fits[0] > 0, lambda: finished(n, index_map, x, u_h, u_l), whole_transfers)[None]


def solution(mesh):
    return jax.shard_map(
        shards,
        mesh=mesh,
        in_specs=(
            P("front", None, "tile", None),
            P("front", None, None, "tile"),
            P("front", None, "tile", None),
            P(),
            P("front", None, "tile"),
        ),
        out_specs=P("front", None, "tile"),
        check_vma=False,
    )
```

```python
import functools
import math

import jax
import jax.numpy as jnp
from jax import lax
from jax.experimental import pallas as pl
from jax.experimental.pallas import tpu as pltpu
from jax.sharding import PartitionSpec as P

MESH = pl.DeviceIdType.MESH


def parts(value):
    high = value.astype(jnp.bfloat16)
    return high, (value - high.astype(jnp.float32)).astype(jnp.bfloat16)


def dot(left, right, contract=(1, 0)):
    dims = (((contract[0],), (contract[1],)), ((), ()))
    return lax.dot_general(left, right, dims, preferred_element_type=jnp.float32)


def one_hot(match):
    return match.astype(jnp.float32).astype(jnp.bfloat16)


def counts_fit(index_ref, order, width, limits):
    total_cap, far_cap, cross = limits
    half = index_ref.shape[2] // 2

    def number(early, test):
        part = index_ref[:, :, :half] if early else index_ref[:, :, half:]
        return jnp.sum(test(part).astype(jnp.int32), axis=2, keepdims=True)

    def first(m):
        return m < width

    def last(m):
        return m >= order - width

    over = number(True, lambda m: m >= order // 2) - cross
    over = jnp.maximum(over, number(False, lambda m: m < order // 2) - cross)
    for test, far_early in ((first, False), (last, True)):
        far = number(far_early, test)
        over = jnp.maximum(over, far - far_cap)
        over = jnp.maximum(over, far + number(not far_early, test) - total_cap)
    return (jnp.max(over) <= 0).astype(jnp.int32)


def front_kernel(
    n, limits, inv_in, up_in, low_in, index_ref, base_in,
    x_out, u_h_out, u_l_out, fits_out,
    map_ref, up, inv, low, up_h, up_l, inv_h, inv_l, low_h, low_l, lx_h, lx_l, f_buf, f_h, f_l, u_h, u_l, x_buf,
    local_sem, part_send, part_recv, up_send, up_recv, inv_send, inv_recv,
    low_send, low_recv, f_send, f_recv, in_sem, out_sem, out_copy_sem, *packing,
):
    packed = limits is not None
    if packed:
        ranks, want, row_want, row_in, c_out, c_in, c_h, c_l, g_h, g_l, c_send, c_recv, late_send, late_recv = packing
        total_cap, far_cap, cross = limits
        split = total_cap - far_cap
    t = lax.axis_index("tile")
    f = lax.axis_index("front")
    partner = lax.rem(f, 2) * -2 + 1 + f
    count = map_ref.shape[2]
    wc = up.shape[3]
    kr = inv.shape[2]
    lr = low.shape[2]
    order, width = x_out.shape
    chunk = min(256, width)
    chunks = width // chunk
    middle = (t >= 1) & (t <= n - 2)
    at_end = (t == 0) | (t == n - 1)
    lower = t < n // 2
    server = (t == 1) | (t == n - 2)
    end = lax.div(t - 1, n - 3) * (n - 1)
    aside = lax.rem(t + 1, n)
    first = jnp.where(lower, 0, n // 2) if packed else 0

    barrier = pltpu.get_barrier_semaphore()
    pl.semaphore_signal(barrier, inc=1, device_id=(partner, t), device_id_type=MESH)

    @pl.when(t > 0)
    def _():
        pl.semaphore_signal(barrier, inc=1, device_id=(f, t - 1), device_id_type=MESH)

    @pl.when(t < n - 1)
    def _():
        pl.semaphore_signal(barrier, inc=1, device_id=(f, t + 1), device_id_type=MESH)

    @pl.when(at_end)
    def _():
        pl.semaphore_wait(barrier, 2)

    @pl.when(middle)
    def _():
        pl.semaphore_wait(barrier, 3)

    sources = (up_in, inv_in, low_in)
    targets = (up, inv, low)

    def place(kind, child, shard):
        return targets[kind].at[child, shard - first if kind == 0 else shard]

    def local(kind):
        return pltpu.make_async_copy(sources[kind].at[0], place(kind, 0, t), local_sem.at[kind])

    def exchange(kind):
        return pltpu.make_async_remote_copy(
            src_ref=sources[kind].at[1], dst_ref=place(kind, 1, t),
            send_sem=part_send.at[kind], recv_sem=part_recv.at[kind],
            device_id=(partner, t), device_id_type=MESH,
        )

    def hop(kind, child, shard, side, source=None):
        send, recv = ((up_send, up_recv), (inv_send, inv_recv), (low_send, low_recv))[kind]
        ref = place(kind, child, shard)
        return pltpu.make_async_remote_copy(
            src_ref=ref if source is None else source, dst_ref=ref,
            send_sem=send.at[side, child, shard], recv_sem=recv.at[child, shard],
            device_id=(f, lax.rem(t + (1 if side == 0 else n - 1), n)), device_id_type=MESH,
        )

    def takes(kind, side):
        if kind == 2:
            return t + 1 <= n - 1 if side == 0 else t - 1 >= 0
        if kind == 0 and packed:
            return t == 0 if side == 0 else t == n - 1
        return t + 1 <= n - 2 if side == 0 else t - 1 >= 1

    def send(kind, child, shard, side, source=None):
        @pl.when(takes(kind, side))
        def _():
            hop(kind, child, shard, side, source).start()

    def send_own(kind, child, source=None):
        send(kind, child, t, 0, source)
        send(kind, child, t, 1, source)

    def pass_on(kinds, child, d, side, where):
        shard = t - d if side == 0 else t + d
        inside = shard >= 0 if side == 0 else shard <= n - 1

        @pl.when(inside & where)
        def _():
            for kind in kinds:
                hop(kind, child, shard, side).wait_recv()
                send(kind, child, shard, side)

    def relay_low(child, d):
        pass_on((2,), child, d, 0, t >= 0)
        pass_on((2,), child, d, 1, t >= 0)

    def inner(child, d, where):
        pass_on((2,), child, d, 1, where & lower)
        pass_on((2,), child, d, 0, where & (t >= n // 2))

    def outer(child, d):
        pass_on((2,), child, d, 0, middle & lower)
        pass_on((2,), child, d, 1, middle & (t >= n // 2))

    kinds = (1,) if packed else (1, 0)

    def near(child):
        @pl.loop(1, n)
        def _(d):
            pass_on(kinds, child, d, 0, middle & lower)
            pass_on(kinds, child, d, 1, middle & (t >= n // 2))

    def far(child):
        @pl.loop(1, n)
        def _(d):
            pass_on(kinds, child, d, 1, middle & lower)
            pass_on(kinds, child, d, 0, middle & (t >= n // 2))

    def listed(child, shard):
        return map_ref[child, :, pl.ds(pl.multiple_of(shard * wc, wc), wc)]

    def tables(child):
        row = lax.broadcasted_iota(jnp.int32, (8, 1), 0)
        side = order // 2
        tile = jnp.where(middle, end, t) * width
        ours = jnp.where(lower, 0, side)
        starts = (tile, tile, side - ours, ours)
        spans = (width, width, side, side)
        low_end = high_end = jnp.zeros((8, 1), jnp.int32)
        for q in range(4):
            low_end = jnp.where(row == q, starts[q], low_end)
            high_end = jnp.where(row == q, starts[q] + spans[q], high_end)
        before = lax.broadcasted_iota(jnp.int32, (wc, wc), 0) < lax.broadcasted_iota(jnp.int32, (wc, wc), 1)
        before = one_hot(before)
        passed = jnp.zeros((8, 1), jnp.float32)
        which = lax.broadcasted_iota(jnp.int32, (8, wc), 0)
        wants = jnp.zeros((total_cap, 8), jnp.float32)
        both = jnp.zeros((8, row_want.shape[2]), jnp.float32)
        inward = jnp.zeros((8, row_in.shape[2]), jnp.float32)
        for s in range(n):
            columns = map_ref[child, :, s * wc:(s + 1) * wc]
            is_ours = (first <= s) & (s < first + n // 2)
            fits = jnp.where(lax.rem(row, 2) == 0, is_ours.astype(jnp.int32), 1 - is_ours.astype(jnp.int32)) > 0
            inside = (columns >= low_end) & (columns < high_end) & fits
            mark = one_hot(inside)
            rank = jnp.where(inside, (dot(mark, before) + passed).astype(jnp.int32), -2 * count)
            passed = passed + jnp.sum(mark.astype(jnp.float32), axis=1, keepdims=True)
            ranks[child, :, s * wc:(s + 1) * wc] = rank
            digits = jnp.where(which == 0, columns >> 7, jnp.where(which == 1, columns & 127, 1))
            digits = digits.astype(jnp.float32).astype(jnp.bfloat16)

            def pick(q, size):
                slot = lax.broadcasted_iota(jnp.int32, (size, wc), 0)
                return one_hot((total_cap - 1 - slot if q == 1 else slot) == rank[q:q + 1])

            for q in range(2):
                wants = wants + dot(pick(q, total_cap), digits, (1, 1))
                both = both + dot(digits, pick(q, both.shape[1]), (1, 1))
            inward = inward + dot(digits, pick(3, inward.shape[1]), (1, 1))

        def across(found):
            value = found[0:1].astype(jnp.int32) * 128 + found[1:2].astype(jnp.int32)
            return jnp.where(found[2:3] > 0, value, -1)

        found = wants.astype(jnp.int32)
        want[child] = jnp.where(found[:, 2:3] > 0, found[:, 0:1] * 128 + found[:, 1:2], -1)
        row_want[child] = across(both)
        row_in[child] = across(inward)

    def cross_copy(child):
        return pltpu.make_async_remote_copy(
            src_ref=c_out.at[child], dst_ref=c_in.at[child],
            send_sem=c_send.at[child], recv_sem=c_recv.at[child],
            device_id=(f, n - 1 - t), device_id_type=MESH,
        )

    def pack(child):
        @pl.when(middle)
        def _():
            @pl.when(lower)
            def _():
                hop(0, child, 0, 0).wait_recv()

            @pl.when(t >= n // 2)
            def _():
                hop(0, child, n - 1, 1).wait_recv()

            for k in range(n // 2):
                high, low_part = parts(up[child, k])
                up_h[child, k] = high
                up_l[child, k] = low_part
            step = cross // 4 if cross % 32 == 0 else cross

            @pl.loop(0, cross // step)
            def _(j):
                base = pl.multiple_of(j * step, 8)
                total = None
                for k in range(n // 2):
                    shard = pl.ds(pl.multiple_of((first + k) * wc, wc), wc)
                    rank = ranks[child, 2:3, shard] - base
                    choose = one_hot(lax.broadcasted_iota(jnp.int32, (step, wc), 0) == rank)
                    piece = dot(choose, up_h[child, k], (1, 1)) + dot(choose, up_l[child, k], (1, 1))
                    total = piece if total is None else total + piece
                c_out[child, pl.ds(base, step), :] = total

            cross_copy(child).start()

    def place_rows(child):
        held = (n - 1 if packed and child == 1 else n) * lr
        from_shard = jnp.where(lower, 0, 1) if packed and child == 1 else 0
        used = pl.ds(pl.multiple_of(from_shard * lr, lr), held)

        @pl.loop(from_shard, from_shard + held // lr)
        def _(s):
            rows = pl.ds(pl.multiple_of(s * lr, lr), lr)
            high, low_part = parts(low[child, s])
            low_h[rows, :] = high
            low_l[rows, :] = low_part

        span = min(512, order)

        @pl.loop(0, order // span)
        def _(j):
            base = pl.multiple_of(j * span, span)
            rows = lax.broadcasted_iota(jnp.int32, (span, held), 0) + base
            choose = one_hot(rows == map_ref[child, :, used])
            lx_h[child, pl.ds(base, span), :] = dot(choose, low_h[used, :]).astype(jnp.bfloat16)
            lx_l[child, pl.ds(base, span), :] = dot(choose, low_l[used, :]).astype(jnp.bfloat16)

    def split_inverse(child):
        @pl.loop(0, n)
        def _(s):
            rows = pl.ds(pl.multiple_of(s * kr, kr), kr)
            high, low_part = parts(inv[child, s])
            inv_h[rows, :] = high
            inv_l[rows, :] = low_part

    def factor(child, columns, near_side=True, far_side=True):
        terms = []
        if near_side:
            for s in range(n // 2 if packed else n):
                choose = one_hot(columns == listed(child, first + s))
                index = (child, s) if packed else s
                terms.append((dot(choose, up_h[index], (1, 1)), dot(choose, up_l[index], (1, 1))))
        if packed and far_side:
            choose = one_hot(columns == row_in[child])
            terms.append((dot(choose, c_h[...]), dot(choose, c_l[...])))
        high, low_part = terms[0]
        for a, b in terms[1:]:
            high = high + a
            low_part = low_part + b
        high = high.astype(jnp.bfloat16)
        low_part = low_part.astype(jnp.bfloat16)
        total = dot(high, inv_h[...], (1, 1))
        total = total + dot(low_part, inv_h[...], (1, 1))
        return total + dot(high, inv_l[...], (1, 1))

    def strip(j):
        return pl.ds(pl.multiple_of(j * chunk, chunk), chunk)

    def range_of(start):
        return lax.broadcasted_iota(jnp.int32, (chunk, 1), 0) + start

    def slots_of(j):
        return slice(0, split) if j == 0 else slice(split, total_cap)

    def end_copy(child, j, target):
        if packed:
            ref = f_buf.at[child, slots_of(j)]
        else:
            ref = f_buf.at[child, j]
        return pltpu.make_async_remote_copy(
            src_ref=ref, dst_ref=ref,
            send_sem=f_send.at[child, j], recv_sem=f_recv.at[child, j],
            device_id=(f, target), device_id_type=MESH,
        )

    def keep(child, j, value):
        for ref, part in zip((f_h, f_l), parts(value)):
            ref[child, strip(j), :] = part

    def serve_near(child):
        @pl.when(middle)
        def _():
            split_inverse(child)
            f_buf[child, slots_of(0)] = factor(child, want[child, slots_of(0)], far_side=False)
            end_copy(child, 0, end).start()

    def serve_far(child):
        @pl.when(middle)
        def _():
            cross_copy(child).wait_recv()
            high, low_part = parts(c_in[child])
            rest = jnp.zeros((c_h.shape[0] - cross, c_h.shape[1]), jnp.bfloat16)
            c_h[:cross] = high
            c_l[:cross] = low_part
            c_h[cross:] = rest
            c_l[cross:] = rest
            f_buf[child, slots_of(1)] = factor(child, want[child, slots_of(1)])
            end_copy(child, 1, end).start()

    def serve_all(child):
        @pl.when(middle)
        def _():
            split_inverse(child)

            @pl.loop(0, n)
            def _(s):
                high, low_part = parts(up[child, s])
                up_h[s] = high
                up_l[s] = low_part

            @pl.when(server)
            def _():
                @pl.loop(0, chunks)
                def _(j):
                    f_buf[child, j] = factor(child, range_of(end * width + j * chunk))
                    end_copy(child, j, end).start()

    def serve_own(child):
        @pl.when(middle)
        def _():
            @pl.loop(0, chunks)
            def _(j):
                keep(child, j, factor(child, range_of(t * width + j * chunk)))

    def expand(child, begin, stop, stop_pad):
        value = f_buf[child, begin:stop]
        for ref, part in zip((g_h, g_l), parts(value)):
            ref[begin:stop] = part
            if stop < stop_pad:
                ref[stop:stop_pad] = jnp.zeros((stop_pad - stop, ref.shape[1]), jnp.bfloat16)

        @pl.loop(0, chunks)
        def _(j):
            choose = one_hot(range_of(t * width + j * chunk) == row_want[child, :, begin:stop_pad])
            for ref, source in ((f_h, g_h), (f_l, g_l)):
                found = dot(choose, source[begin:stop_pad, :]).astype(jnp.bfloat16)
                ref[child, strip(j), :] = found if begin == 0 else ref[child, strip(j), :] + found

    def take_first(child):
        @pl.when(at_end)
        def _():
            end_copy(child, 0, aside).wait_recv()
            expand(child, 0, split // 128 * 128, split // 128 * 128)

    def take_factor(child):
        @pl.when(at_end)
        def _():
            if packed:
                end_copy(child, 1, aside).wait_recv()
                expand(child, split // 128 * 128, total_cap, g_h.shape[0])
            else:
                @pl.loop(0, chunks)
                def _(j):
                    end_copy(child, j, aside).wait_recv()
                    keep(child, j, f_buf[child, j])

    slots = x_buf.shape[0]
    ahead = slots // 2
    tall = x_buf.shape[1]
    per = order // tall
    blocks = per * chunks

    def window(ref, i):
        rows = pl.ds(pl.multiple_of(lax.rem(i, per) * tall, tall), tall)
        return ref.at[rows, strip(lax.div(i, per))]

    def store(i):
        slot = lax.rem(i, slots)
        return pltpu.make_async_copy(x_buf.at[slot], window(x_out, i), out_sem.at[slot])

    def settle(begin, stop):
        for i in range(max(stop - slots, begin), stop):
            store(i).wait()

    def subtract(child, begin, stop):
        source = base_in if child == 0 else x_out

        def load(i):
            slot = lax.rem(i, slots)
            return pltpu.make_async_copy(window(source, i), x_buf.at[slot], in_sem.at[slot])

        for i in range(begin, min(begin + ahead, stop)):
            load(i).start()
        if begin == 0:
            take_factor(child)

        @pl.loop(begin, stop)
        def _(i):
            j = lax.div(i, per)

            @pl.when(i + ahead < stop)
            def _():
                @pl.when(i >= begin + slots - ahead)
                def _():
                    store(i - (slots - ahead)).wait()

                load(i + ahead).start()

            rows = pl.ds(pl.multiple_of(lax.rem(i, per) * tall, tall), tall)
            high = f_h[child, strip(j), :]
            left = lx_h[child, rows, :]
            total = dot(left, high, (1, 1))
            total = total + dot(left, f_l[child, strip(j), :], (1, 1))
            total = total + dot(lx_l[child, rows, :], high, (1, 1))
            load(i).wait()
            slot = lax.rem(i, slots)
            x_buf[slot] = x_buf[slot] - total
            store(i).start()

    def hand_on(k, q):
        return pltpu.make_async_copy(
            (u_h, u_l)[k].at[late_rows(q)], (u_h_out, u_l_out)[k].at[late_rows(q)], out_copy_sem.at[k, q]
        )

    late = jnp.where(lower, n - 1, 0)

    def late_rows(k):
        return slice(k * (lr // 2), (k + 1) * (lr // 2))

    def late_copy(k, target):
        ref = low.at[1, late, late_rows(k)]
        return pltpu.make_async_remote_copy(
            src_ref=ref, dst_ref=ref, send_sem=late_send.at[k], recv_sem=late_recv.at[k],
            device_id=(f, target), device_id_type=MESH,
        )

    def take_late():
        @pl.when(middle)
        def _():
            @pl.when(lower)
            def _():
                hop(2, 1, n - 1, 1).wait_recv()

            @pl.when(t >= n // 2)
            def _():
                hop(2, 1, 0, 0).wait_recv()

            for k in range(2):
                late_copy(k, end).start()

    def last_update():
        @pl.loop(0, 2)
        def _(k):
            @pl.when(at_end)
            def _():
                for q in range(2):
                    @pl.when(k == q)
                    def _():
                        late_copy(q, aside).wait_recv()

            rows = pl.ds(pl.multiple_of(k * (lr // 2), lr // 2), lr // 2)
            left = parts(low[1, late, rows, :])
            for j in range(chunks):
                columns = slice(j * chunk, (j + 1) * chunk)
                total = dot(left[0], f_h[1, columns, :], (1, 1))
                total = total + dot(left[0], f_l[1, columns, :], (1, 1))
                total = total + dot(left[1], f_h[1, columns, :], (1, 1))
                u_h[rows, columns], u_l[rows, columns] = parts(total)

            for q in range(2):
                @pl.when(k == q)
                def _():
                    for m in range(2):
                        hand_on(m, q).start()
    send_own(2, 0, low_in.at[0])
    for kind in (2, 1, 0):
        exchange(kind).start()
        local(kind).start()
    exchange(2).wait()

    @pl.when(middle if packed else t >= 0)
    def _():
        send_own(2, 1)

    local(2).wait()
    for kind in (1, 0):
        local(kind).wait()
        exchange(kind).wait()

    @pl.when(at_end)
    def _():
        for child in range(2):
            for kind in (1, 0):
                send_own(kind, child)
        if packed:
            send_own(2, 1)

    for child in range(2):
        map_ref[child] = index_ref[f if child == 0 else partner, child:child + 1, :]
    if packed:
        pl.loop(0, 2)(tables)
        fits_out[0] = counts_fit(index_ref, order, width, limits)

        @pl.when(middle)
        def _():
            outer(0, 1)
            inner(0, 1, middle)
            send_own(1, 0)
            near(0)
            inner(1, 1, middle)
            pack(0)
            send_own(1, 1)
            near(1)
            inner(0, 2, middle)

        @pl.when(at_end)
        def _():
            for child, d in ((0, 1), (1, 1), (0, 2), (1, 2)):
                inner(child, d, at_end)
            place_rows(1)
            inner(0, 3, at_end)

        place_rows(0)

        @pl.when(middle)
        def _():
            pack(1)
            far(0)
            serve_near(0)
            outer(1, 1)
            serve_far(0)
            serve_own(0)
            place_rows(1)
            far(1)
            serve_near(1)

        take_first(0)
        subtract(0, 0, blocks // 2)
        settle(0, blocks // 2)

        @pl.when(middle)
        def _():
            serve_far(1)
            serve_own(1)

        subtract(0, blocks // 2, blocks)
        settle(blocks // 2, blocks)
        take_first(1)
        take_late()
        subtract(1, 0, blocks)
        last_update()
        settle(0, blocks)
        for m in range(2):
            for q in range(2):
                hand_on(m, q).wait()
    else:
        relay_low(0, 1)
        relay_low(1, 1)

        @pl.when(middle)
        def _():
            send_own(1, 0)
            send_own(0, 0)

        relay_low(0, 2)
        near(0)

        @pl.when(middle)
        def _():
            send_own(1, 1)
            send_own(0, 1)

        relay_low(1, 2)

        @pl.loop(3, n)
        def _(d):
            relay_low(0, d)
            relay_low(1, d)

        near(1)
        place_rows(0)
        place_rows(1)
        for child in range(2):
            far(child)
            serve_all(child)
            serve_own(child)
            subtract(child, 0, blocks)
            settle(0, blocks)
        for m, ref in enumerate((u_h, u_l)):
            ref[...] = jnp.zeros_like(ref)
            for q in range(2):
                hand_on(m, q).start()
                hand_on(m, q).wait()
        fits_out[0] = 1

    for child in range(2):
        @pl.loop(0, n)
        def _(s):
            for side in range(2):
                for kind in range(3):
                    whole = ~(middle & (s == late)) if packed and (kind, child) == (2, 1) else t >= 0

                    @pl.when(takes(kind, side) & (s <= t if side == 0 else s >= t) & whole)
                    def _():
                        hop(kind, child, s, side).wait_send()

        @pl.when(server)
        def _():
            if packed:
                for j in range(2):
                    end_copy(child, j, aside).wait_send()
            else:
                @pl.loop(0, chunks)
                def _(j):
                    end_copy(child, j, aside).wait_send()

        if packed:
            @pl.when(middle)
            def _():
                cross_copy(child).wait_send()

            @pl.when(server)
            def _():
                if child == 1:
                    for k in range(2):
                        late_copy(k, aside).wait_send()


def capacity(draws, share, order):
    spread_of = math.sqrt(draws * share * (1 - share) * (1 - draws / order))
    return -(-math.ceil(draws * share + 4.5 * spread_of) // 8) * 8


def padded(rows):
    return -(-rows // 128) * 128


def assembled(inverse, upper, lower, maps, base, n, limits):
    order, width = base.shape
    pivots = inverse.shape[2]
    count = maps.shape[2]
    kr, wc, lr = inverse.shape[1], upper.shape[2], lower.shape[1]
    vmem = pltpu.VMEM
    dma = pltpu.SemaphoreType.DMA
    f32, b16 = jnp.float32, jnp.bfloat16
    chunk = min(256, width)
    chunks = width // chunk
    slots = 4
    packed = limits is not None
    held, extra = n, []
    f_shape, f_sems = (2, chunks, chunk, pivots), (2, chunks)
    u_shape = (n, pivots, wc)
    if packed:
        total_cap, _, cross = limits
        cap_pad, cross_pad = padded(total_cap), padded(cross)
        held = n // 2
        f_shape, f_sems = (2, total_cap, pivots), (2, 2)
        u_shape = (2, held, pivots, wc)
        extra = [
            vmem((2, 8, count), jnp.int32),
            vmem((2, total_cap, 1), jnp.int32),
            vmem((2, 1, cap_pad), jnp.int32),
            vmem((2, 1, cross_pad), jnp.int32),
            vmem((2, cross, pivots), f32),
            vmem((2, cross, pivots), f32),
            vmem((cross_pad, pivots), b16),
            vmem((cross_pad, pivots), b16),
            vmem((cap_pad, pivots), b16),
            vmem((cap_pad, pivots), b16),
            dma((2,)), dma((2,)), dma((2,)), dma((2,)),
        ]
    whole = pl.BlockSpec(memory_space=pl.ANY)
    return pl.pallas_call(
        functools.partial(front_kernel, n, limits),
        out_shape=[jax.ShapeDtypeStruct((order, width), f32)]
        + [jax.ShapeDtypeStruct((lr, width), b16)] * 2
        + [jax.ShapeDtypeStruct((1,), jnp.int32)],
        in_specs=[whole] * 3 + [pl.BlockSpec(memory_space=vmem), whole],
        out_specs=[whole] * 3 + [pl.BlockSpec(memory_space=pltpu.SMEM)],
        scratch_shapes=[
            vmem((2, 1, count), jnp.int32),
            vmem((2, held, pivots, wc), f32),
            vmem((2, n, kr, pivots), f32),
            vmem((2, n, lr, pivots), f32),
            vmem(u_shape, b16),
            vmem(u_shape, b16),
            vmem((n * kr, pivots), b16),
            vmem((n * kr, pivots), b16),
            vmem((count, pivots), b16),
            vmem((count, pivots), b16),
            vmem((2, order, pivots), b16),
            vmem((2, order, pivots), b16),
            vmem(f_shape, f32),
            vmem((2, width, pivots), b16),
            vmem((2, width, pivots), b16),
            vmem((lr, width), b16),
            vmem((lr, width), b16),
            vmem((slots, min(1024, order), chunk), f32),
            dma((3,)), dma((3,)), dma((3,)),
            dma((2, 2, n)), dma((2, n)),
            dma((2, 2, n)), dma((2, n)),
            dma((2, 2, n)), dma((2, n)),
            dma(f_sems), dma(f_sems),
            dma((slots,)), dma((slots,)), dma((2, 2)),
        ] + extra,
        compiler_params=pltpu.CompilerParams(
            collective_id=int(packed), has_side_effects=True, vmem_limit_bytes=63 * 1024 * 1024
        ),
    )(inverse, upper, lower, maps, base)


def finish_kernel(
    n, index_ref, x_in, u_h_in, u_l_in, out,
    x_buf, u_h, u_l, x_sem, out_sem, u_sem,
):
    t = lax.axis_index("tile")
    f = lax.axis_index("front")
    partner = lax.rem(f, 2) * -2 + 1 + f
    slots, rows, width = x_buf.shape
    lr = u_h.shape[0]
    blocks = out.shape[0] // rows
    ahead = slots // 2
    chunk = min(256, width)
    shard = jnp.where(t < n // 2, n - 1, 0)
    places = index_ref[partner, 1:2, pl.ds(pl.multiple_of(shard * lr, lr), lr)]

    def window(i):
        return pl.ds(pl.multiple_of(i * rows, rows), rows)

    def load(i):
        slot = lax.rem(i, slots)
        return pltpu.make_async_copy(x_in.at[window(i)], x_buf.at[slot], x_sem.at[slot])

    def store(i):
        slot = lax.rem(i, slots)
        return pltpu.make_async_copy(x_buf.at[slot], out.at[window(i)], out_sem.at[slot])

    first = [
        pltpu.make_async_copy(source, target, u_sem.at[k])
        for k, (source, target) in enumerate(((u_h_in, u_h), (u_l_in, u_l)))
    ]
    for copy in first:
        copy.start()
    load(0).start()
    for copy in first:
        copy.wait()
    for i in range(1, min(ahead, blocks)):
        load(i).start()

    @pl.loop(0, blocks)
    def _(i):
        @pl.when(i + ahead < blocks)
        def _():
            @pl.when(i >= slots - ahead)
            def _():
                store(i - (slots - ahead)).wait()

            load(i + ahead).start()

        choose = one_hot(lax.broadcasted_iota(jnp.int32, (rows, lr), 0) + i * rows == places)
        load(i).wait()
        slot = lax.rem(i, slots)
        for j in range(width // chunk):
            columns = slice(j * chunk, (j + 1) * chunk)
            total = dot(choose, u_h[:, columns]) + dot(choose, u_l[:, columns])
            x_buf[slot, :, columns] = x_buf[slot, :, columns] - total
        store(i).start()

    for i in range(max(blocks - slots, 0), blocks):
        store(i).wait()


def finished(n, index_map, x, u_h, u_l):
    order, width = x.shape
    rows, slots = min(512, order), 6
    vmem, dma, b16 = pltpu.VMEM, pltpu.SemaphoreType.DMA, jnp.bfloat16
    whole = pl.BlockSpec(memory_space=pl.ANY)
    return pl.pallas_call(
        functools.partial(finish_kernel, n),
        out_shape=jax.ShapeDtypeStruct(x.shape, x.dtype),
        in_specs=[pl.BlockSpec(memory_space=vmem)] + [whole] * 3,
        out_specs=whole,
        scratch_shapes=[
            vmem((slots, rows, width), x.dtype),
            vmem(u_h.shape, b16),
            vmem(u_h.shape, b16),
            dma((slots,)), dma((slots,)), dma((2,)),
        ],
        compiler_params=pltpu.CompilerParams(vmem_limit_bytes=60 * 1024 * 1024),
    )(index_map, x, u_h, u_l)


def shards(pivot_inverse, panel_upper, panel_lower, index_map, parent_base):
    n = lax.axis_size("tile")
    order, width = parent_base.shape[1:]
    count = index_map.shape[2]
    operands = (pivot_inverse[0], panel_upper[0], panel_lower[0], index_map, parent_base[0])

    side = order // 2
    total = capacity(count, width / order, order)
    far = capacity(count // 2, width / order, order)
    cross = capacity(count // 2, 1 / 2, order)

    def run(limits, *args):
        return tuple(assembled(*args, n, limits))

    def whole_transfers():
        return finished(n, index_map, *run(None, *operands)[:3])

    if n != 4 or total >= width or total - far < 128 or cross >= count // 2:
        return whole_transfers()[None]

    x, u_h, u_l, fits = run((total, far, cross), *operands)
    return lax.cond(fits[0] > 0, lambda: finished(n, index_map, x, u_h, u_l), whole_transfers)[None]


def solution(mesh):
    return jax.shard_map(
        shards,
        mesh=mesh,
        in_specs=(
            P("front", None, "tile", None),
            P("front", None, None, "tile"),
            P("front", None, "tile", None),
            P(),
            P("front", None, "tile"),
        ),
        out_specs=P("front", None, "tile"),
        check_vma=False,
    )
```
